32 devices in a mesh: ens: 2 (over x), tile: 16 (over z, y, core).
Axes of the slice: x: 2, y: 2, z: 4, core: 2. Of those that a mesh axis runs over, the one named last changes fastest.
Arguments:
- final_adjoint: float32 [320, 32, 1024], P('ens', 'tile'), parts along dimension 0, may hold values from -0.5 to 1.5
- first_density: float32 [320, 32, 1024], P('ens', 'tile'), parts along dimension 0, may hold values from 0.05 to 2
- second_density: float32 [320, 32, 1024], P('ens', 'tile'), parts along dimension 0, may hold values from 0.05 to 2
- forage: float32 [4, 6, 32, 1024], P('ens', None, 'tile'), parts along dimension 0, may hold values from 5 to 50
- preference: float32 [32, 6], P('ens'), parts along dimension 0, may hold values from 0.02 to 0.3
- base_mortality: float32 [160], replicated, may hold values from 0.01 to 0.5
- age_class: int32 [160], replicated, may hold values from 0 to 15, never falling along the last dimension, each value on 1 to 20 neighbouring positions
- land_mask: int32 [32, 1024], P('tile'), may hold values 0 or 1
- east_velocity: float32 [32, 1024], P('tile'), may hold values from -0.1 to 0.1
- north_velocity: float32 [32, 1024], P('tile'), may hold values from -0.1 to 0.1
Outputs:
- initial_adjoint: float32 [320, 32, 1024], P('ens', 'tile'), parts along dimension 0
- forage_sensitivity: float32 [4, 6, 32, 1024], P('ens', None, 'tile'), parts along dimension 0
- preference_gradient: float32 [32, 6], P('ens'), parts along dimension 0
The draws below stay inside these ranges and needn't reach their ends.
There are 2 independent parts, one for each index of `ens`. The reference program is written for one: setup_inputs(seed, part) draws one part's arguments, and reference() takes and returns one part's arrays. A program takes and returns all parts, laid end to end along the dimension named above; an argument that names none is the same for every part. Nothing has to cross between parts.
Inputs may be any that keep to these rules, and one draw needn't show every extreme that they name: `age_class`: never falls along the cohorts; every class holds 1 to 20 cohorts, one exactly that many.
All inputs are finite; a program needn't handle non-finite values. No bound on the sum of `land_mask` on one device may be relied on, other than what follows from the above.
Results may differ from the reference program's by a relative error of at most 0.00011.
Values sent between devices are 32-bit elements; how exact they have to be, the bound alone decides.
A program may use at most 64 MiB of HBM per device.

```python
import math
import jax
import jax.numpy as jnp
import numpy as np
from jax import lax

COH = 160
NX = 1024
FORAGE = 6
CLASSES = 16
SUBSTEPS = 4
MONTHS = 2
NY = 32


def touch_ends(result, stream_key, smallest, high):
    longest = result.shape.index(max(result.shape))
    spots = []
    for shift in (0, 1):
        where = [jax.random.randint(jax.random.fold_in(stream_key, axis), (), 0, length) for axis, length in enumerate(result.shape)]
        where[longest] = (where[longest] + shift) % result.shape[longest]
        spots.append(tuple(where))
    return result.at[spots[0]].set(smallest).at[spots[1]].set(high)


def block_levels(key, shape, pieces, smallest, largest):
    def one(position, parts):
        steps = jax.random.uniform(jax.random.fold_in(jax.random.fold_in(key, 6), position), (parts,), jnp.float32, smallest / len(pieces), largest / len(pieces))
        return jnp.repeat(jnp.exp(steps), shape[position] // parts).reshape((-1,) + (1,) * (len(shape) - position - 1))

    gain = one(*pieces[0])
    for cut in pieces[1:]:
        gain = gain * one(*cut)
    return gain


def length_profile(count, total, reach, lean):
    loads = [(1 << 20) // math.isqrt(standing ** lean) + 1 for standing in range(2, count + 1)]
    surplus, counts = total - reach - (count - 1), [1] * (count - 1)
    while surplus > 0:
        movable = [i for i in range(count - 1) if counts[i] < reach]
        mass, remaining = sum([loads[i] for i in movable]), surplus
        for i in movable:
            addition = min(reach - counts[i], max(1, remaining * loads[i] // mass), surplus)
            counts[i] = counts[i] + addition
            surplus = surplus - addition
    return np.array([reach] + counts)


def uneven_parts(stream_key, number_of, total, bound, slope):
    if number_of == 2:
        one = jax.random.randint(stream_key, (), max(1, total - bound), min(bound, total - 1) + 1)
        return jnp.stack([one, total - one])
    lengths = jnp.asarray(length_profile(number_of, total, bound, slope), jnp.int32)
    twos = (number_of - 1) // 2
    source_of, sink = lengths[1:1 + 2 * twos:2], lengths[2:2 + 2 * twos:2]
    slack = jnp.minimum(source_of - 1, bound - sink)
    shifted = jax.random.randint(jax.random.fold_in(stream_key, 1), (twos,), 0, 1 << 20) % (slack + 1)
    lengths = lengths.at[1:1 + 2 * twos:2].set(source_of - shifted).at[2:2 + 2 * twos:2].set(sink + shifted)
    return lengths[jax.random.permutation(jax.random.fold_in(stream_key, 2), number_of)]


def setup_inputs(seed: int = 0, part: int = 0) -> dict:
    splits = jax.random.split(jax.random.key(seed), 11)
    own_keys = jax.random.split(jax.random.fold_in(splits[10], part), 11)
    return {
        "final_adjoint": jnp.clip(-0.5 + 2.0 * jax.random.uniform(own_keys[0], (COH, NY, NX), jnp.float32) ** block_levels(own_keys[0], (COH, NY, NX), ((1, 16),), -0.2, 0.2), -0.5, 1.5),
        "first_density": jnp.clip(jnp.exp(math.log(2.0) - 3.6888794 * jax.random.uniform(own_keys[1], (COH, NY, NX), jnp.float32) ** block_levels(own_keys[1], (COH, NY, NX), ((1, 16),), -0.2, 0.2)), 0.05, 2.0),
        "second_density": jnp.clip(jnp.exp(math.log(2.0) - 3.6888794 * jax.random.uniform(own_keys[2], (COH, NY, NX), jnp.float32) ** block_levels(own_keys[2], (COH, NY, NX), ((1, 16),), -0.2, 0.2)), 0.05, 2.0),
        "forage": jnp.clip(jnp.exp(math.log(50.0) - 2.3025851 * jax.random.uniform(own_keys[3], (MONTHS, FORAGE, NY, NX), jnp.float32) ** block_levels(own_keys[3], (MONTHS, FORAGE, NY, NX), ((2, 16),), -0.2, 0.2)), 5.0, 50.0),
        "preference": jnp.clip(jax.random.uniform(own_keys[4], (CLASSES, FORAGE), jnp.float32, 0.02, 0.3), 0.02, 0.3),
        "base_mortality": jnp.clip(jnp.exp(jax.random.uniform(splits[5], (COH,), jnp.float32, math.log(0.01), math.log(0.5))), 0.01, 0.5),
        "age_class": jnp.searchsorted(jnp.cumsum(uneven_parts(splits[6], CLASSES, COH, COH // CLASSES * 2, 1)), jnp.arange(COH), side="right").astype(jnp.int32),
        "land_mask": touch_ends((jax.random.randint(splits[7], (NY, NX), 0, 4) < 3).astype(jnp.int32), jax.random.fold_in(splits[7], 1), 0, 1),
        "east_velocity": jnp.clip(jax.random.uniform(splits[8], (NY, NX), jnp.float32, -0.1, 0.1) * block_levels(splits[8], (NY, NX), ((0, 16),), -0.4, 0.0), -0.1, 0.1),
        "north_velocity": jnp.clip(jax.random.uniform(splits[9], (NY, NX), jnp.float32, -0.1, 0.1) * block_levels(splits[9], (NY, NX), ((0, 16),), -0.4, 0.0), -0.1, 0.1),
    }


HIGH = lax.Precision.HIGHEST


def make_rates(land_mask, east_velocity, north_velocity):
    mask = land_mask.astype(jnp.float32)
    padded = jnp.pad(mask, ((1, 1), (0, 0)))
    north_mask = padded[:-2]
    south_mask = padded[2:]
    east_mask = jnp.roll(mask, -1, axis=1)
    west_mask = jnp.roll(mask, 1, axis=1)
    rate_n = mask * north_mask * (0.1 + jnp.maximum(north_velocity, 0.0))
    rate_s = mask * south_mask * (0.1 + jnp.maximum(-north_velocity, 0.0))
    rate_e = mask * east_mask * (0.1 + jnp.maximum(east_velocity, 0.0))
    rate_w = mask * west_mask * (0.1 + jnp.maximum(-east_velocity, 0.0))
    keep = 1.0 - rate_n - rate_s - rate_e - rate_w
    return keep, rate_n, rate_s, rate_e, rate_w


def transpose_step(field, rates):
    keep, rate_n, rate_s, rate_e, rate_w = rates
    padded = jnp.pad(field, ((0, 0), (1, 1), (0, 0)))
    return (keep * field + rate_n * padded[:, :-2] + rate_s * padded[:, 2:]
            + rate_e * jnp.roll(field, -1, axis=2) + rate_w * jnp.roll(field, 1, axis=2))


def month_adjoint(incoming, density, food, pref_rows, base_mortality, rates, onehot):
    carried = incoming
    for step in range(SUBSTEPS):
        carried = transpose_step(carried, rates)
    cohorts = carried.shape[0]
    aged = jnp.concatenate([carried[1:], carried[cohorts - 1:]], axis=0).reshape(cohorts, -1)
    dens = density.reshape(cohorts, -1)
    feed = food.reshape(food.shape[0], -1)
    demand = jnp.dot(pref_rows.T, dens, precision=HIGH)
    total = feed + demand
    short = demand / total
    survival = jnp.exp(-(base_mortality[:, None] + jnp.dot(pref_rows, short, precision=HIGH)))
    grown = survival * dens
    adj_mort = -aged * grown
    adj_ratio = -jnp.dot(pref_rows.T, adj_mort, precision=HIGH)
    squared = total * total
    adj_demand = -adj_ratio * feed / squared
    sensitivity = adj_ratio * demand * feed / squared
    outgoing = aged * survival + jnp.dot(pref_rows, adj_demand, precision=HIGH)
    cohort_grad = jnp.dot(adj_mort, short.T, precision=HIGH) + jnp.dot(dens, adj_demand.T, precision=HIGH)
    class_grad = jnp.dot(onehot, cohort_grad, precision=HIGH)
    return outgoing.reshape(density.shape), sensitivity.reshape(food.shape), class_grad


def reference(final_adjoint, first_density, second_density, forage, preference, base_mortality,
              age_class, land_mask, east_velocity, north_velocity):
    classes = preference.shape[0]
    onehot = (age_class[None, :] == jnp.arange(classes, dtype=jnp.int32)[:, None]).astype(jnp.float32)
    pref_rows = jnp.dot(onehot.T, preference, precision=HIGH)
    rates = make_rates(land_mask, east_velocity, north_velocity)
    middle, sens_two, grad_two = month_adjoint(final_adjoint, second_density, forage[1], pref_rows,
                                               base_mortality, rates, onehot)
    initial, sens_one, grad_one = month_adjoint(middle, first_density, forage[0], pref_rows,
                                                base_mortality, rates, onehot)
    cells = land_mask.shape[0] * land_mask.shape[1]
    return initial, jnp.stack([sens_one, sens_two], axis=0), (grad_one + grad_two) / cells
```

```python
import jax
import jax.numpy as jnp
from jax import lax
from jax.experimental import pallas as pl
from jax.experimental.pallas import tpu as pltpu
from jax.sharding import PartitionSpec as P

SUBSTEPS = 4
LANES = 128
MESH = pl.DeviceIdType.MESH


def cuts(total, parts):
    size = max(1, total // parts)
    starts = [i * size for i in range(parts)]
    return [(s, (size if i < parts - 1 else total - s)) for i, s in enumerate(starts)]


def kernel(
    dims,
    table,
    base_row,
    cls,
    lead,
    dens1_in,
    dens2_in,
    food_in,
    mask_in,
    east_in,
    north_in,
    out,
    sens,
    grad_out,
    wide2,
    wide1,
    wide_a,
    done2,
    done1,
    done_a,
    aged2,
    aged1,
    mask_strip,
    east_strip,
    north_strip,
    rates,
    short_all,
    short1,
    feed_sq,
    dens1,
    dens2,
    food,
    decay,
    kinds2,
    kinds1,
    adding,
    living,
    crowd,
    dead,
    prefix,
    by_class,
    near_sum,
    far_sum,
    bounds,
    lsend,
    lrecv,
    zsend,
    zrecv,
    osend,
    orecv,
    z1send,
    z1recv,
    o1send,
    o1recv,
    fsend,
    frecv,
    hsend,
    hrecv,
    ssend,
    srecv,
    asend,
    arecv,
    nsend,
    nrecv,
    tsend,
    trecv,
    zasend,
    zarecv,
    own_sem,
):
    tiles, group, cohorts, quarter, forage, chunks, ahead, early = dims
    half = group // 2
    blocks = food.shape[2]
    classes = table.shape[1]
    me = lax.axis_index("tile")
    q = lax.rem(me, group)
    first = me - q
    has_prev = me >= group
    has_next = me < tiles - group

    def peer(o):
        return first + lax.rem(q + o, group)

    def source(o):
        return lax.rem(q + group - o, group)

    loads = [
        pltpu.make_async_copy(src, dst, own_sem.at[3 + i])
        for i, (src, dst) in enumerate(((dens2_in, dens2), (food_in, food), (dens1_in, dens1)))
    ]
    for copy in loads:
        copy.start()

    barrier = pltpu.get_barrier_semaphore()
    for o in range(1, group):
        pl.semaphore_signal(barrier, inc=1, device_id={"tile": peer(o)}, device_id_type=MESH)

    spans = tiles // group
    for g in range(1, spans):
        far = lax.rem(me + g * group, tiles)
        pl.semaphore_signal(barrier, inc=1, device_id={"tile": far}, device_id_type=MESH)

    strips = ((mask_in, mask_strip), (east_in, east_strip), (north_in, north_strip))
    own_fields = [
        pltpu.make_async_copy(src, dst.at[half + q], own_sem.at[f])
        for f, (src, dst) in enumerate(strips)
    ]
    for copy in own_fields:
        copy.start()

    zero = jnp.zeros((blocks, LANES), jnp.float32)

    fall = jnp.exp(-base_row[...])
    across = lax.broadcasted_iota(jnp.int32, (cohorts, cohorts), 1)
    down = lax.broadcasted_iota(jnp.int32, (cohorts, cohorts), 0)
    spread = jnp.where(across == down, fall, 0.0)
    decay[...] = jnp.broadcast_to(jnp.sum(spread, axis=1, keepdims=True), (cohorts, LANES))

    def bound(kind):
        spot = jnp.int32(0)
        size = 1
        while 2 * size <= cohorts:
            size = 2 * size
        while size >= 1:
            last = jnp.minimum(spot + size, cohorts) - 1
            ok = jnp.logical_and(spot + size <= cohorts, cls[last] < kind)
            spot = jnp.where(ok, spot + size, spot)
            size = size // 2
        return spot

    bounds[0] = jnp.int32(0)
    for kind in range(1, classes):
        bounds[kind] = bound(kind)
    bounds[classes] = jnp.int32(cohorts)

    pl.semaphore_wait(barrier, group + spans - 2)

    def remote(src, dst, ssem, rsem, target):
        return pltpu.make_async_remote_copy(
            src_ref=src, dst_ref=dst, send_sem=ssem, recv_sem=rsem,
            device_id={"tile": target}, device_id_type=MESH,
        )

    def gather_copy(buf, ssem, rsem, o, lift=0):
        return remote(buf.at[lift + q], buf.at[lift + q], ssem.at[o], rsem.at[o], peer(o))

    def gather_wait(buf, ssem, rsem, o, lift=0):
        spot = buf.at[lift + source(o)]
        remote(spot, spot, ssem.at[o], rsem.at[o], peer(o)).wait_recv()

    def halo(buf, lo, size, ssem, rsem, c):
        def rows(begin):
            if lo is None:
                return buf.at[pl.ds(begin, half)]
            return buf.at[pl.ds(begin, half), pl.ds(lo, size)]

        down = remote(rows(group), rows(0), ssem.at[0, c], rsem.at[0, c], me + group)
        up = remote(rows(half), rows(group + half), ssem.at[1, c], rsem.at[1, c], me - group)
        return down, up

    def halo_start(*args):
        down, up = halo(*args)

        @pl.when(has_next)
        def _():
            down.start()

        @pl.when(has_prev)
        def _():
            up.start()

    def halo_wait(*args):
        down, up = halo(*args)

        @pl.when(has_prev)
        def _():
            down.wait_recv()

        @pl.when(has_next)
        def _():
            up.wait_recv()

    def halo_sent(*args):
        down, up = halo(*args)

        @pl.when(has_next)
        def _():
            down.wait_send()

        @pl.when(has_prev)
        def _():
            up.wait_send()

    def field_copy(o, f):
        src, dst = strips[f]
        return remote(src, dst.at[half + q], fsend.at[o, f], frecv.at[o, f], peer(o))

    for f in range(3):
        for o in range(1, group):
            field_copy(o, f).start()

    part_cuts = cuts(quarter, chunks)
    lead_cuts = [(lo + (lo > 0), size + (lo == 0)) for lo, size in part_cuts]
    tail = lead_cuts[-1][0]
    lead_parts = lead_cuts[:-1] + [(tail, quarter - 1 - tail), (quarter - 1, 1), (quarter, 1)]

    def lead_copy(o, p):
        lo, size = lead_parts[p]
        begin = lax.rem(q + o, group) * quarter + 1 + lo
        return remote(
            lead.at[pl.ds(jnp.minimum(begin, cohorts - size), size)],
            wide2.at[half + q, pl.ds(lo, size)],
            lsend.at[o, p], lrecv.at[o, p], peer(o),
        )

    def lead_own(p):
        lo, size = lead_parts[p]
        begin = jnp.minimum(q * quarter + 1 + lo, cohorts - size)
        return pltpu.make_async_copy(
            lead.at[pl.ds(begin, size)], wide2.at[half + q, pl.ds(lo, size)], lrecv.at[0, p]
        )

    def lead_start(p):
        for o in range(1, group):
            lead_copy(o, p).start()
        lead_own(p).start()

    for p in range(ahead):
        lead_start(p)

    strips_all = (mask_strip, east_strip, north_strip)
    wides = (wide2, wide1, wide_a)

    @pl.when(jnp.logical_not(has_prev))
    def _():
        for strip in strips_all:
            strip[0:half] = jnp.zeros((half,) + strip.shape[1:], strip.dtype)
        for wide in wides:
            wide[0:half] = jnp.zeros((half,) + wide.shape[1:], jnp.float32)

    @pl.when(jnp.logical_not(has_next))
    def _():
        for strip in strips_all:
            strip[group + half :] = jnp.zeros((half,) + strip.shape[1:], strip.dtype)
        for wide in wides:
            wide[group + half :] = jnp.zeros((half,) + wide.shape[1:], jnp.float32)

    for part in range(group):
        prefix[part, 0] = zero

    def upto(spot):
        total = prefix[0, jnp.minimum(spot, quarter)]
        for part in range(1, group):
            total = total + prefix[part, jnp.clip(spot - part * quarter, 0, quarter)]
        return total

    def weighted(kind, values):
        total = table[0, kind] * values[0]
        for k in range(1, forage):
            total = total + table[k, kind] * values[k]
        return total

    def class_sums(store):
        def step(kind, carry):
            before, sums = carry
            here = upto(bounds[kind + 1])
            own = here - before
            store(kind, own)
            return here, tuple(sums[k] + table[k, kind] * own for k in range(forage))

        return lax.fori_loop(0, classes, step, (zero, (zero,) * forage), unroll=4)[1]

    def prepare(month, dens, by_kind, short_store):
        def add(i, runs):
            new = []
            for part in range(group):
                new.append(runs[part] + dens[part * quarter + i])
                prefix[part, i + 1] = new[part]
            return tuple(new)

        lax.fori_loop(0, quarter, add, (zero,) * group, unroll=2)

        def store(kind, own):
            crowd[month, kind] = own

        hungry = class_sums(store)
        shorts = []
        for k in range(forage):
            feed = food[month, k]
            total = feed + hungry[k]
            shorts.append(hungry[k] / total)
            short_store(k, shorts[k])
            feed_sq[month, k] = feed / (total * total)
            feed_sq[2 + month, k] = hungry[k]

        def each(kind, carry):
            by_kind[kind] = jnp.exp(-weighted(kind, shorts))
            return carry

        lax.fori_loop(0, classes, each, 0, unroll=2)

    def store_two(k, value):
        short_all[q, k] = value

    def store_one(k, value):
        short1[k] = value

    loads[0].wait()
    loads[1].wait()
    prepare(1, dens2, kinds2, store_two)
    for o in range(1, group):
        gather_copy(short_all, ssend, srecv, o).start()
    for p in range(ahead, len(lead_parts)):
        lead_start(p)

    for f, (src, dst) in enumerate(strips):
        own_fields[f].wait()
        for o in range(1, group):
            spot = dst.at[half + source(o)]
            remote(spot, spot, fsend.at[o, f], frecv.at[o, f], peer(o)).wait_recv()
        halo_start(dst, None, None, hsend, hrecv, f)
    lane = lax.broadcasted_iota(jnp.int32, (blocks, LANES), 1)
    odd = lax.rem(lax.broadcasted_iota(jnp.int32, (blocks, LANES), 0), 2) == 1
    last_lane = lane == LANES - 1
    first_lane = lane == 0

    def east_of(x):
        near = pltpu.roll(x, LANES - 1, 1)
        return jnp.where(last_lane, pltpu.roll(near, blocks - 2, 0), near)

    def west_of(x):
        near = pltpu.roll(x, 1, 1)
        return jnp.where(first_lane, pltpu.roll(near, 2, 0), near)

    def vertical(slots, s):
        above = slots[s - 1] if s > 0 and slots[s - 1] is not None else zero
        below = slots[s + 1] if s + 1 < len(slots) and slots[s + 1] is not None else zero
        north = jnp.where(odd, pltpu.roll(slots[s], 1, 0), pltpu.roll(above, blocks - 1, 0))
        south = jnp.where(odd, pltpu.roll(below, 1, 0), pltpu.roll(slots[s], blocks - 1, 0))
        return north, south

    def lead_wait(c):
        for p in [c] if c < chunks - 1 else range(c, len(lead_parts)):
            lo, size = lead_parts[p]
            for o in range(1, group):
                spot = wide2.at[half + source(o), pl.ds(lo, size)]
                remote(spot, spot, lsend.at[o, p], lrecv.at[o, p], peer(o)).wait_recv()
            lead_own(p).wait()

    lead_wait(0)
    halo_start(wide2, *lead_cuts[0], zsend, zrecv, 0)
    for f, (src, dst) in enumerate(strips):
        halo_wait(dst, None, None, hsend, hrecv, f)
    masks = [mask_strip[s].astype(jnp.float32) for s in range(2 * group)]
    for s in range(2 * group):
        mask, east, north = masks[s], east_strip[s], north_strip[s]
        mask_n, mask_s = vertical(masks, s)
        rate_n = mask * mask_n * (0.1 + jnp.maximum(north, 0.0))
        rate_s = mask * mask_s * (0.1 + jnp.maximum(-north, 0.0))
        rate_e = mask * east_of(mask) * (0.1 + jnp.maximum(east, 0.0))
        rate_w = mask * west_of(mask) * (0.1 + jnp.maximum(-east, 0.0))
        rates[s, 0] = 1.0 - rate_n - rate_s - rate_e - rate_w
        rates[s, 1] = rate_n
        rates[s, 2] = rate_s
        rates[s, 3] = rate_e
        rates[s, 4] = rate_w

    def transport(wide, done, lo, size):
        def body(i, carry):
            slots = [wide[s, i] for s in range(2 * group)]
            for step in range(SUBSTEPS):
                margin = (step + 1) // 2
                new = [None] * (2 * group)
                for s in range(margin, 2 * group - margin):
                    north, south = vertical(slots, s)
                    new[s] = (
                        rates[s, 0] * slots[s]
                        + rates[s, 1] * north
                        + rates[s, 2] * south
                        + rates[s, 3] * east_of(slots[s])
                        + rates[s, 4] * west_of(slots[s])
                    )
                slots = new
            for s in range(group):
                done[s, i] = slots[half + s]
            return carry

        lax.fori_loop(lo, lo + size, body, 0)

    def out_copy(done, aged, o, c, ssem, rsem):
        lo, size = part_cuts[c]
        return remote(
            done.at[lax.rem(q + o, group), pl.ds(lo, size)],
            aged.at[pl.ds(q * quarter + lo, size)], ssem.at[o, c], rsem.at[o, c], peer(o),
        )

    def out_own(done, aged, c, sem):
        lo, size = part_cuts[c]
        return pltpu.make_async_copy(
            done.at[q, pl.ds(lo, size)], aged.at[pl.ds(q * quarter + lo, size)], sem.at[0, c]
        )

    def out_start(done, aged, c, ssem, rsem):
        for o in range(1, group):
            out_copy(done, aged, o, c, ssem, rsem).start()
        out_own(done, aged, c, rsem).start()

    def out_wait(done, aged, c, ssem, rsem):
        lo, size = part_cuts[c]
        for o in range(1, group):
            spot = aged.at[pl.ds(source(o) * quarter + lo, size)]
            remote(spot, spot, ssem.at[o, c], rsem.at[o, c], peer(o)).wait_recv()
        out_own(done, aged, c, rsem).wait()

    def middle(c):
        lo, size = part_cuts[c]

        def each(i, carry):
            a = jnp.minimum(q * quarter + i + 1, cohorts - 1)
            kind = cls[a]
            fading = decay[pl.ds(a, 1)]
            for s in range(group):
                wide1[half + s, i] = done2[s, i + 1] * (fading * living[kind, s])
            return carry

        lax.fori_loop(lo, lo + size, each, 0)

    def halo_one(c):
        halo_start(wide1, *part_cuts[c], z1send, z1recv, c)

    def tally(c, aged, dens, by_kind, extra=None):
        lo, size = part_cuts[c]

        def step(i, runs):
            new = []
            for part in range(group):
                a = part * quarter + i
                value = aged[a]
                if extra is not None:
                    value = value + extra[cls[jnp.minimum(a + 1, cohorts - 1)]]
                kept = value * (decay[pl.ds(a, 1)] * by_kind[cls[a]])
                if extra is not None:
                    out[a] = kept
                new.append(runs[part] + kept * dens[a])
                prefix[part, i + 1] = new[part]
            return tuple(new)

        lax.fori_loop(lo, lo + size, step, tuple(prefix[part, lo] for part in range(group)))

    def finish(month):
        def store(kind, own):
            dead[kind] = own

        ratio = class_sums(store)
        adem = []
        for k in range(forage):
            adem.append(-ratio[k] * feed_sq[month, k])
            sens[month, k] = ratio[k] * feed_sq[2 + month, k] * feed_sq[month, k]
        return adem

    def class_rows(month, adem, short, add):
        def each(kind, carry):
            many, lost = crowd[month, kind], dead[kind]
            for k in range(forage):
                row = jnp.sum(many * adem[k] - lost * short[k], axis=0, keepdims=True)
                if add:
                    row = row + by_class[k, pl.ds(kind, 1)]
                by_class[k, pl.ds(kind, 1)] = row
            return carry

        lax.fori_loop(0, classes, each, 0, unroll=2)

    for c in range(chunks):
        if c + 1 < chunks:
            lead_wait(c + 1)
            halo_start(wide2, *lead_cuts[c + 1], zsend, zrecv, c + 1)
        halo_wait(wide2, *lead_cuts[c], zsend, zrecv, c)
        transport(wide2, done2, *lead_cuts[c])
        out_start(done2, aged2, c, osend, orecv)
        if c == 0:
            for o in range(1, group):
                gather_wait(short_all, ssend, srecv, o)
            for s in range(group):
                shorts = [short_all[s, k] for k in range(forage)]

                def each(kind, carry, s=s, shorts=shorts):
                    living[kind, s] = jnp.exp(-weighted(kind, shorts))
                    return carry

                lax.fori_loop(0, classes, each, 0, unroll=2)
            loads[2].wait()
            prepare(0, dens1, kinds1, store_one)
        middle(c)
        if c == chunks - 2:
            for b in range(c):
                halo_one(b)
        if c >= chunks - 2:
            halo_one(c)

    for c in range(chunks):
        halo_wait(wide1, *part_cuts[c], z1send, z1recv, c)
        transport(wide1, done1, *part_cuts[c])
        if c < early:
            out_start(done1, aged1, c, o1send, o1recv)
        out_wait(done2, aged2, c, osend, orecv)
        tally(c, aged2, dens2, kinds2)

    adem2 = finish(1)
    for k in range(forage):
        wide_a[half + q, k] = adem2[k]
    for o in range(1, group):
        gather_copy(wide_a, asend, arecv, o, half).start()
    for c in range(early, chunks):
        out_start(done1, aged1, c, o1send, o1recv)
    class_rows(1, adem2, [short_all[q, k] for k in range(forage)], False)
    for o in range(1, group):
        gather_wait(wide_a, asend, arecv, o, half)
    halo_start(wide_a, None, None, zasend, zarecv, 0)
    halo_wait(wide_a, None, None, zasend, zarecv, 0)
    transport(wide_a, done_a, 0, forage)
    spread_adem = [done_a[q, k] for k in range(forage)]

    def fill(values):
        def each(kind, carry):
            adding[kind] = weighted(kind, values)
            return carry

        lax.fori_loop(0, classes, each, 0, unroll=2)

    fill(spread_adem)
    for c in range(chunks):
        out_wait(done1, aged1, c, o1send, o1recv)
        tally(c, aged1, dens1, kinds1, adding)
    adem1 = finish(0)
    class_rows(0, adem1, [short1[k] for k in range(forage)], True)

    ones = jnp.ones((8, LANES), jnp.float32)
    rows = []
    for k in range(forage):
        lanes_sum = lax.dot_general(
            ones, by_class[k], (((1,), (1,)), ((), ())), precision=lax.Precision.HIGHEST,
            preferred_element_type=jnp.float32,
        )
        rows.append(lanes_sum[0:1])
    near_sum[q] = jnp.concatenate(rows, axis=0)
    for o in range(1, group):
        gather_copy(near_sum, nsend, nrecv, o).start()
    fill(adem1)

    def outgoing(lo, hi):
        def step(a, carry):
            out[a] = out[a] + adding[cls[a]]
            return carry

        lax.fori_loop(lo, hi, step, 0, unroll=4)

    outgoing(0, cohorts // 2)
    for o in range(1, group):
        gather_wait(near_sum, nsend, nrecv, o)
    span = me // group
    far_sum[span] = sum(near_sum[i] for i in range(1, group)) + near_sum[0]

    def far_copy(g):
        far = lax.rem(me + g * group, tiles)
        return remote(far_sum.at[span], far_sum.at[span], tsend.at[g], trecv.at[g], far)

    for g in range(1, spans):
        far_copy(g).start()
    outgoing(cohorts // 2, cohorts)
    for g in range(1, spans):
        spot = far_sum.at[lax.rem(span + spans - g, spans)]
        remote(spot, spot, tsend.at[g], trecv.at[g], lax.rem(me + g * group, tiles)).wait_recv()
    grad_out[...] = lax.fori_loop(
        1, spans, lambda g, total: total + far_sum[g], far_sum[0]
    ) / (tiles * blocks * LANES)
    for g in range(1, spans):
        far_copy(g).wait_send()

    for o in range(1, group):
        gather_copy(near_sum, nsend, nrecv, o).wait_send()
        for f in range(3):
            field_copy(o, f).wait_send()
        for p in range(len(lead_parts)):
            lead_copy(o, p).wait_send()
        gather_copy(short_all, ssend, srecv, o).wait_send()
        gather_copy(wide_a, asend, arecv, o, half).wait_send()
        for c in range(chunks):
            out_copy(done2, aged2, o, c, osend, orecv).wait_send()
            out_copy(done1, aged1, o, c, o1send, o1recv).wait_send()
    for f, (src, dst) in enumerate(strips):
        halo_sent(dst, None, None, hsend, hrecv, f)
    halo_sent(wide_a, None, None, zasend, zarecv, 0)
    for c in range(chunks):
        halo_sent(wide2, *lead_cuts[c], zsend, zrecv, c)
        halo_sent(wide1, *part_cuts[c], z1send, z1recv, c)


def blocked(x):
    rows, columns = x.shape[-2:]
    head = x.shape[:-2]
    n = len(head)
    y = x.reshape(head + (rows, columns // LANES, LANES))
    y = jnp.swapaxes(y, n, n + 1)
    return y.reshape(head + (rows * columns // LANES, LANES))


def unblocked(x, rows):
    head = x.shape[:-2]
    n = len(head)
    y = x.reshape(head + (x.shape[-2] // rows, rows, LANES))
    y = jnp.swapaxes(y, n, n + 1)
    return y.reshape(head + (rows, -1))


def shards(
    final_adjoint,
    first_density,
    second_density,
    forage,
    preference,
    base_mortality,
    age_class,
    land_mask,
    east_velocity,
    north_velocity,
):
    classes, groups = preference.shape
    cohorts, rows, columns = final_adjoint.shape
    tiles = lax.axis_size("tile")
    group = 2 * SUBSTEPS // rows
    quarter = cohorts // group
    chunks = 8
    blocks = rows * columns // LANES
    f32 = jnp.float32
    dma = pltpu.SemaphoreType.DMA
    vmem = pl.BlockSpec(memory_space=pltpu.VMEM)
    smem = pl.BlockSpec(memory_space=pltpu.SMEM)
    hbm = pl.BlockSpec(memory_space=pl.ANY)
    dims = (tiles, group, cohorts, quarter, groups, chunks, 2, 3)
    cell = (blocks, LANES)
    pair = [dma((group, chunks)), dma((group, chunks))]
    hop = [dma((2, chunks)), dma((2, chunks))]
    one = [dma((group,)), dma((group,))]

    def body(*refs):
        kernel(dims, *refs)

    out, sens, grad = pl.pallas_call(
        body,
        out_shape=(
            jax.ShapeDtypeStruct((cohorts,) + cell, f32),
            jax.ShapeDtypeStruct((2, groups) + cell, f32),
            jax.ShapeDtypeStruct((groups, classes), f32),
        ),
        in_specs=[smem, vmem, smem] + [hbm] * 7,
        out_specs=(vmem, vmem, vmem),
        scratch_shapes=[
            pltpu.VMEM((2 * group, quarter + 1) + cell, f32),
            pltpu.VMEM((2 * group, quarter) + cell, f32),
            pltpu.VMEM((2 * group, groups) + cell, f32),
            pltpu.VMEM((group, quarter + 1) + cell, f32),
            pltpu.VMEM((group, quarter) + cell, f32),
            pltpu.VMEM((group, groups) + cell, f32),
            pltpu.VMEM((cohorts,) + cell, f32),
            pltpu.VMEM((cohorts,) + cell, f32),
            pltpu.VMEM((2 * group,) + cell, jnp.int32),
            pltpu.VMEM((2 * group,) + cell, f32),
            pltpu.VMEM((2 * group,) + cell, f32),
            pltpu.VMEM((2 * group, 5) + cell, f32),
            pltpu.VMEM((group, groups) + cell, f32),
            pltpu.VMEM((groups,) + cell, f32),
            pltpu.VMEM((4, groups) + cell, f32),
            pltpu.VMEM((cohorts,) + cell, f32),
            pltpu.VMEM((cohorts,) + cell, f32),
            pltpu.VMEM((2, groups) + cell, f32),
            pltpu.VMEM((cohorts, LANES), f32),
            pltpu.VMEM((classes,) + cell, f32),
            pltpu.VMEM((classes,) + cell, f32),
            pltpu.VMEM((classes,) + cell, f32),
            pltpu.VMEM((classes, group) + cell, f32),
            pltpu.VMEM((2, classes) + cell, f32),
            pltpu.VMEM((classes,) + cell, f32),
            pltpu.VMEM((group, quarter + 1) + cell, f32),
            pltpu.VMEM((groups, classes, LANES), f32),
            pltpu.VMEM((group, groups, classes), f32),
            pltpu.VMEM((tiles // group, groups, classes), f32),
            pltpu.SMEM((classes + 1,), jnp.int32),
        ]
        + [dma((group, chunks + 2))] * 2 + hop + pair + hop + pair + [dma((group, 3))] * 2
        + [dma((2, 3))] * 2 + one + one + one + [dma((tiles // group,))] * 2
        + [dma((2, 1))] * 2 + [dma((6,))],
        compiler_params=pltpu.CompilerParams(
            collective_id=0, has_side_effects=True, vmem_limit_bytes=60 * 1024 * 1024
        ),
        name="adjoint",
    )(
        preference.T,
        base_mortality.reshape(1, -1),
        age_class,
        blocked(final_adjoint),
        blocked(first_density),
        blocked(second_density),
        blocked(forage),
        blocked(land_mask),
        blocked(east_velocity),
        blocked(north_velocity),
    )
    summed = grad.T
    return (unblocked(out, rows), unblocked(sens, rows), summed)


def solution(mesh):
    in_specs = (
        P("ens", "tile", None),
        P("ens", "tile", None),
        P("ens", "tile", None),
        P("ens", None, "tile", None),
        P("ens", None),
        P(),
        P(),
        P("tile", None),
        P("tile", None),
        P("tile", None),
    )
    out_specs = (P("ens", "tile", None), P("ens", None, "tile", None), P("ens", None))
    return jax.shard_map(shards, mesh=mesh, in_specs=in_specs, out_specs=out_specs, check_vma=False)
```

```python
import jax
import jax.numpy as jnp
from jax import lax
from jax.experimental import pallas as pl
from jax.experimental.pallas import tpu as pltpu
from jax.sharding import PartitionSpec as P

SUBSTEPS = 4
LANES = 128
MESH = pl.DeviceIdType.MESH


def kernel(
    dims,
    table,
    base_row,
    cls,
    lead,
    dens1_in,
    dens2_in,
    food_in,
    mask_in,
    east_in,
    north_in,
    kept,
    adding,
    sens,
    grad_out,
    wide2,
    wide1,
    wide_a,
    done2,
    done1,
    aged2,
    carried1,
    mask_strip,
    east_strip,
    north_strip,
    rates,
    short_all,
    short1,
    strewn,
    feed_sq,
    dens1,
    dens2,
    food,
    decay,
    kinds2,
    kinds1,
    moved,
    living,
    crowd,
    dead,
    prefix,
    by_class,
    totals,
    bounds,
    lsend,
    lrecv,
    zsend,
    zrecv,
    osend,
    orecv,
    z1send,
    z1recv,
    o1send,
    o1recv,
    fsend,
    frecv,
    hsend,
    hrecv,
    ssend,
    srecv,
    asend,
    arecv,
    nsend,
    nrecv,
    own_sem,
):
    tiles, group, rows, cohorts, quarter, forage, chunks, lead_ahead, out_lag, halo_ahead = dims
    half = group // 2
    size = quarter // chunks
    blocks = food.shape[2]
    per = blocks // rows
    reach = half * rows
    classes = table.shape[1]
    me = lax.axis_index("tile")
    q = lax.rem(me, group)
    first = me - q
    has_prev = me >= group
    has_next = me < tiles - group

    def peer(o):
        return first + lax.rem(q + o, group)

    def source(o):
        return lax.rem(q + group - o, group)

    barrier = pltpu.get_barrier_semaphore()
    def greet(t, carry):
        other = lax.rem(me + t, tiles)
        pl.semaphore_signal(barrier, inc=1, device_id={"tile": other}, device_id_type=MESH)
        return carry

    lax.fori_loop(1, tiles, greet, 0)
    near = [d for d in range(-half, half + 1) if d != 0]

    loads = [
        pltpu.make_async_copy(src, dst, own_sem.at[3 + i])
        for i, (src, dst) in enumerate(((dens2_in, dens2), (food_in, food), (dens1_in, dens1)))
    ]
    for copy in loads:
        copy.start()
    strips = ((mask_in, mask_strip), (east_in, east_strip), (north_in, north_strip))
    own_fields = [
        pltpu.make_async_copy(src, dst.at[half + q], own_sem.at[f])
        for f, (src, dst) in enumerate(strips)
    ]
    for copy in own_fields:
        copy.start()

    zero = jnp.zeros((blocks, LANES), jnp.float32)

    fall = jnp.exp(-base_row[...])
    across = lax.broadcasted_iota(jnp.int32, (cohorts, cohorts), 1)
    down = lax.broadcasted_iota(jnp.int32, (cohorts, cohorts), 0)
    spread = jnp.where(across == down, fall, 0.0)
    decay[...] = jnp.broadcast_to(jnp.sum(spread, axis=1, keepdims=True), (cohorts, LANES))

    def bound(kind):
        spot = jnp.int32(0)
        width = 1
        while 2 * width <= cohorts:
            width = 2 * width
        while width >= 1:
            last = jnp.minimum(spot + width, cohorts) - 1
            ok = jnp.logical_and(spot + width <= cohorts, cls[last] < kind)
            spot = jnp.where(ok, spot + width, spot)
            width = width // 2
        return spot

    bounds[0] = jnp.int32(0)
    for kind in range(1, classes):
        bounds[kind] = bound(kind)
    bounds[classes] = jnp.int32(cohorts)

    pl.semaphore_wait(barrier, tiles - 1)

    def remote(src, dst, ssem, rsem, target):
        return pltpu.make_async_remote_copy(
            src_ref=src, dst_ref=dst, send_sem=ssem, recv_sem=rsem,
            device_id={"tile": target}, device_id_type=MESH,
        )

    def gather_copy(buf, ssem, rsem, o):
        return remote(buf.at[q], buf.at[q], ssem.at[o], rsem.at[o], peer(o))

    def gather_wait(buf, ssem, rsem, o):
        spot = buf.at[source(o)]
        remote(spot, spot, ssem.at[o], rsem.at[o], peer(o)).wait_recv()

    def halo(buf, lo, ssem, rsem, c):
        def part(begin):
            if lo is None:
                return buf.at[pl.ds(begin, half)]
            return buf.at[pl.ds(begin, half), pl.ds(lo, size)]

        down = remote(part(group), part(0), ssem.at[0, c], rsem.at[0, c], me + group)
        up = remote(part(half), part(group + half), ssem.at[1, c], rsem.at[1, c], me - group)
        return down, up

    def halo_start(*args):
        down, up = halo(*args)

        @pl.when(has_next)
        def _():
            down.start()

        @pl.when(has_prev)
        def _():
            up.start()

    def halo_wait(*args):
        down, up = halo(*args)

        @pl.when(has_prev)
        def _():
            down.wait_recv()

        @pl.when(has_next)
        def _():
            up.wait_recv()

    def halo_sent(*args):
        down, up = halo(*args)

        @pl.when(has_next)
        def _():
            down.wait_send()

        @pl.when(has_prev)
        def _():
            up.wait_send()

    def field_copy(o, f):
        src, dst = strips[f]
        return remote(src, dst.at[half + q], fsend.at[o, f], frecv.at[o, f], peer(o))

    for f in range(3):
        for o in range(1, group):
            field_copy(o, f).start()

    def lead_pieces(c):
        return ((c * size, size - 1, 2 * c), (c * size + size - 1, 1, 2 * c + 1))

    def lead_copy(o, lo, count, sem):
        begin = jnp.minimum(lax.rem(q + o, group) * quarter + 1 + lo, cohorts - count)
        return remote(
            lead.at[pl.ds(begin, count)], wide2.at[half + q, pl.ds(lo, count)],
            lsend.at[o, sem], lrecv.at[o, sem], peer(o),
        )

    def lead_own(lo, count, sem):
        begin = jnp.minimum(q * quarter + 1 + lo, cohorts - count)
        return pltpu.make_async_copy(
            lead.at[pl.ds(begin, count)], wide2.at[half + q, pl.ds(lo, count)], lrecv.at[0, sem]
        )

    def lead_start(c):
        for piece in lead_pieces(c):
            for o in range(1, group):
                lead_copy(o, *piece).start()
            lead_own(*piece).start()

    def lead_wait(c):
        for lo, count, sem in lead_pieces(c):
            for o in range(1, group):
                spot = wide2.at[half + source(o), pl.ds(lo, count)]
                remote(spot, spot, lsend.at[o, sem], lrecv.at[o, sem], peer(o)).wait_recv()
            lead_own(lo, count, sem).wait()

    def lead_sent(c):
        for piece in lead_pieces(c):
            for o in range(1, group):
                lead_copy(o, *piece).wait_send()

    lead_start(0)
    lead_start(1)

    strips_all = (mask_strip, east_strip, north_strip)
    wides = (wide2, wide1)

    @pl.when(jnp.logical_not(has_prev))
    def _():
        for strip in strips_all:
            strip[0:half] = jnp.zeros((half,) + strip.shape[1:], strip.dtype)
        for wide in wides:
            wide[0:half] = jnp.zeros((half,) + wide.shape[1:], jnp.float32)

    @pl.when(jnp.logical_not(has_next))
    def _():
        for strip in strips_all:
            strip[group + half :] = jnp.zeros((half,) + strip.shape[1:], strip.dtype)
        for wide in wides:
            wide[group + half :] = jnp.zeros((half,) + wide.shape[1:], jnp.float32)

    for d in near:

        @pl.when(jnp.logical_not(jnp.logical_and(me + d >= 0, me + d < tiles)))
        def _(d=d):
            wide_a[half + d] = jnp.zeros(wide_a.shape[1:], jnp.float32)

    for part in range(group):
        prefix[part, 0] = zero

    def upto(spot):
        total = prefix[0, jnp.clip(spot, 0, quarter)]
        for part in range(1, group):
            top = quarter + (part == group - 1)
            total = total + prefix[part, jnp.clip(spot - part * quarter, 0, top)]
        return total

    def weighted(kind, values):
        total = table[0, kind] * values[0]
        for k in range(1, forage):
            total = total + table[k, kind] * values[k]
        return total

    def class_sums(store, shift):
        def step(kind, carry):
            before, sums = carry
            here = upto(bounds[kind + 1] + shift)
            own = here - before
            store(kind, own)
            return here, tuple(sums[k] + table[k, kind] * own for k in range(forage))

        return lax.fori_loop(0, classes, step, (upto(shift), (zero,) * forage), unroll=4)[1]

    def fill(into, values, decaying=False):
        def each(kind, carry):
            total = weighted(kind, values)
            into[kind] = jnp.exp(-total) if decaying else total
            return carry

        lax.fori_loop(0, classes, each, 0, unroll=2)

    def prepare(month, dens, by_kind, short_store):
        def add(i, runs):
            new = []
            for part in range(group):
                new.append(runs[part] + dens[part * quarter + i])
                prefix[part, i + 1] = new[part]
            return tuple(new)

        lax.fori_loop(0, quarter, add, (zero,) * group, unroll=2)

        def store(kind, own):
            crowd[month, kind] = own

        hungry = class_sums(store, 0)
        shorts = []
        for k in range(forage):
            feed = food[month, k]
            total = feed + hungry[k]
            shorts.append(hungry[k] / total)
            short_store(k, shorts[k])
            feed_sq[month, k] = feed / (total * total)
            feed_sq[2 + month, k] = hungry[k]
        return shorts

    def store_two(k, value):
        short_all[q, k] = value

    def store_one(k, value):
        short1[k] = value

    loads[0].wait()
    loads[1].wait()
    shorts2 = prepare(1, dens2, kinds2, store_two)
    for o in range(1, group):
        gather_copy(short_all, ssend, srecv, o).start()
    lead_start(2)
    fill(kinds2, shorts2, True)

    for f, (src, dst) in enumerate(strips):
        own_fields[f].wait()
        for o in range(1, group):
            spot = dst.at[half + source(o)]
            remote(spot, spot, fsend.at[o, f], frecv.at[o, f], peer(o)).wait_recv()
        halo_start(dst, None, hsend, hrecv, f)
    loads[2].wait()
    shorts1 = prepare(0, dens1, kinds1, store_one)
    fill(kinds1, shorts1, True)
    lead_start(3)

    lane = lax.broadcasted_iota(jnp.int32, (per, LANES), 1)
    last_lane = lane == LANES - 1
    first_lane = lane == 0

    def east_of(x):
        near = pltpu.roll(x, LANES - 1, 1)
        return jnp.where(last_lane, pltpu.roll(near, per - 1, 0), near)

    def west_of(x):
        near = pltpu.roll(x, 1, 1)
        return jnp.where(first_lane, pltpu.roll(near, 1, 0), near)

    def row_of(r):
        return pl.ds(r % rows, per, stride=rows)

    lead_wait(0)
    halo_start(wide2, 0, zsend, zrecv, 0)
    lead_start(4)
    for f, (src, dst) in enumerate(strips):
        halo_wait(dst, None, hsend, hrecv, f)
    span_rows = rows * 2 * group
    masks = [mask_strip[r // rows, row_of(r)].astype(jnp.float32) for r in range(span_rows)]
    for r in range(1, span_rows - 1):
        mask = masks[r]
        east, north = east_strip[r // rows, row_of(r)], north_strip[r // rows, row_of(r)]
        rate_n = mask * masks[r - 1] * (0.1 + jnp.maximum(north, 0.0))
        rate_s = mask * masks[r + 1] * (0.1 + jnp.maximum(-north, 0.0))
        rate_e = mask * east_of(mask) * (0.1 + jnp.maximum(east, 0.0))
        rate_w = mask * west_of(mask) * (0.1 + jnp.maximum(-east, 0.0))
        rates[r, 0] = 1.0 - rate_n - rate_s - rate_e - rate_w
        rates[r, 1] = rate_n
        rates[r, 2] = rate_s
        rates[r, 3] = rate_e
        rates[r, 4] = rate_w

    def advance(fields, shift):
        count = len(fields[0])
        for step in range(SUBSTEPS):
            margin = step + 1
            fresh = [[None] * count for _ in fields]
            for u, old in enumerate(fields):
                for r in range(margin, count - margin):
                    rate = rates.at[r + shift]
                    fresh[u][r] = (
                        rate[0] * old[r]
                        + rate[1] * old[r - 1]
                        + rate[2] * old[r + 1]
                        + rate[3] * east_of(old[r])
                        + rate[4] * west_of(old[r])
                    )
            fields = fresh
        return fields

    def transport(wide, done, c):
        fields = [
            [wide[r // rows, c * size + u, row_of(r)] for r in range(span_rows)]
            for u in range(size)
        ]
        for u, field in enumerate(advance(fields, 0)):
            for r in range(rows * group):
                done[r // rows, c * size + u, row_of(r)] = field[reach + r]

    def out_copy(done, into, o, c, ssem, rsem):
        return remote(
            done.at[lax.rem(q + o, group), pl.ds(c * size, size)],
            into.at[pl.ds(q * quarter + c * size, size)], ssem.at[o, c], rsem.at[o, c], peer(o),
        )

    def out_own(done, into, c, sem):
        return pltpu.make_async_copy(
            done.at[q, pl.ds(c * size, size)], into.at[pl.ds(q * quarter + c * size, size)],
            sem.at[0, c],
        )

    def out_start(done, into, c, ssem, rsem):
        for o in range(1, group):
            out_copy(done, into, o, c, ssem, rsem).start()
        out_own(done, into, c, rsem).start()

    def out_wait(done, into, c, ssem, rsem):
        for o in range(1, group):
            spot = into.at[pl.ds(source(o) * quarter + c * size, size)]
            remote(spot, spot, ssem.at[o, c], rsem.at[o, c], peer(o)).wait_recv()
        out_own(done, into, c, rsem).wait()

    def out_sent(done, into, c, ssem, rsem):
        for o in range(1, group):
            out_copy(done, into, o, c, ssem, rsem).wait_send()

    def middle(c):
        def each(i, carry):
            a = q * quarter + i
            kind = cls[a]
            fading = decay[pl.ds(a, 1)]
            for s in range(group):
                wide1[half + s, i] = done2[s, i] * (fading * living[s, kind])
            return carry

        lax.fori_loop(c * size, c * size + size, each, 0)

    def halo_one(c):
        halo_start(wide1, c * size, z1send, z1recv, c)

    def tally_two(c):
        def step(i, runs):
            new = []
            for part in range(group):
                a = part * quarter + i
                gone = aged2[a] * (decay[pl.ds(a, 1)] * kinds2[cls[a]])
                new.append(runs[part] + gone * dens2[a])
                prefix[part, i + 1] = new[part]
            return tuple(new)

        begin = tuple(prefix[part, c * size] for part in range(group))
        lax.fori_loop(c * size, c * size + size, step, begin)

    def keep_one(a, before):
        value = carried1[a] + moved[cls[a]]
        stay = value * (decay[pl.ds(before, 1)] * kinds1[cls[before]])
        return stay, stay * dens1[before]

    def tally_one(c):
        def step(i, runs):
            new = []
            for part in range(group):
                a = part * quarter + i
                stay, gone = keep_one(a, jnp.maximum(a - 1, 0))
                kept[a] = stay
                new.append(runs[part] + gone)
                prefix[part, i + 1] = new[part]
            return tuple(new)

        begin = tuple(prefix[part, c * size] for part in range(group))
        lax.fori_loop(c * size, c * size + size, step, begin)

    def finish(month, shift):
        def store(kind, own):
            dead[kind] = own

        ratio = class_sums(store, shift)
        adem = []
        for k in range(forage):
            adem.append(-ratio[k] * feed_sq[month, k])
            sens[month, k] = ratio[k] * feed_sq[2 + month, k] * feed_sq[month, k]
        return adem

    def class_rows(month, adem, short, add):
        def each(kind, carry):
            many, lost = crowd[month, kind], dead[kind]
            for k in range(forage):
                row = jnp.sum(many * adem[k] - lost * short[k], axis=0, keepdims=True)
                if add:
                    row = row + by_class[k, pl.ds(kind, 1)]
                by_class[k, pl.ds(kind, 1)] = row
            return carry

        lax.fori_loop(0, classes, each, 0, unroll=2)

    def live(s, carry):
        shorts = [short_all[s, k] for k in range(forage)]
        fill(living.at[s], shorts, True)
        return carry

    def second(c, carry):
        halo_wait(wide2, c * size, zsend, zrecv, c)

        @pl.when(c == chunks - 1)
        def _():
            for b in range(halo_ahead):
                halo_one(b)

        transport(wide2, done2, c)

        @pl.when(c >= out_lag)
        def _():
            out_start(done2, aged2, c - out_lag, osend, orecv)

        @pl.when(c == 0)
        def _():
            for o in range(1, group):
                gather_wait(short_all, ssend, srecv, o)
            lax.fori_loop(0, group, live, 0)

        middle(c)

        @pl.when(c + 2 < chunks)
        def _():
            lead_wait(c + 2)
            halo_start(wide2, (c + 2) * size, zsend, zrecv, c + 2)

        @pl.when(c + 2 + lead_ahead < chunks)
        def _():
            lead_start(c + 2 + lead_ahead)

        return carry

    lead_wait(1)
    halo_start(wide2, size, zsend, zrecv, 1)
    lead_start(5)
    lax.fori_loop(0, chunks, second, 0)
    for c in range(chunks - out_lag, chunks):
        out_start(done2, aged2, c, osend, orecv)

    def near_copy(i):
        d = near[i]
        return remote(
            wide_a.at[half], wide_a.at[half - d], asend.at[i], arecv.at[len(near) - 1 - i], me + d
        )

    def near_wait(i):
        spot = wide_a.at[half + near[i]]
        remote(spot, spot, asend.at[i], arecv.at[i], me + near[i]).wait_recv()

    def if_near(i, action):
        d = near[i]

        @pl.when(jnp.logical_and(me + d >= 0, me + d < tiles))
        def _():
            action(i)

    def gather_two(c, carry):
        out_wait(done2, aged2, c, osend, orecv)
        tally_two(c)
        return carry

    def leading(c, carry):
        halo_wait(wide1, c * size, z1send, z1recv, c)

        @pl.when(c + halo_ahead < chunks)
        def _():
            halo_one(c + halo_ahead)

        transport(wide1, done1, c)
        out_start(done1, carried1, c, o1send, o1recv)

        @pl.when(c == chunks // 2 - 1)
        def _():
            lax.fori_loop(0, chunks, gather_two, 0)
            adem2 = finish(1, 0)
            for k in range(forage):
                wide_a[half, k] = adem2[k]
            for i in range(len(near)):
                if_near(i, lambda i: near_copy(i).start())
            class_rows(1, adem2, [short_all[q, k] for k in range(forage)], False)

        return carry

    lax.fori_loop(0, chunks, leading, 0)

    def settle(c, carry):
        lead_sent(c)
        halo_sent(wide2, c * size, zsend, zrecv, c)
        halo_sent(wide1, c * size, z1send, z1recv, c)
        out_sent(done2, aged2, c, osend, orecv)
        return carry

    lax.fori_loop(0, chunks, settle, 0)
    for o in range(1, group):
        for f in range(3):
            field_copy(o, f).wait_send()
        gather_copy(short_all, ssend, srecv, o).wait_send()
    for f, (src, dst) in enumerate(strips):
        halo_sent(dst, None, hsend, hrecv, f)
    for i in range(len(near)):
        if_near(i, lambda i: near_wait(i))

    reach_rows = rows * (2 * half + 1)
    fields = [
        [wide_a[r // rows, k, row_of(r)] for r in range(reach_rows)] for k in range(forage)
    ]
    for k, field in enumerate(advance(fields, rows * q)):
        for r in range(rows):
            strewn[k, row_of(r)] = field[reach + r]
    fill(moved, [strewn[k] for k in range(forage)])

    def ending(c, carry):
        out_wait(done1, carried1, c, o1send, o1recv)
        tally_one(c)
        return carry

    lax.fori_loop(0, chunks, ending, 0)
    stay, gone = keep_one(cohorts - 1, cohorts - 1)
    kept[cohorts] = stay
    prefix[group - 1, quarter + 1] = prefix[group - 1, quarter] + gone
    adem1 = finish(0, 1)
    class_rows(0, adem1, [short1[k] for k in range(forage)], True)

    ones = jnp.ones((8, LANES), jnp.float32)
    sums = []
    for k in range(forage):
        lanes_sum = lax.dot_general(
            ones, by_class[k], (((1,), (1,)), ((), ())), precision=lax.Precision.HIGHEST,
            preferred_element_type=jnp.float32,
        )
        sums.append(lanes_sum[0:1])
    totals[me] = jnp.concatenate(sums, axis=0)

    def total_copy(t):
        other = lax.rem(me + t, tiles)
        return remote(totals.at[me], totals.at[me], nsend.at[t], nrecv.at[t], other)

    def total_start(t, carry):
        total_copy(t).start()
        return carry

    def total_wait(t, carry):
        spot = totals.at[lax.rem(me + tiles - t, tiles)]
        remote(spot, spot, nsend.at[t], nrecv.at[t], lax.rem(me + t, tiles)).wait_recv()
        return carry

    def total_sent(t, carry):
        total_copy(t).wait_send()
        return carry

    lax.fori_loop(1, tiles, total_start, 0)
    fill(adding, adem1)

    def settled(c, carry):
        out_sent(done1, carried1, c, o1send, o1recv)
        return carry

    lax.fori_loop(0, chunks, settled, 0)
    for i in range(len(near)):
        if_near(i, lambda i: near_copy(i).wait_send())
    lax.fori_loop(1, tiles, total_wait, 0)
    grad_out[...] = lax.fori_loop(
        1, tiles, lambda t, total: total + totals[t], totals[0]
    ) / (tiles * blocks * LANES)
    lax.fori_loop(1, tiles, total_sent, 0)


def last_kernel(cls, kept, adding, sens, grad, out, sens_out, grad_out):
    step = pl.program_id(0)
    count = out.shape[0]

    def each(i, carry):
        a = step * count + i
        out[i] = kept[a + 1] + adding[cls[a]]
        return carry

    lax.fori_loop(0, count, each, 0, unroll=4)

    @pl.when(step == 0)
    def _():
        sens_out[...] = sens[...]
        grad_out[...] = grad[...]


def blocked(x):
    rows, columns = x.shape[-2:]
    head = x.shape[:-2]
    n = len(head)
    y = x.reshape(head + (rows, columns // LANES, LANES))
    y = jnp.swapaxes(y, n, n + 1)
    return y.reshape(head + (rows * columns // LANES, LANES))


def unblocked(x, rows):
    head = x.shape[:-2]
    n = len(head)
    y = x.reshape(head + (x.shape[-2] // rows, rows, LANES))
    y = jnp.swapaxes(y, n, n + 1)
    return y.reshape(head + (rows, -1))


def shards(
    final_adjoint,
    first_density,
    second_density,
    forage,
    preference,
    base_mortality,
    age_class,
    land_mask,
    east_velocity,
    north_velocity,
):
    classes, groups = preference.shape
    cohorts, rows, columns = final_adjoint.shape
    tiles = lax.axis_size("tile")
    group = 2 * SUBSTEPS // rows
    quarter = cohorts // group
    chunks = 8
    blocks = rows * columns // LANES
    f32 = jnp.float32
    dma = pltpu.SemaphoreType.DMA
    vmem = pl.BlockSpec(memory_space=pltpu.VMEM)
    smem = pl.BlockSpec(memory_space=pltpu.SMEM)
    hbm = pl.BlockSpec(memory_space=pl.ANY)
    dims = (tiles, group, rows, cohorts, quarter, groups, chunks, 4, 2, 3)
    cell = (blocks, LANES)
    pair = [dma((group, chunks)), dma((group, chunks))]
    hop = [dma((2, chunks)), dma((2, chunks))]
    one = [dma((group,)), dma((group,))]

    def body(*refs):
        kernel(dims, *refs)

    def cells(*lead):
        return pltpu.VMEM(lead + cell, f32)

    passed = pl.pallas_call(
        body,
        out_shape=(
            cells(cohorts + 1),
            cells(classes),
            cells(2, groups),
            pltpu.VMEM((groups, classes), f32),
        ),
        in_specs=[smem, vmem, smem] + [hbm] * 7,
        out_specs=(vmem, vmem, vmem, vmem),
        scratch_shapes=[
            cells(2 * group, quarter),
            cells(2 * group, quarter),
            cells(group + 1, groups),
            cells(group, quarter),
            cells(group, quarter),
            cells(cohorts),
            cells(cohorts),
            pltpu.VMEM((2 * group,) + cell, jnp.int32),
            cells(2 * group),
            cells(2 * group),
            pltpu.VMEM((2 * group * rows, 5, blocks // rows, LANES), f32),
            cells(group, groups),
            cells(groups),
            cells(groups),
            cells(4, groups),
            cells(cohorts),
            cells(cohorts),
            cells(2, groups),
            pltpu.VMEM((cohorts, LANES), f32),
            cells(classes),
            cells(classes),
            cells(classes),
            cells(group, classes),
            cells(2, classes),
            cells(classes),
            cells(group, quarter + 2),
            pltpu.VMEM((groups, classes, LANES), f32),
            pltpu.VMEM((tiles, groups, classes), f32),
            pltpu.SMEM((classes + 1,), jnp.int32),
        ]
        + [dma((group, 2 * chunks))] * 2 + hop + pair + hop + pair + [dma((group, 3))] * 2
        + [dma((2, 3))] * 2 + one + one + [dma((tiles,))] * 2 + [dma((6,))],
        compiler_params=pltpu.CompilerParams(
            collective_id=0, has_side_effects=True, vmem_limit_bytes=56 * 1024 * 1024
        ),
        name="adjoint",
    )(
        preference.T,
        base_mortality.reshape(1, -1),
        age_class,
        blocked(final_adjoint),
        blocked(first_density),
        blocked(second_density),
        blocked(forage),
        blocked(land_mask),
        blocked(east_velocity),
        blocked(north_velocity),
    )
    steps = 4
    whole = lambda *shape: pl.BlockSpec(shape, lambda i: (0,) * len(shape))
    slab = pl.BlockSpec((cohorts // steps,) + cell, lambda i: (i, 0, 0))
    small = [whole(2, groups, *cell), whole(groups, classes)]
    out, sens, grad = pl.pallas_call(
        last_kernel,
        grid=(steps,),
        out_shape=(
            jax.ShapeDtypeStruct((cohorts,) + cell, f32),
            jax.ShapeDtypeStruct((2, groups) + cell, f32),
            jax.ShapeDtypeStruct((groups, classes), f32),
        ),
        in_specs=[smem] + [vmem] * 4,
        out_specs=(slab, *small),
        name="outgoing",
    )(age_class, *(pltpu.with_memory_space_constraint(x, pltpu.VMEM) for x in passed))
    summed = grad.T
    return (unblocked(out, rows), unblocked(sens, rows), summed)


def solution(mesh):
    in_specs = (
        P("ens", "tile", None),
        P("ens", "tile", None),
        P("ens", "tile", None),
        P("ens", None, "tile", None),
        P("ens", None),
        P(),
        P(),
        P("tile", None),
        P("tile", None),
        P("tile", None),
    )
    out_specs = (P("ens", "tile", None), P("ens", None, "tile", None), P("ens", None))
    return jax.shard_map(shards, mesh=mesh, in_specs=in_specs, out_specs=out_specs, check_vma=False)
```

```python
import jax
import jax.numpy as jnp
from jax import lax
from jax.experimental import pallas as pl
from jax.experimental.pallas import tpu as pltpu
from jax.sharding import PartitionSpec as P

SUBSTEPS = 4
LANES = 128
MESH = pl.DeviceIdType.MESH


def kernel(
    dims,
    table,
    base_row,
    cls,
    lead,
    dens1_in,
    dens2_in,
    food_in,
    mask_in,
    east_in,
    north_in,
    out,
    sens,
    grad_out,
    wide2,
    wide1,
    wide_a,
    done2,
    done1,
    aged2,
    carried1,
    mask_strip,
    east_strip,
    north_strip,
    rates,
    short_all,
    short1,
    strewn,
    feed_sq,
    dens1,
    dens2,
    food,
    decay,
    kinds2,
    kinds1,
    moved,
    adding,
    living,
    crowd,
    dead,
    prefix,
    by_class,
    totals,
    bounds,
    lsend,
    lrecv,
    zsend,
    zrecv,
    osend,
    orecv,
    z1send,
    z1recv,
    o1send,
    o1recv,
    fsend,
    frecv,
    hsend,
    hrecv,
    ssend,
    srecv,
    asend,
    arecv,
    nsend,
    nrecv,
    own_sem,
):
    tiles, group, rows, cohorts, quarter, forage, chunks, lead_ahead, out_lag, halo_ahead = dims
    half = group // 2
    size = quarter // chunks
    blocks = food.shape[2]
    per = blocks // rows
    reach = half * rows
    classes = table.shape[1]
    me = lax.axis_index("tile")
    q = lax.rem(me, group)
    first = me - q
    has_prev = me >= group
    has_next = me < tiles - group

    def peer(o):
        return first + lax.rem(q + o, group)

    def source(o):
        return lax.rem(q + group - o, group)

    barrier = pltpu.get_barrier_semaphore()
    def greet(t, carry):
        other = lax.rem(me + t, tiles)
        pl.semaphore_signal(barrier, inc=1, device_id={"tile": other}, device_id_type=MESH)
        return carry

    lax.fori_loop(1, tiles, greet, 0)
    near = [d for d in range(-half, half + 1) if d != 0]

    loads = [
        pltpu.make_async_copy(src, dst, own_sem.at[3 + i])
        for i, (src, dst) in enumerate(((dens2_in, dens2), (food_in, food), (dens1_in, dens1)))
    ]
    for copy in loads:
        copy.start()
    strips = ((mask_in, mask_strip), (east_in, east_strip), (north_in, north_strip))
    own_fields = [
        pltpu.make_async_copy(src, dst.at[half + q], own_sem.at[f])
        for f, (src, dst) in enumerate(strips)
    ]
    for copy in own_fields:
        copy.start()

    zero = jnp.zeros((blocks, LANES), jnp.float32)

    fall = jnp.exp(-base_row[...])
    across = lax.broadcasted_iota(jnp.int32, (cohorts, cohorts), 1)
    down = lax.broadcasted_iota(jnp.int32, (cohorts, cohorts), 0)
    spread = jnp.where(across == down, fall, 0.0)
    decay[...] = jnp.broadcast_to(jnp.sum(spread, axis=1, keepdims=True), (cohorts, LANES))

    def bound(kind):
        spot = jnp.int32(0)
        width = 1
        while 2 * width <= cohorts:
            width = 2 * width
        while width >= 1:
            last = jnp.minimum(spot + width, cohorts) - 1
            ok = jnp.logical_and(spot + width <= cohorts, cls[last] < kind)
            spot = jnp.where(ok, spot + width, spot)
            width = width // 2
        return spot

    bounds[0] = jnp.int32(0)
    for kind in range(1, classes):
        bounds[kind] = bound(kind)
    bounds[classes] = jnp.int32(cohorts)

    pl.semaphore_wait(barrier, tiles - 1)

    def remote(src, dst, ssem, rsem, target):
        return pltpu.make_async_remote_copy(
            src_ref=src, dst_ref=dst, send_sem=ssem, recv_sem=rsem,
            device_id={"tile": target}, device_id_type=MESH,
        )

    def short_copy(o):
        return remote(short_all.at[q], short_all.at[q], ssend.at[0], srecv.at[0], peer(o))

    def halo(buf, lo, ssem, rsem, c):
        def part(begin):
            if lo is None:
                return buf.at[pl.ds(begin, half)]
            return buf.at[pl.ds(begin, half), pl.ds(lo, size)]

        down = remote(part(group), part(0), ssem.at[0], rsem.at[0, c], me + group)
        up = remote(part(half), part(group + half), ssem.at[1], rsem.at[1, c], me - group)
        return down, up

    def halo_start(*args):
        down, up = halo(*args)

        @pl.when(has_next)
        def _():
            down.start()

        @pl.when(has_prev)
        def _():
            up.start()

    def halo_wait(*args):
        down, up = halo(*args)

        @pl.when(has_prev)
        def _():
            down.wait_recv()

        @pl.when(has_next)
        def _():
            up.wait_recv()

    def halo_sent(spot, ssem, rsem):
        @pl.when(has_next)
        def _():
            sent_all(spot, ssem.at[0], rsem.at[0, 0])

        @pl.when(has_prev)
        def _():
            sent_all(spot, ssem.at[1], rsem.at[1, 0])

    def field_copy(o, f):
        src, dst = strips[f]
        return remote(src, dst.at[half + q], fsend.at[f], frecv.at[f], peer(o))

    for f in range(3):
        for o in range(1, group):
            field_copy(o, f).start()

    def lead_pieces(c):
        return ((c * size, size - 1), (c * size + size - 1, 1))

    def lead_copy(o, c, lo, count):
        begin = jnp.minimum(lax.rem(q + o, group) * quarter + 1 + lo, cohorts - count)
        return remote(
            lead.at[pl.ds(begin, count)], wide2.at[half + q, pl.ds(lo, count)],
            lsend.at[0], lrecv.at[c], peer(o),
        )

    def lead_own(c, lo, count):
        begin = jnp.minimum(q * quarter + 1 + lo, cohorts - count)
        return pltpu.make_async_copy(
            lead.at[pl.ds(begin, count)], wide2.at[half + q, pl.ds(lo, count)], lrecv.at[c]
        )

    def lead_start(c):
        for piece in lead_pieces(c):
            for o in range(1, group):
                lead_copy(o, c, *piece).start()
            lead_own(c, *piece).start()

    def wait_all(spot, sem):
        pltpu.make_async_copy(spot, spot, sem).wait()

    def sent_all(spot, ssem, rsem):
        remote(spot, spot, ssem, rsem, peer(1)).wait_send()

    def lead_wait(c):
        wait_all(wide2.at[pl.ds(half, group), pl.ds(c * size, size)], lrecv.at[c])

    lead_start(0)
    lead_start(1)

    strips_all = (mask_strip, east_strip, north_strip)
    wides = (wide2, wide1)

    @pl.when(jnp.logical_not(has_prev))
    def _():
        for strip in strips_all:
            strip[0:half] = jnp.zeros((half,) + strip.shape[1:], strip.dtype)
        for wide in wides:
            wide[0:half] = jnp.zeros((half,) + wide.shape[1:], jnp.float32)

    @pl.when(jnp.logical_not(has_next))
    def _():
        for strip in strips_all:
            strip[group + half :] = jnp.zeros((half,) + strip.shape[1:], strip.dtype)
        for wide in wides:
            wide[group + half :] = jnp.zeros((half,) + wide.shape[1:], jnp.float32)

    for d in near:

        @pl.when(jnp.logical_not(jnp.logical_and(me + d >= 0, me + d < tiles)))
        def _(d=d):
            wide_a[half + d] = jnp.zeros(wide_a.shape[1:], jnp.float32)

    for part in range(group):
        prefix[part, 0] = zero

    def upto(spot):
        total = prefix[0, jnp.clip(spot, 0, quarter)]
        for part in range(1, group):
            top = quarter + (part == group - 1)
            total = total + prefix[part, jnp.clip(spot - part * quarter, 0, top)]
        return total

    def weighted(kind, values):
        total = table[0, kind] * values[0]
        for k in range(1, forage):
            total = total + table[k, kind] * values[k]
        return total

    def class_sums(store, shift):
        def step(kind, carry):
            before, sums = carry
            here = upto(bounds[kind + 1] + shift)
            own = here - before
            store(kind, own)
            return here, tuple(sums[k] + table[k, kind] * own for k in range(forage))

        return lax.fori_loop(0, classes, step, (upto(shift), (zero,) * forage), unroll=4)[1]

    def fill(into, values, decaying=False):
        def each(kind, carry):
            total = weighted(kind, values)
            into[kind] = jnp.exp(-total) if decaying else total
            return carry

        lax.fori_loop(0, classes, each, 0, unroll=2)

    def prepare(month, dens, by_kind, short_store):
        def add(i, runs):
            new = []
            for part in range(group):
                new.append(runs[part] + dens[part * quarter + i])
                prefix[part, i + 1] = new[part]
            return tuple(new)

        lax.fori_loop(0, quarter, add, (zero,) * group, unroll=2)

        def store(kind, own):
            crowd[month, kind] = own

        hungry = class_sums(store, 0)
        shorts = []
        for k in range(forage):
            feed = food[month, k]
            total = feed + hungry[k]
            shorts.append(hungry[k] / total)
            short_store(k, shorts[k])
            feed_sq[month, k] = feed / (total * total)
            feed_sq[2 + month, k] = hungry[k]
        return shorts

    def store_two(k, value):
        short_all[q, k] = value

    def store_one(k, value):
        short1[k] = value

    loads[0].wait()
    loads[1].wait()
    shorts2 = prepare(1, dens2, kinds2, store_two)
    for o in range(1, group):
        short_copy(o).start()
    lead_start(2)
    fill(kinds2, shorts2, True)

    for f, (src, dst) in enumerate(strips):
        own_fields[f].wait()
        wait_all(dst.at[pl.ds(half, group - 1)], frecv.at[f])
        halo_start(dst, None, hsend.at[f], hrecv, f)
    loads[2].wait()
    shorts1 = prepare(0, dens1, kinds1, store_one)
    fill(kinds1, shorts1, True)
    lead_start(3)

    lane = lax.broadcasted_iota(jnp.int32, (per, LANES), 1)
    last_lane = lane == LANES - 1
    first_lane = lane == 0

    def east_of(x):
        near = pltpu.roll(x, LANES - 1, 1)
        return jnp.where(last_lane, pltpu.roll(near, per - 1, 0), near)

    def west_of(x):
        near = pltpu.roll(x, 1, 1)
        return jnp.where(first_lane, pltpu.roll(near, 1, 0), near)

    def row_of(r):
        return pl.ds(r % rows, per, stride=rows)

    lead_wait(0)
    halo_start(wide2, 0, zsend, zrecv, 0)
    lead_start(4)
    for f, (src, dst) in enumerate(strips):
        halo_wait(dst, None, hsend.at[f], hrecv, f)
    span_rows = rows * 2 * group
    masks = [mask_strip[r // rows, row_of(r)].astype(jnp.float32) for r in range(span_rows)]
    for r in range(1, span_rows - 1):
        mask = masks[r]
        east, north = east_strip[r // rows, row_of(r)], north_strip[r // rows, row_of(r)]
        rate_n = mask * masks[r - 1] * (0.1 + jnp.maximum(north, 0.0))
        rate_s = mask * masks[r + 1] * (0.1 + jnp.maximum(-north, 0.0))
        rate_e = mask * east_of(mask) * (0.1 + jnp.maximum(east, 0.0))
        rate_w = mask * west_of(mask) * (0.1 + jnp.maximum(-east, 0.0))
        rates[r, 0] = 1.0 - rate_n - rate_s - rate_e - rate_w
        rates[r, 1] = rate_n
        rates[r, 2] = rate_s
        rates[r, 3] = rate_e
        rates[r, 4] = rate_w

    def advance(fields, shift):
        count = len(fields[0])
        for step in range(SUBSTEPS):
            margin = step + 1
            fresh = [[None] * count for _ in fields]
            for u, old in enumerate(fields):
                for r in range(margin, count - margin):
                    rate = rates.at[r + shift]
                    fresh[u][r] = (
                        rate[0] * old[r]
                        + rate[1] * old[r - 1]
                        + rate[2] * old[r + 1]
                        + rate[3] * east_of(old[r])
                        + rate[4] * west_of(old[r])
                    )
            fields = fresh
        return fields

    def transport(wide, done, c):
        fields = [
            [wide[r // rows, c * size + u, row_of(r)] for r in range(span_rows)]
            for u in range(size)
        ]
        for u, field in enumerate(advance(fields, 0)):
            for r in range(rows * group):
                done[r // rows, c * size + u, row_of(r)] = field[reach + r]

    def out_start(done, into, c, ssem, rsem):
        spot = into.at[q, pl.ds(c * size, size)]
        for o in range(1, group):
            part = done.at[lax.rem(q + o, group), pl.ds(c * size, size)]
            remote(part, spot, ssem.at[0], rsem.at[c], peer(o)).start()
        pltpu.make_async_copy(done.at[q, pl.ds(c * size, size)], spot, rsem.at[c]).start()

    def out_wait(into, c, rsem):
        wait_all(into.at[pl.ds(0, group), pl.ds(c * size, size)], rsem.at[c])

    def middle(c):
        def each(i, carry):
            a = q * quarter + i
            kind = cls[a]
            fading = decay[pl.ds(a, 1)]
            for s in range(group):
                wide1[half + s, i] = done2[s, i] * (fading * living[s, kind])
            return carry

        lax.fori_loop(c * size, c * size + size, each, 0)

    def halo_one(c):
        halo_start(wide1, c * size, z1send, z1recv, c)

    def tally_two(c):
        def step(i, runs):
            new = []
            for part in range(group):
                a = part * quarter + i
                gone = aged2[part, i] * (decay[pl.ds(a, 1)] * kinds2[cls[a]])
                new.append(runs[part] + gone * dens2[a])
                prefix[part, i + 1] = new[part]
            return tuple(new)

        begin = tuple(prefix[part, c * size] for part in range(group))
        lax.fori_loop(c * size, c * size + size, step, begin)

    def keep_one(part, i, before):
        value = carried1[part, i] + moved[cls[part * quarter + i]]
        stay = value * (decay[pl.ds(before, 1)] * kinds1[cls[before]])
        out[before] = stay
        return stay * dens1[before]

    def tally_one(c):
        def step(i, runs):
            new = []
            for part in range(group):
                before = jnp.maximum(part * quarter + i - 1, 0)
                new.append(runs[part] + keep_one(part, i, before))
                prefix[part, i + 1] = new[part]
            return tuple(new)

        begin = tuple(prefix[part, c * size] for part in range(group))
        lax.fori_loop(c * size, c * size + size, step, begin)

    def finish(month, shift):
        def store(kind, own):
            dead[kind] = own

        ratio = class_sums(store, shift)
        adem = []
        for k in range(forage):
            adem.append(-ratio[k] * feed_sq[month, k])
            sens[month, k] = ratio[k] * feed_sq[2 + month, k] * feed_sq[month, k]
        return adem

    def class_rows(month, adem, short, add):
        def each(kind, carry):
            many, lost = crowd[month, kind], dead[kind]
            for k in range(forage):
                row = jnp.sum(many * adem[k] - lost * short[k], axis=0, keepdims=True)
                if add:
                    row = row + by_class[k, pl.ds(kind, 1)]
                by_class[k, pl.ds(kind, 1)] = row
            return carry

        lax.fori_loop(0, classes, each, 0, unroll=2)

    def live(s, carry):
        shorts = [short_all[s, k] for k in range(forage)]
        fill(living.at[s], shorts, True)
        return carry

    def second(c, carry):
        halo_wait(wide2, c * size, zsend, zrecv, c)

        @pl.when(c == chunks - 1)
        def _():
            for b in range(halo_ahead):
                halo_one(b)

        transport(wide2, done2, c)

        @pl.when(c >= out_lag)
        def _():
            out_start(done2, aged2, c - out_lag, osend, orecv)

        @pl.when(c == 0)
        def _():
            wait_all(short_all.at[pl.ds(0, group - 1)], srecv.at[0])
            lax.fori_loop(0, group, live, 0)

        middle(c)

        @pl.when(c + 2 < chunks)
        def _():
            lead_wait(c + 2)
            halo_start(wide2, (c + 2) * size, zsend, zrecv, c + 2)

        @pl.when(c + 2 + lead_ahead < chunks)
        def _():
            lead_start(c + 2 + lead_ahead)

        return carry

    lead_wait(1)
    halo_start(wide2, size, zsend, zrecv, 1)
    lead_start(5)
    lax.fori_loop(0, chunks, second, 0)
    for c in range(chunks - out_lag, chunks):
        out_start(done2, aged2, c, osend, orecv)

    def near_copy(i):
        d = near[i]
        return remote(
            wide_a.at[half], wide_a.at[half - d], asend.at[i], arecv.at[len(near) - 1 - i], me + d
        )

    def near_wait(i):
        spot = wide_a.at[half + near[i]]
        remote(spot, spot, asend.at[i], arecv.at[i], me + near[i]).wait_recv()

    def if_near(i, action):
        d = near[i]

        @pl.when(jnp.logical_and(me + d >= 0, me + d < tiles))
        def _():
            action(i)

    def gather_two(c, carry):
        out_wait(aged2, c, orecv)
        tally_two(c)
        return carry

    def leading(c, carry):
        halo_wait(wide1, c * size, z1send, z1recv, c)

        @pl.when(c + halo_ahead < chunks)
        def _():
            halo_one(c + halo_ahead)

        transport(wide1, done1, c)
        out_start(done1, carried1, c, o1send, o1recv)

        @pl.when(c == chunks // 2 - 1)
        def _():
            lax.fori_loop(0, chunks, gather_two, 0)
            adem2 = finish(1, 0)
            for k in range(forage):
                wide_a[half, k] = adem2[k]
            for i in range(len(near)):
                if_near(i, lambda i: near_copy(i).start())
            class_rows(1, adem2, [short_all[q, k] for k in range(forage)], False)

        return carry

    lax.fori_loop(0, chunks, leading, 0)

    mine = pl.ds(0, group - 1)
    sent_all(wide2.at[mine], lsend.at[0], lrecv.at[0])
    sent_all(done2.at[mine], osend.at[0], orecv.at[0])
    sent_all(short_all.at[mine], ssend.at[0], srecv.at[0])
    halo_sent(wide2.at[pl.ds(0, half)], zsend, zrecv)
    halo_sent(wide1.at[pl.ds(0, half)], z1send, z1recv)
    for f, (src, dst) in enumerate(strips):
        sent_all(dst.at[mine], fsend.at[f], frecv.at[f])
        halo_sent(dst.at[pl.ds(0, half)], hsend.at[f], hrecv)
    for i in range(len(near)):
        if_near(i, lambda i: near_wait(i))

    reach_rows = rows * (2 * half + 1)
    fields = [
        [wide_a[r // rows, k, row_of(r)] for r in range(reach_rows)] for k in range(forage)
    ]
    for k, field in enumerate(advance(fields, rows * q)):
        for r in range(rows):
            strewn[k, row_of(r)] = field[reach + r]
    fill(moved, [strewn[k] for k in range(forage)])

    def ending(c, carry):
        out_wait(carried1, c, o1recv)
        tally_one(c)
        return carry

    lax.fori_loop(0, chunks, ending, 0)
    gone = keep_one(group - 1, quarter - 1, cohorts - 1)
    prefix[group - 1, quarter + 1] = prefix[group - 1, quarter] + gone
    adem1 = finish(0, 1)
    class_rows(0, adem1, [short1[k] for k in range(forage)], True)

    ones = jnp.ones((8, LANES), jnp.float32)
    sums = []
    for k in range(forage):
        lanes_sum = lax.dot_general(
            ones, by_class[k], (((1,), (1,)), ((), ())), precision=lax.Precision.HIGHEST,
            preferred_element_type=jnp.float32,
        )
        sums.append(lanes_sum[0:1])
    totals[me] = jnp.concatenate(sums, axis=0)

    def total_start(t, carry):
        other = lax.rem(me + t, tiles)
        remote(totals.at[me], totals.at[me], nsend.at[0], nrecv.at[0], other).start()
        return carry

    lax.fori_loop(1, tiles, total_start, 0)
    fill(adding, adem1)

    def outgoing(a, carry):
        out[a] = out[a] + adding[cls[a]]
        return carry

    lax.fori_loop(0, cohorts, outgoing, 0, unroll=4)
    sent_all(done1.at[mine], o1send.at[0], o1recv.at[0])
    for i in range(len(near)):
        if_near(i, lambda i: near_copy(i).wait_send())
    others = totals.at[pl.ds(0, tiles - 1)]
    wait_all(others, nrecv.at[0])
    grad_out[...] = lax.fori_loop(
        1, tiles, lambda t, total: total + totals[t], totals[0]
    ) / (tiles * blocks * LANES)
    sent_all(others, nsend.at[0], nrecv.at[0])


def last_kernel(*refs):
    count = len(refs) // 2
    copies = [
        pltpu.make_async_copy(refs[i], refs[count + i], refs[2 * count].at[i])
        for i in range(count)
    ]
    for copy in copies:
        copy.start()
    for copy in copies:
        copy.wait()


def blocked(x):
    rows, columns = x.shape[-2:]
    head = x.shape[:-2]
    n = len(head)
    y = x.reshape(head + (rows, columns // LANES, LANES))
    y = jnp.swapaxes(y, n, n + 1)
    return y.reshape(head + (rows * columns // LANES, LANES))


def unblocked(x, rows):
    head = x.shape[:-2]
    n = len(head)
    y = x.reshape(head + (x.shape[-2] // rows, rows, LANES))
    y = jnp.swapaxes(y, n, n + 1)
    return y.reshape(head + (rows, -1))


def shards(
    final_adjoint,
    first_density,
    second_density,
    forage,
    preference,
    base_mortality,
    age_class,
    land_mask,
    east_velocity,
    north_velocity,
):
    classes, groups = preference.shape
    cohorts, rows, columns = final_adjoint.shape
    tiles = lax.axis_size("tile")
    group = 2 * SUBSTEPS // rows
    quarter = cohorts // group
    chunks = 8
    blocks = rows * columns // LANES
    f32 = jnp.float32
    dma = pltpu.SemaphoreType.DMA
    vmem = pl.BlockSpec(memory_space=pltpu.VMEM)
    smem = pl.BlockSpec(memory_space=pltpu.SMEM)
    hbm = pl.BlockSpec(memory_space=pl.ANY)
    dims = (tiles, group, rows, cohorts, quarter, groups, chunks, 4, 2, 3)
    cell = (blocks, LANES)

    def body(*refs):
        kernel(dims, *refs)

    def cells(*lead):
        return pltpu.VMEM(lead + cell, f32)

    results = pl.pallas_call(
        body,
        out_shape=(
            cells(cohorts),
            cells(2, groups),
            pltpu.VMEM((groups, classes), f32),
        ),
        in_specs=[smem, vmem, smem] + [hbm] * 7,
        out_specs=(vmem, vmem, vmem),
        scratch_shapes=[
            cells(2 * group, quarter),
            cells(2 * group, quarter),
            cells(group + 1, groups),
            cells(group, quarter),
            cells(group, quarter),
            cells(group, quarter),
            cells(group, quarter),
            pltpu.VMEM((2 * group,) + cell, jnp.int32),
            cells(2 * group),
            cells(2 * group),
            pltpu.VMEM((2 * group * rows, 5, blocks // rows, LANES), f32),
            cells(group, groups),
            cells(groups),
            cells(groups),
            cells(4, groups),
            cells(cohorts),
            cells(cohorts),
            cells(2, groups),
            pltpu.VMEM((cohorts, LANES), f32),
            cells(classes),
            cells(classes),
            cells(classes),
            cells(classes),
            cells(group, classes),
            cells(2, classes),
            cells(classes),
            cells(group, quarter + 2),
            pltpu.VMEM((groups, classes, LANES), f32),
            pltpu.VMEM((tiles, groups, classes), f32),
            pltpu.SMEM((classes + 1,), jnp.int32),
        ]
        + [dma((1,)), dma((chunks,)), dma((2,)), dma((2, chunks)), dma((1,)), dma((chunks,))]
        + [dma((2,)), dma((2, chunks)), dma((1,)), dma((chunks,)), dma((3,)), dma((3,))]
        + [dma((3, 2)), dma((2, 3)), dma((1,)), dma((1,)), dma((group,)), dma((group,))]
        + [dma((1,)), dma((1,)), dma((6,))],
        compiler_params=pltpu.CompilerParams(
            collective_id=0, has_side_effects=True, vmem_limit_bytes=56 * 1024 * 1024
        ),
        name="adjoint",
    )(
        preference.T,
        base_mortality.reshape(1, -1),
        age_class,
        blocked(final_adjoint),
        blocked(first_density),
        blocked(second_density),
        blocked(forage),
        blocked(land_mask),
        blocked(east_velocity),
        blocked(north_velocity),
    )
    out, sens, grad = pl.pallas_call(
        last_kernel,
        out_shape=tuple(jax.ShapeDtypeStruct(x.shape, x.dtype) for x in results),
        in_specs=[vmem] * len(results),
        out_specs=(hbm,) * len(results),
        scratch_shapes=[dma((len(results),))],
        name="outgoing",
    )(*(pltpu.with_memory_space_constraint(x, pltpu.VMEM) for x in results))
    summed = grad.T
    return (unblocked(out, rows), unblocked(sens, rows), summed)


def solution(mesh):
    in_specs = (
        P("ens", "tile", None),
        P("ens", "tile", None),
        P("ens", "tile", None),
        P("ens", None, "tile", None),
        P("ens", None),
        P(),
        P(),
        P("tile", None),
        P("tile", None),
        P("tile", None),
    )
    out_specs = (P("ens", "tile", None), P("ens", None, "tile", None), P("ens", None))
    return jax.shard_map(shards, mesh=mesh, in_specs=in_specs, out_specs=out_specs, check_vma=False)
```

```python
import jax
import jax.numpy as jnp
from jax import lax
from jax.experimental import pallas as pl
from jax.experimental.pallas import tpu as pltpu
from jax.sharding import PartitionSpec as P

SUBSTEPS = 4
LANES = 128
MESH = pl.DeviceIdType.MESH


def kernel(
    dims,
    table_in,
    base_in,
    cls_in,
    lead,
    dens1_in,
    dens2_in,
    food_in,
    mask_in,
    east_in,
    north_in,
    out,
    sens,
    grad_out,
    wide2,
    wide1,
    wide_a,
    done2,
    done1,
    aged2,
    carried1,
    mask_strip,
    east_strip,
    north_strip,
    rates,
    short_all,
    short1,
    strewn,
    feed_sq,
    dens1,
    dens2,
    food,
    decay,
    kinds2,
    kinds1,
    moved,
    adding,
    living,
    crowd,
    dead,
    prefix,
    by_class,
    totals,
    bounds,
    table,
    base_row,
    cls,
    lsend,
    lrecv,
    zsend,
    zrecv,
    osend,
    orecv,
    z1send,
    z1recv,
    o1send,
    o1recv,
    fsend,
    frecv,
    hsend,
    hrecv,
    ssend,
    srecv,
    asend,
    arecv,
    nsend,
    nrecv,
    own_sem,
):
    tiles, group, rows, cohorts, quarter, forage, chunks, lead_ahead, out_lag, halo_ahead = dims
    half = group // 2
    size = quarter // chunks
    blocks = food.shape[2]
    per = blocks // rows
    reach = half * rows
    classes = table.shape[1]
    me = lax.axis_index("tile")
    q = lax.rem(me, group)
    first = me - q
    has_prev = me >= group
    has_next = me < tiles - group

    def peer(o):
        return first + lax.rem(q + o, group)

    def source(o):
        return lax.rem(q + group - o, group)

    barrier = pltpu.get_barrier_semaphore()
    spans = tiles // group
    twin = me + 1 - 2 * lax.rem(q, 2)
    across = peer(half)
    low = q < half
    beyond = [
        (has_next, me + group),
        (has_prev, me - group),
        (jnp.logical_and(jnp.logical_not(low), has_next), me + half),
        (jnp.logical_and(low, has_prev), me - half),
    ]
    if spans > 4:

        def greet(t, carry):
            other = lax.rem(me + t, tiles)
            pl.semaphore_signal(barrier, inc=1, device_id={"tile": other}, device_id_type=MESH)
            return carry

        lax.fori_loop(1, tiles, greet, 0)
    else:
        for o in range(1, group):
            pl.semaphore_signal(barrier, inc=1, device_id={"tile": peer(o)}, device_id_type=MESH)
        for there, other in beyond:

            @pl.when(there)
            def _(other=other):
                pl.semaphore_signal(
                    barrier, inc=1, device_id={"tile": other}, device_id_type=MESH
                )

    smalls = [
        pltpu.make_async_copy(src, dst, own_sem.at[6 + i])
        for i, (src, dst) in enumerate(((base_in, base_row), (cls_in, cls), (table_in, table)))
    ]
    for copy in smalls:
        copy.start()
    loads = [
        pltpu.make_async_copy(src, dst, own_sem.at[3 + i])
        for i, (src, dst) in enumerate(((dens2_in, dens2), (food_in, food), (dens1_in, dens1)))
    ]
    for copy in loads:
        copy.start()
    strips = ((mask_in, mask_strip), (east_in, east_strip), (north_in, north_strip))
    own_fields = [
        pltpu.make_async_copy(src, dst.at[half + q], own_sem.at[f])
        for f, (src, dst) in enumerate(strips)
    ]
    for copy in own_fields:
        copy.start()

    zero = jnp.zeros((blocks, LANES), jnp.float32)

    smalls[0].wait()
    fall = jnp.exp(-base_row[...])
    along = lax.broadcasted_iota(jnp.int32, (cohorts, cohorts), 1)
    down = lax.broadcasted_iota(jnp.int32, (cohorts, cohorts), 0)
    spread = jnp.where(along == down, fall, 0.0)
    decay[...] = jnp.broadcast_to(jnp.sum(spread, axis=1, keepdims=True), (cohorts, LANES))

    def bound(kind):
        spot = jnp.int32(0)
        width = 1
        while 2 * width <= cohorts:
            width = 2 * width
        while width >= 1:
            last = jnp.minimum(spot + width, cohorts) - 1
            ok = jnp.logical_and(spot + width <= cohorts, cls[last] < kind)
            spot = jnp.where(ok, spot + width, spot)
            width = width // 2
        return spot

    smalls[1].wait()
    smalls[2].wait()
    bounds[0] = jnp.int32(0)
    for kind in range(1, classes):
        bounds[kind] = bound(kind)
    bounds[classes] = jnp.int32(cohorts)

    if spans > 4:
        pl.semaphore_wait(barrier, tiles - 1)
    else:
        pl.semaphore_wait(barrier, group - 1 + sum(there.astype(jnp.int32) for there, _ in beyond))

    def remote(src, dst, ssem, rsem, target):
        return pltpu.make_async_remote_copy(
            src_ref=src, dst_ref=dst, send_sem=ssem, recv_sem=rsem,
            device_id={"tile": target}, device_id_type=MESH,
        )

    def spread_copy(buf, slot, ssem, rsem, i, target):
        return remote(buf.at[slot], buf.at[slot], ssem.at[i], rsem.at[i], target)

    def spread_start(buf, lift, ssem, rsem):
        spread_copy(buf, lift + q, ssem, rsem, 1, across).start()
        spread_copy(buf, lift + q, ssem, rsem, 0, twin).start()

    def spread_pass(buf, lift, ssem, rsem):
        slot = lift + across - first
        spread_copy(buf, slot, ssem, rsem, 1, across).wait_recv()
        spread_copy(buf, slot, ssem, rsem, 2, twin).start()

    def spread_wait(buf, lift, ssem, rsem):
        spread_copy(buf, lift + twin - first, ssem, rsem, 0, twin).wait_recv()
        spread_copy(buf, lift + lax.rem(twin - first + half, group), ssem, rsem, 2, twin).wait_recv()

    def spread_sent(buf, lift, ssem, rsem):
        for i in range(3):
            spread_copy(buf, lift + q, ssem, rsem, i, twin).wait_send()

    def halo(buf, lo, ssem, rsem, c):
        def part(begin):
            if lo is None:
                return buf.at[pl.ds(begin, half)]
            return buf.at[pl.ds(begin, half), pl.ds(lo, size)]

        down = remote(part(group), part(0), ssem.at[0], rsem.at[0, c], me + group)
        up = remote(part(half), part(group + half), ssem.at[1], rsem.at[1, c], me - group)
        return down, up

    def halo_start(*args):
        down, up = halo(*args)

        @pl.when(has_next)
        def _():
            down.start()

        @pl.when(has_prev)
        def _():
            up.start()

    def halo_wait(*args):
        down, up = halo(*args)

        @pl.when(has_prev)
        def _():
            down.wait_recv()

        @pl.when(has_next)
        def _():
            up.wait_recv()

    def halo_sent(spot, ssem, rsem):
        @pl.when(has_next)
        def _():
            sent_all(spot, ssem.at[0], rsem.at[0, 0])

        @pl.when(has_prev)
        def _():
            sent_all(spot, ssem.at[1], rsem.at[1, 0])

    for f, (src, dst) in enumerate(strips):
        own_fields[f].wait()
        spread_start(dst, half, fsend.at[f], frecv.at[f])

    def lead_pieces(c):
        return ((c * size, size - 1), (c * size + size - 1, 1))

    def lead_copy(o, c, lo, count):
        begin = jnp.minimum(lax.rem(q + o, group) * quarter + 1 + lo, cohorts - count)
        return remote(
            lead.at[pl.ds(begin, count)], wide2.at[half + q, pl.ds(lo, count)],
            lsend.at[0], lrecv.at[c], peer(o),
        )

    def lead_own(c, lo, count):
        begin = jnp.minimum(q * quarter + 1 + lo, cohorts - count)
        return pltpu.make_async_copy(
            lead.at[pl.ds(begin, count)], wide2.at[half + q, pl.ds(lo, count)], lrecv.at[c]
        )

    def lead_start(c):
        for piece in lead_pieces(c):
            for o in range(1, group):
                lead_copy(o, c, *piece).start()
            lead_own(c, *piece).start()

    def wait_all(spot, sem):
        pltpu.make_async_copy(spot, spot, sem).wait()

    def sent_all(spot, ssem, rsem):
        remote(spot, spot, ssem, rsem, peer(1)).wait_send()

    def lead_wait(c):
        wait_all(wide2.at[pl.ds(half, group), pl.ds(c * size, size)], lrecv.at[c])

    lead_start(0)
    lead_start(1)

    strips_all = (mask_strip, east_strip, north_strip)
    wides = (wide2, wide1)

    @pl.when(jnp.logical_not(has_prev))
    def _():
        for strip in strips_all:
            strip[0:half] = jnp.zeros((half,) + strip.shape[1:], strip.dtype)
        for wide in wides:
            wide[0:half] = jnp.zeros((half,) + wide.shape[1:], jnp.float32)

    @pl.when(jnp.logical_not(has_next))
    def _():
        for strip in strips_all:
            strip[group + half :] = jnp.zeros((half,) + strip.shape[1:], strip.dtype)
        for wide in wides:
            wide[group + half :] = jnp.zeros((half,) + wide.shape[1:], jnp.float32)

    for d in (d for d in range(-half, half + 1) if d != 0):

        @pl.when(jnp.logical_not(jnp.logical_and(me + d >= 0, me + d < tiles)))
        def _(d=d):
            wide_a[half + d] = jnp.zeros(wide_a.shape[1:], jnp.float32)

    for part in range(group):
        prefix[part, 0] = zero

    def upto(spot):
        total = prefix[0, jnp.clip(spot, 0, quarter)]
        for part in range(1, group):
            top = quarter + (part == group - 1)
            total = total + prefix[part, jnp.clip(spot - part * quarter, 0, top)]
        return total

    def weighted(kind, values):
        total = table[0, kind] * values[0]
        for k in range(1, forage):
            total = total + table[k, kind] * values[k]
        return total

    def class_sums(store, shift):
        def step(kind, carry):
            before, sums = carry
            here = upto(bounds[kind + 1] + shift)
            own = here - before
            store(kind, own)
            return here, tuple(sums[k] + table[k, kind] * own for k in range(forage))

        return lax.fori_loop(0, classes, step, (upto(shift), (zero,) * forage), unroll=4)[1]

    def fill(into, values, decaying=False):
        def each(kind, carry):
            total = weighted(kind, values)
            into[kind] = jnp.exp(-total) if decaying else total
            return carry

        lax.fori_loop(0, classes, each, 0, unroll=2)

    def prepare(month, dens, by_kind, short_store):
        def add(i, runs):
            new = []
            for part in range(group):
                new.append(runs[part] + dens[part * quarter + i])
                prefix[part, i + 1] = new[part]
            return tuple(new)

        lax.fori_loop(0, quarter, add, (zero,) * group, unroll=2)

        def store(kind, own):
            crowd[month, kind] = own

        hungry = class_sums(store, 0)
        shorts = []
        for k in range(forage):
            feed = food[month, k]
            total = feed + hungry[k]
            shorts.append(hungry[k] / total)
            short_store(k, shorts[k])
            feed_sq[month, k] = feed / (total * total)
            feed_sq[2 + month, k] = hungry[k]
        return shorts

    def store_two(k, value):
        short_all[q, k] = value

    def store_one(k, value):
        short1[k] = value

    loads[0].wait()
    loads[1].wait()
    shorts2 = prepare(1, dens2, kinds2, store_two)
    spread_start(short_all, 0, ssend, srecv)
    lead_start(2)
    fill(kinds2, shorts2, True)

    for f, (src, dst) in enumerate(strips):
        spread_pass(dst, half, fsend.at[f], frecv.at[f])
    loads[2].wait()
    shorts1 = prepare(0, dens1, kinds1, store_one)
    fill(kinds1, shorts1, True)
    lead_start(3)
    for f, (src, dst) in enumerate(strips):
        spread_wait(dst, half, fsend.at[f], frecv.at[f])
        halo_start(dst, None, hsend.at[f], hrecv, f)

    lane = lax.broadcasted_iota(jnp.int32, (per, LANES), 1)
    last_lane = lane == LANES - 1
    first_lane = lane == 0

    def east_of(x):
        near = pltpu.roll(x, LANES - 1, 1)
        return jnp.where(last_lane, pltpu.roll(near, per - 1, 0), near)

    def west_of(x):
        near = pltpu.roll(x, 1, 1)
        return jnp.where(first_lane, pltpu.roll(near, 1, 0), near)

    def row_of(r):
        return pl.ds(r % rows, per, stride=rows)

    lead_wait(0)
    halo_start(wide2, 0, zsend, zrecv, 0)
    lead_start(4)
    for f, (src, dst) in enumerate(strips):
        halo_wait(dst, None, hsend.at[f], hrecv, f)
    span_rows = rows * 2 * group
    masks = [mask_strip[r // rows, row_of(r)].astype(jnp.float32) for r in range(span_rows)]
    for r in range(1, span_rows - 1):
        mask = masks[r]
        east, north = east_strip[r // rows, row_of(r)], north_strip[r // rows, row_of(r)]
        rate_n = mask * masks[r - 1] * (0.1 + jnp.maximum(north, 0.0))
        rate_s = mask * masks[r + 1] * (0.1 + jnp.maximum(-north, 0.0))
        rate_e = mask * east_of(mask) * (0.1 + jnp.maximum(east, 0.0))
        rate_w = mask * west_of(mask) * (0.1 + jnp.maximum(-east, 0.0))
        rates[r, 0] = 1.0 - rate_n - rate_s - rate_e - rate_w
        rates[r, 1] = rate_n
        rates[r, 2] = rate_s
        rates[r, 3] = rate_e
        rates[r, 4] = rate_w

    def advance(fields, shift):
        count = len(fields[0])
        for step in range(SUBSTEPS):
            margin = step + 1
            fresh = [[None] * count for _ in fields]
            for u, old in enumerate(fields):
                for r in range(margin, count - margin):
                    rate = rates.at[r + shift]
                    fresh[u][r] = (
                        rate[0] * old[r]
                        + rate[1] * old[r - 1]
                        + rate[2] * old[r + 1]
                        + rate[3] * east_of(old[r])
                        + rate[4] * west_of(old[r])
                    )
            fields = fresh
        return fields

    def transport(wide, done, c):
        fields = [
            [wide[r // rows, c * size + u, row_of(r)] for r in range(span_rows)]
            for u in range(size)
        ]
        for u, field in enumerate(advance(fields, 0)):
            for r in range(rows * group):
                done[r // rows, c * size + u, row_of(r)] = field[reach + r]

    def out_start(done, into, c, ssem, rsem):
        spot = into.at[q, pl.ds(c * size, size)]
        for o in range(1, group):
            part = done.at[lax.rem(q + o, group), pl.ds(c * size, size)]
            remote(part, spot, ssem.at[0], rsem.at[c], peer(o)).start()
        pltpu.make_async_copy(done.at[q, pl.ds(c * size, size)], spot, rsem.at[c]).start()

    def out_wait(into, c, rsem):
        wait_all(into.at[pl.ds(0, group), pl.ds(c * size, size)], rsem.at[c])

    def middle(c):
        def each(i, carry):
            a = q * quarter + i
            kind = cls[a]
            fading = decay[pl.ds(a, 1)]
            for s in range(group):
                wide1[half + s, i] = done2[s, i] * (fading * living[s, kind])
            return carry

        lax.fori_loop(c * size, c * size + size, each, 0)

    def halo_one(c):
        halo_start(wide1, c * size, z1send, z1recv, c)

    def tally_two(c):
        def step(i, runs):
            new = []
            for part in range(group):
                a = part * quarter + i
                gone = aged2[part, i] * (decay[pl.ds(a, 1)] * kinds2[cls[a]])
                new.append(runs[part] + gone * dens2[a])
                prefix[part, i + 1] = new[part]
            return tuple(new)

        begin = tuple(prefix[part, c * size] for part in range(group))
        lax.fori_loop(c * size, c * size + size, step, begin)

    def keep_one(part, i, before):
        value = carried1[part, i] + moved[cls[part * quarter + i]]
        stay = value * (decay[pl.ds(before, 1)] * kinds1[cls[before]])
        out[before] = stay
        return stay * dens1[before]

    def tally_one(c):
        def step(i, runs):
            new = []
            for part in range(group):
                before = jnp.maximum(part * quarter + i - 1, 0)
                new.append(runs[part] + keep_one(part, i, before))
                prefix[part, i + 1] = new[part]
            return tuple(new)

        begin = tuple(prefix[part, c * size] for part in range(group))
        lax.fori_loop(c * size, c * size + size, step, begin)

    def finish(month, shift):
        def store(kind, own):
            dead[kind] = own

        ratio = class_sums(store, shift)
        adem = []
        for k in range(forage):
            adem.append(-ratio[k] * feed_sq[month, k])
            sens[month, k] = ratio[k] * feed_sq[2 + month, k] * feed_sq[month, k]
        return adem

    def class_rows(month, adem, short, add):
        def each(kind, carry):
            many, lost = crowd[month, kind], dead[kind]
            for k in range(forage):
                row = jnp.sum(many * adem[k] - lost * short[k], axis=0, keepdims=True)
                if add:
                    row = row + by_class[k, pl.ds(kind, 1)]
                by_class[k, pl.ds(kind, 1)] = row
            return carry

        lax.fori_loop(0, classes, each, 0, unroll=2)

    def live(s, carry):
        shorts = [short_all[s, k] for k in range(forage)]
        fill(living.at[s], shorts, True)
        return carry

    def second(c, carry):
        halo_wait(wide2, c * size, zsend, zrecv, c)

        @pl.when(c == chunks - 1)
        def _():
            for b in range(halo_ahead):
                halo_one(b)

        transport(wide2, done2, c)

        @pl.when(c >= out_lag)
        def _():
            out_start(done2, aged2, c - out_lag, osend, orecv)

        @pl.when(c == 0)
        def _():
            spread_wait(short_all, 0, ssend, srecv)
            lax.fori_loop(0, group, live, 0)

        middle(c)

        @pl.when(c + 2 < chunks)
        def _():
            lead_wait(c + 2)
            halo_start(wide2, (c + 2) * size, zsend, zrecv, c + 2)

        @pl.when(c + 2 + lead_ahead < chunks)
        def _():
            lead_start(c + 2 + lead_ahead)

        return carry

    spread_pass(short_all, 0, ssend, srecv)
    lead_wait(1)
    halo_start(wide2, size, zsend, zrecv, 1)
    lead_start(5)
    lax.fori_loop(0, chunks, second, 0)
    for c in range(chunks - out_lag, chunks):
        out_start(done2, aged2, c, osend, orecv)

    odd = lax.rem(q, 2)
    side = 1 - 2 * odd
    steps = [(jnp.logical_or(low, has_next), half), (jnp.logical_or(~low, has_prev), -half)]
    onward = jnp.where(odd == 0, steps[0][0], steps[1][0])
    inward = jnp.where(odd == 0, steps[1][0], steps[0][0])

    def near_copy(d, i):
        return remote(
            wide_a.at[half], wide_a.at[half - d], asend.at[i], arecv.at[i], me + d
        )

    def near_start():
        for i, (there, d) in enumerate(steps):

            @pl.when(there)
            def _(i=i, d=d):
                near_copy(d, i).start()

        near_copy(side, 2).start()

    def near_from(slot, i):
        spot = wide_a.at[slot]
        remote(spot, spot, asend.at[i], arecv.at[i], twin).wait_recv()

    def near_pass():
        for i, (there, d) in enumerate(steps):

            @pl.when(steps[1 - i][0])
            def _(i=i, d=d):
                near_from(half - d, i)

        @pl.when(onward)
        def _():
            remote(
                wide_a.at[half + half * side], wide_a.at[half + side], asend.at[3], arecv.at[3],
                twin,
            ).start()

    def near_wait():
        near_from(half + side, 2)

        @pl.when(inward)
        def _():
            near_from(half - side, 3)

    def near_sent():
        for i, (there, d) in enumerate(steps):

            @pl.when(there)
            def _(i=i, d=d):
                near_copy(d, i).wait_send()

        near_copy(side, 2).wait_send()

        @pl.when(onward)
        def _():
            near_copy(side, 3).wait_send()

    def gather_two(c, carry):
        out_wait(aged2, c, orecv)
        tally_two(c)
        return carry

    def leading(c, carry):
        halo_wait(wide1, c * size, z1send, z1recv, c)

        @pl.when(c + halo_ahead < chunks)
        def _():
            halo_one(c + halo_ahead)

        transport(wide1, done1, c)
        out_start(done1, carried1, c, o1send, o1recv)

        @pl.when(c == chunks // 2 - 1)
        def _():
            lax.fori_loop(0, chunks, gather_two, 0)
            adem2 = finish(1, 0)
            for k in range(forage):
                wide_a[half, k] = adem2[k]
            near_start()
            class_rows(1, adem2, [short_all[q, k] for k in range(forage)], False)

        return carry

    lax.fori_loop(0, chunks, leading, 0)

    mine = pl.ds(0, group - 1)
    sent_all(wide2.at[mine], lsend.at[0], lrecv.at[0])
    sent_all(done2.at[mine], osend.at[0], orecv.at[0])
    spread_sent(short_all, 0, ssend, srecv)
    halo_sent(wide2.at[pl.ds(0, half)], zsend, zrecv)
    halo_sent(wide1.at[pl.ds(0, half)], z1send, z1recv)
    for f, (src, dst) in enumerate(strips):
        spread_sent(dst, half, fsend.at[f], frecv.at[f])
        halo_sent(dst.at[pl.ds(0, half)], hsend.at[f], hrecv)
    near_pass()
    near_wait()

    reach_rows = rows * (2 * half + 1)
    fields = [
        [wide_a[r // rows, k, row_of(r)] for r in range(reach_rows)] for k in range(forage)
    ]
    for k, field in enumerate(advance(fields, rows * q)):
        for r in range(rows):
            strewn[k, row_of(r)] = field[reach + r]
    fill(moved, [strewn[k] for k in range(forage)])

    def ending(c, carry):
        out_wait(carried1, c, o1recv)
        tally_one(c)
        return carry

    lax.fori_loop(0, chunks, ending, 0)
    gone = keep_one(group - 1, quarter - 1, cohorts - 1)
    prefix[group - 1, quarter + 1] = prefix[group - 1, quarter] + gone
    adem1 = finish(0, 1)
    class_rows(0, adem1, [short1[k] for k in range(forage)], True)

    ones = jnp.ones((8, LANES), jnp.float32)
    sums = []
    for k in range(forage):
        lanes_sum = lax.dot_general(
            ones, by_class[k], (((1,), (1,)), ((), ())), precision=lax.Precision.HIGHEST,
            preferred_element_type=jnp.float32,
        )
        sums.append(lanes_sum[0:1])
    totals[me] = jnp.concatenate(sums, axis=0)

    def total_start(t, carry):
        other = lax.rem(me + t, tiles)
        remote(totals.at[me], totals.at[me], nsend.at[0], nrecv.at[0], other).start()
        return carry

    lax.fori_loop(1, tiles, total_start, 0)
    fill(adding, adem1)

    def outgoing(a, carry):
        out[a] = out[a] + adding[cls[a]]
        return carry

    lax.fori_loop(0, cohorts, outgoing, 0, unroll=4)
    sent_all(done1.at[mine], o1send.at[0], o1recv.at[0])
    near_sent()
    others = totals.at[pl.ds(0, tiles - 1)]
    wait_all(others, nrecv.at[0])
    grad_out[...] = lax.fori_loop(
        1, tiles, lambda t, total: total + totals[t], totals[0]
    ) / (tiles * blocks * LANES)
    sent_all(others, nsend.at[0], nrecv.at[0])


def last_kernel(*refs):
    count = len(refs) // 2
    copies = [
        pltpu.make_async_copy(refs[i], refs[count + i], refs[2 * count].at[i])
        for i in range(count)
    ]
    for copy in copies:
        copy.start()
    for copy in copies:
        copy.wait()


def blocked(x):
    rows, columns = x.shape[-2:]
    head = x.shape[:-2]
    n = len(head)
    y = x.reshape(head + (rows, columns // LANES, LANES))
    y = jnp.swapaxes(y, n, n + 1)
    return y.reshape(head + (rows * columns // LANES, LANES))


def unblocked(x, rows):
    head = x.shape[:-2]
    n = len(head)
    y = x.reshape(head + (x.shape[-2] // rows, rows, LANES))
    y = jnp.swapaxes(y, n, n + 1)
    return y.reshape(head + (rows, -1))


def shards(
    final_adjoint,
    first_density,
    second_density,
    forage,
    preference,
    base_mortality,
    age_class,
    land_mask,
    east_velocity,
    north_velocity,
):
    classes, groups = preference.shape
    cohorts, rows, columns = final_adjoint.shape
    tiles = lax.axis_size("tile")
    group = 2 * SUBSTEPS // rows
    quarter = cohorts // group
    chunks = 8
    blocks = rows * columns // LANES
    f32 = jnp.float32
    dma = pltpu.SemaphoreType.DMA
    vmem = pl.BlockSpec(memory_space=pltpu.VMEM)
    smem = pl.BlockSpec(memory_space=pltpu.SMEM)
    hbm = pl.BlockSpec(memory_space=pl.ANY)
    dims = (tiles, group, rows, cohorts, quarter, groups, chunks, 4, 2, 3)
    cell = (blocks, LANES)

    def body(*refs):
        kernel(dims, *refs)

    def cells(*lead):
        return pltpu.VMEM(lead + cell, f32)

    results = pl.pallas_call(
        body,
        out_shape=(
            cells(cohorts),
            cells(2, groups),
            pltpu.VMEM((groups, classes), f32),
        ),
        in_specs=[hbm] * 10,
        out_specs=(vmem, vmem, vmem),
        scratch_shapes=[
            cells(2 * group, quarter),
            cells(2 * group, quarter),
            cells(group + 1, groups),
            cells(group, quarter),
            cells(group, quarter),
            cells(group, quarter),
            cells(group, quarter),
            pltpu.VMEM((2 * group,) + cell, jnp.int32),
            cells(2 * group),
            cells(2 * group),
            pltpu.VMEM((2 * group * rows, 5, blocks // rows, LANES), f32),
            cells(group, groups),
            cells(groups),
            cells(groups),
            cells(4, groups),
            cells(cohorts),
            cells(cohorts),
            cells(2, groups),
            pltpu.VMEM((cohorts, LANES), f32),
            cells(classes),
            cells(classes),
            cells(classes),
            cells(classes),
            cells(group, classes),
            cells(2, classes),
            cells(classes),
            cells(group, quarter + 2),
            pltpu.VMEM((groups, classes, LANES), f32),
            pltpu.VMEM((tiles, groups, classes), f32),
            pltpu.SMEM((classes + 1,), jnp.int32),
            pltpu.SMEM((groups, classes), f32),
            pltpu.VMEM((1, cohorts), f32),
            pltpu.SMEM((cohorts,), jnp.int32),
        ]
        + [dma((1,)), dma((chunks,)), dma((2,)), dma((2, chunks)), dma((1,)), dma((chunks,))]
        + [dma((2,)), dma((2, chunks)), dma((1,)), dma((chunks,)), dma((3, 3)), dma((3, 3))]
        + [dma((3, 2)), dma((2, 3)), dma((3,)), dma((3,)), dma((4,)), dma((4,))]
        + [dma((1,)), dma((1,)), dma((9,))],
        compiler_params=pltpu.CompilerParams(
            collective_id=0, has_side_effects=True, vmem_limit_bytes=56 * 1024 * 1024
        ),
        name="adjoint",
    )(
        preference.T,
        base_mortality.reshape(1, -1),
        age_class,
        blocked(final_adjoint),
        blocked(first_density),
        blocked(second_density),
        blocked(forage),
        blocked(land_mask),
        blocked(east_velocity),
        blocked(north_velocity),
    )
    out, sens, grad = pl.pallas_call(
        last_kernel,
        out_shape=tuple(jax.ShapeDtypeStruct(x.shape, x.dtype) for x in results),
        in_specs=[vmem] * len(results),
        out_specs=(hbm,) * len(results),
        scratch_shapes=[dma((len(results),))],
        name="outgoing",
    )(*(pltpu.with_memory_space_constraint(x, pltpu.VMEM) for x in results))
    summed = grad.T
    return (unblocked(out, rows), unblocked(sens, rows), summed)


def solution(mesh):
    in_specs = (
        P("ens", "tile", None),
        P("ens", "tile", None),
        P("ens", "tile", None),
        P("ens", None, "tile", None),
        P("ens", None),
        P(),
        P(),
        P("tile", None),
        P("tile", None),
        P("tile", None),
    )
    out_specs = (P("ens", "tile", None), P("ens", None, "tile", None), P("ens", None))
    return jax.shard_map(shards, mesh=mesh, in_specs=in_specs, out_specs=out_specs, check_vma=False)
```

```python
import jax
import jax.numpy as jnp
from jax import lax
from jax.experimental import pallas as pl
from jax.experimental.pallas import tpu as pltpu
from jax.sharding import PartitionSpec as P

SUBSTEPS = 4
LANES = 128
MESH = pl.DeviceIdType.MESH


def kernel(
    dims,
    table_in,
    base_in,
    cls_in,
    lead,
    dens1_in,
    dens2_in,
    food_in,
    mask_in,
    east_in,
    north_in,
    out,
    sens,
    grad_out,
    wide2,
    wide1,
    wide_a,
    done2,
    done1,
    done_b,
    aged2,
    aged_b,
    carried1,
    carried_b,
    mask_strip,
    east_strip,
    north_strip,
    rates,
    short_all,
    short1,
    strewn,
    feed_sq,
    dens1,
    dens2,
    food,
    decay,
    kinds2,
    kinds1,
    moved,
    adding,
    living,
    crowd,
    dead,
    prefix,
    by_class,
    totals,
    bounds,
    table,
    base_row,
    cls,
    lsend,
    lrecv,
    zsend,
    zrecv,
    osend,
    orecv,
    z1send,
    z1recv,
    o1send,
    o1recv,
    fsend,
    frecv,
    hsend,
    hrecv,
    ssend,
    srecv,
    asend,
    arecv,
    nsend,
    nrecv,
    own_sem,
):
    tiles, group, rows, cohorts, size, alone, chunks, forage, lead_ahead, out_lag, halo_ahead = dims
    half = group // 2
    own = alone * size
    both = (chunks - alone) * size
    pooled = group * own
    blocks = food.shape[2]
    per = blocks // rows
    reach = half * rows
    classes = table.shape[1]
    me = lax.axis_index("tile")
    q = lax.rem(me, group)
    first = me - q
    has_prev = me >= group
    has_next = me < tiles - group

    def peer(o):
        return first + lax.rem(q + o, group)

    def source(o):
        return lax.rem(q + group - o, group)

    barrier = pltpu.get_barrier_semaphore()
    spans = tiles // group
    twin = me + 1 - 2 * lax.rem(q, 2)
    across = peer(half)
    low = q < half
    core = lax.rem(q, 2)
    beyond = [
        (has_next, me + group),
        (has_prev, me - group),
        (jnp.logical_and(jnp.logical_not(low), has_next), me + half),
        (jnp.logical_and(low, has_prev), me - half),
    ]
    if spans > 4:

        def greet(t, carry):
            other = lax.rem(me + t, tiles)
            pl.semaphore_signal(barrier, inc=1, device_id={"tile": other}, device_id_type=MESH)
            return carry

        lax.fori_loop(1, tiles, greet, 0)
    else:
        for o in range(1, group):
            pl.semaphore_signal(barrier, inc=1, device_id={"tile": peer(o)}, device_id_type=MESH)
        for there, other in beyond:

            @pl.when(there)
            def _(other=other):
                pl.semaphore_signal(
                    barrier, inc=1, device_id={"tile": other}, device_id_type=MESH
                )

    smalls = [
        pltpu.make_async_copy(src, dst, own_sem.at[6 + i])
        for i, (src, dst) in enumerate(((base_in, base_row), (cls_in, cls), (table_in, table)))
    ]
    for copy in smalls:
        copy.start()
    loads = [
        pltpu.make_async_copy(src, dst, own_sem.at[3 + i])
        for i, (src, dst) in enumerate(((dens2_in, dens2), (food_in, food), (dens1_in, dens1)))
    ]
    for copy in loads:
        copy.start()
    strips = ((mask_in, mask_strip), (east_in, east_strip), (north_in, north_strip))
    own_fields = [
        pltpu.make_async_copy(src, dst.at[half + q], own_sem.at[f])
        for f, (src, dst) in enumerate(strips)
    ]
    for copy in own_fields:
        copy.start()

    zero = jnp.zeros((blocks, LANES), jnp.float32)

    smalls[0].wait()
    fall = jnp.exp(-base_row[...])
    along = lax.broadcasted_iota(jnp.int32, (cohorts, cohorts), 1)
    down = lax.broadcasted_iota(jnp.int32, (cohorts, cohorts), 0)
    spread = jnp.where(along == down, fall, 0.0)
    decay[...] = jnp.broadcast_to(jnp.sum(spread, axis=1, keepdims=True), (cohorts, LANES))

    def bound(kind):
        spot = jnp.int32(0)
        width = 1
        while 2 * width <= cohorts:
            width = 2 * width
        while width >= 1:
            last = jnp.minimum(spot + width, cohorts) - 1
            ok = jnp.logical_and(spot + width <= cohorts, cls[last] < kind)
            spot = jnp.where(ok, spot + width, spot)
            width = width // 2
        return spot

    smalls[1].wait()
    smalls[2].wait()
    bounds[0] = jnp.int32(0)
    for kind in range(1, classes):
        bounds[kind] = bound(kind)
    bounds[classes] = jnp.int32(cohorts)

    if spans > 4:
        pl.semaphore_wait(barrier, tiles - 1)
    else:
        pl.semaphore_wait(barrier, group - 1 + sum(there.astype(jnp.int32) for there, _ in beyond))

    def remote(src, dst, ssem, rsem, target):
        return pltpu.make_async_remote_copy(
            src_ref=src, dst_ref=dst, send_sem=ssem, recv_sem=rsem,
            device_id={"tile": target}, device_id_type=MESH,
        )

    def spread_copy(buf, slot, ssem, rsem, i, target):
        return remote(buf.at[slot], buf.at[slot], ssem.at[i], rsem.at[i], target)

    def spread_start(buf, lift, ssem, rsem):
        spread_copy(buf, lift + q, ssem, rsem, 1, across).start()
        spread_copy(buf, lift + q, ssem, rsem, 0, twin).start()

    def spread_pass(buf, lift, ssem, rsem):
        slot = lift + across - first
        spread_copy(buf, slot, ssem, rsem, 1, across).wait_recv()
        spread_copy(buf, slot, ssem, rsem, 2, twin).start()

    def spread_wait(buf, lift, ssem, rsem):
        spread_copy(buf, lift + twin - first, ssem, rsem, 0, twin).wait_recv()
        spread_copy(buf, lift + lax.rem(twin - first + half, group), ssem, rsem, 2, twin).wait_recv()

    def spread_sent(buf, lift, ssem, rsem):
        for i in range(3):
            spread_copy(buf, lift + q, ssem, rsem, i, twin).wait_send()

    def halo(buf, lo, ssem, rsem, c):
        def part(begin):
            if lo is None:
                return buf.at[pl.ds(begin, half)]
            return buf.at[pl.ds(begin, half), pl.ds(lo, size)]

        down = remote(part(group), part(0), ssem.at[0], rsem.at[0, c], me + group)
        up = remote(part(half), part(group + half), ssem.at[1], rsem.at[1, c], me - group)
        return down, up

    def halo_start(*args):
        down, up = halo(*args)

        @pl.when(has_next)
        def _():
            down.start()

        @pl.when(has_prev)
        def _():
            up.start()

    def halo_wait(*args):
        down, up = halo(*args)

        @pl.when(has_prev)
        def _():
            down.wait_recv()

        @pl.when(has_next)
        def _():
            up.wait_recv()

    def halo_sent(spot, ssem, rsem):
        @pl.when(has_next)
        def _():
            sent_all(spot, ssem.at[0], rsem.at[0, 0])

        @pl.when(has_prev)
        def _():
            sent_all(spot, ssem.at[1], rsem.at[1, 0])

    for f, (src, dst) in enumerate(strips):
        own_fields[f].wait()
        spread_start(dst, half, fsend.at[f], frecv.at[f])

    def lead_pieces(c):
        return ((c * size, size - 1), (c * size + size - 1, 1))

    def item_shift(c, who):
        shared = pooled + both * lax.rem(who, 2) - own
        return jnp.where(c < alone, own * who, shared)

    def lead_copy(o, c, lo, count):
        begin = jnp.minimum(item_shift(c, lax.rem(q + o, group)) + 1 + lo, cohorts - count)
        return remote(
            lead.at[pl.ds(begin, count)], wide2.at[half + q, pl.ds(lo, count)],
            lsend.at[0], lrecv.at[c], peer(o),
        )

    def lead_own(c, lo, count):
        begin = jnp.minimum(item_shift(c, q) + 1 + lo, cohorts - count)
        return pltpu.make_async_copy(
            lead.at[pl.ds(begin, count)], wide2.at[half + q, pl.ds(lo, count)], lrecv.at[c]
        )

    def lead_start(c):
        for piece in lead_pieces(c):
            for o in range(1, group):
                lead_copy(o, c, *piece).start()
            lead_own(c, *piece).start()

    def wait_all(spot, sem):
        pltpu.make_async_copy(spot, spot, sem).wait()

    def sent_all(spot, ssem, rsem):
        remote(spot, spot, ssem, rsem, peer(1)).wait_send()

    def lead_wait(c):
        wait_all(wide2.at[pl.ds(half, group), pl.ds(c * size, size)], lrecv.at[c])

    lead_start(0)
    lead_start(1)

    strips_all = (mask_strip, east_strip, north_strip)
    wides = (wide2, wide1)

    @pl.when(jnp.logical_not(has_prev))
    def _():
        for strip in strips_all:
            strip[0:half] = jnp.zeros((half,) + strip.shape[1:], strip.dtype)
        for wide in wides:
            wide[0:half] = jnp.zeros((half,) + wide.shape[1:], jnp.float32)

    @pl.when(jnp.logical_not(has_next))
    def _():
        for strip in strips_all:
            strip[group + half :] = jnp.zeros((half,) + strip.shape[1:], strip.dtype)
        for wide in wides:
            wide[group + half :] = jnp.zeros((half,) + wide.shape[1:], jnp.float32)

    for d in (d for d in range(-half, half + 1) if d != 0):

        @pl.when(jnp.logical_not(jnp.logical_and(me + d >= 0, me + d < tiles)))
        def _(d=d):
            wide_a[half + d] = jnp.zeros(wide_a.shape[1:], jnp.float32)

    for part in range(group + 2):
        prefix[part, 0] = zero
    starts = [part * own for part in range(group)] + [pooled, pooled + both]
    lengths = [own] * group + [both] * 2

    def upto(spot):
        total = zero
        for part in range(group + 2):
            top = lengths[part] + (part == group + 1)
            total = total + prefix[part, jnp.clip(spot - starts[part], 0, top)]
        return total

    def weighted(kind, values):
        total = table[0, kind] * values[0]
        for k in range(1, forage):
            total = total + table[k, kind] * values[k]
        return total

    def class_sums(store, shift):
        def step(kind, carry):
            before, sums = carry
            here = upto(bounds[kind + 1] + shift)
            some = here - before
            store(kind, some)
            return here, tuple(sums[k] + table[k, kind] * some for k in range(forage))

        return lax.fori_loop(0, classes, step, (upto(shift), (zero,) * forage), unroll=4)[1]

    def fill(into, values, decaying=False):
        def each(kind, carry):
            total = weighted(kind, values)
            into[kind] = jnp.exp(-total) if decaying else total
            return carry

        lax.fori_loop(0, classes, each, 0, unroll=2)

    def prepare(month, dens, by_kind, short_store):
        def adder(parts):
            def add(i, runs):
                new = []
                for part, run in zip(parts, runs):
                    new.append(run + dens[starts[part] + i])
                    prefix[part, i + 1] = new[-1]
                return tuple(new)

            return add

        for parts in (range(group), range(group, group + 2)):
            lax.fori_loop(
                0, lengths[parts[0]], adder(parts), (zero,) * len(parts), unroll=2
            )

        def store(kind, some):
            crowd[month, kind] = some

        hungry = class_sums(store, 0)
        shorts = []
        for k in range(forage):
            feed = food[month, k]
            total = feed + hungry[k]
            shorts.append(hungry[k] / total)
            short_store(k, shorts[k])
            feed_sq[month, k] = feed / (total * total)
            feed_sq[2 + month, k] = hungry[k]
        return shorts

    def store_two(k, value):
        short_all[q, k] = value

    def store_one(k, value):
        short1[k] = value

    loads[0].wait()
    loads[1].wait()
    shorts2 = prepare(1, dens2, kinds2, store_two)
    spread_start(short_all, 0, ssend, srecv)
    lead_start(2)
    fill(kinds2, shorts2, True)

    for f, (src, dst) in enumerate(strips):
        spread_pass(dst, half, fsend.at[f], frecv.at[f])
    loads[2].wait()
    shorts1 = prepare(0, dens1, kinds1, store_one)
    fill(kinds1, shorts1, True)
    lead_start(3)
    for f, (src, dst) in enumerate(strips):
        spread_wait(dst, half, fsend.at[f], frecv.at[f])
        halo_start(dst, None, hsend.at[f], hrecv, f)

    lane = lax.broadcasted_iota(jnp.int32, (per, LANES), 1)
    last_lane = lane == LANES - 1
    first_lane = lane == 0

    def east_of(x):
        near = pltpu.roll(x, LANES - 1, 1)
        return jnp.where(last_lane, pltpu.roll(near, per - 1, 0), near)

    def west_of(x):
        near = pltpu.roll(x, 1, 1)
        return jnp.where(first_lane, pltpu.roll(near, 1, 0), near)

    def row_of(r):
        return pl.ds(r % rows, per, stride=rows)

    lead_wait(0)
    halo_start(wide2, 0, zsend, zrecv, 0)
    lead_start(4)
    for f, (src, dst) in enumerate(strips):
        halo_wait(dst, None, hsend.at[f], hrecv, f)
    span_rows = rows * 2 * group
    masks = [mask_strip[r // rows, row_of(r)].astype(jnp.float32) for r in range(span_rows)]
    for r in range(1, span_rows - 1):
        mask = masks[r]
        east, north = east_strip[r // rows, row_of(r)], north_strip[r // rows, row_of(r)]
        rate_n = mask * masks[r - 1] * (0.1 + jnp.maximum(north, 0.0))
        rate_s = mask * masks[r + 1] * (0.1 + jnp.maximum(-north, 0.0))
        rate_e = mask * east_of(mask) * (0.1 + jnp.maximum(east, 0.0))
        rate_w = mask * west_of(mask) * (0.1 + jnp.maximum(-east, 0.0))
        rates[r, 0] = 1.0 - rate_n - rate_s - rate_e - rate_w
        rates[r, 1] = rate_n
        rates[r, 2] = rate_s
        rates[r, 3] = rate_e
        rates[r, 4] = rate_w

    def advance(fields, shift):
        count = len(fields[0])
        for step in range(SUBSTEPS):
            margin = step + 1
            fresh = [[None] * count for _ in fields]
            for u, old in enumerate(fields):
                for r in range(margin, count - margin):
                    rate = rates.at[r + shift]
                    fresh[u][r] = (
                        rate[0] * old[r]
                        + rate[1] * old[r - 1]
                        + rate[2] * old[r + 1]
                        + rate[3] * east_of(old[r])
                        + rate[4] * west_of(old[r])
                    )
            fields = fresh
        return fields

    def transport(wide, done, c):
        fields = [
            [wide[r // rows, c * size + u, row_of(r)] for r in range(span_rows)]
            for u in range(size)
        ]
        for u, field in enumerate(advance(fields, 0)):
            for r in range(rows * group):
                done[r // rows, c * size + u, row_of(r)] = field[reach + r]

    def transport_both(c):
        base = jnp.where(low, 0, half)
        fields = [
            [wide1[base + r // rows, c * size + u, row_of(r)] for r in range(rows * 3 * half)]
            for u in range(size)
        ]
        for u, field in enumerate(advance(fields, base * rows)):
            for r in range(rows * half):
                done_b[r // rows, (c - alone) * size + u, row_of(r)] = field[reach + r]

    def out_start(done, into, c, ssem, rsem):
        spot = into.at[q, pl.ds(c * size, size)]
        for o in range(1, group):
            part = done.at[lax.rem(q + o, group), pl.ds(c * size, size)]
            remote(part, spot, ssem.at[0], rsem.at[c], peer(o)).start()
        pltpu.make_async_copy(done.at[q, pl.ds(c * size, size)], spot, rsem.at[c]).start()

    def out_wait(into, c, rsem):
        wait_all(into.at[pl.ds(0, group), pl.ds(c * size, size)], rsem.at[c])

    def both_start(done, base, lo, into, c, ssem, rsem):
        spot = into.at[core, pl.ds((c - alone) * size, size)]
        part = done.at[base + 1 - core, pl.ds(lo, size)]
        remote(part, spot, ssem.at[1], rsem.at[c], twin).start()
        pltpu.make_async_copy(done.at[base + core, pl.ds(lo, size)], spot, rsem.at[c]).start()

    def both_wait(into, c, rsem):
        wait_all(into.at[pl.ds(0, 2), pl.ds((c - alone) * size, size)], rsem.at[c])

    def both_sent(spot, ssem, rsem):
        sent_all(spot, ssem.at[1], rsem.at[0])

    def aged_start(c):
        @pl.when(c < alone)
        def _():
            out_start(done2, aged2, c, osend, orecv)

        @pl.when(c >= alone)
        def _():
            both_start(done2, q - core, c * size, aged_b, c, osend, orecv)

    def middle(c):
        def each(i, carry):
            a = item_shift(c, q) + i
            kind = cls[a]
            fading = decay[pl.ds(a, 1)]
            for s in range(group):
                wide1[half + s, i] = done2[s, i] * (fading * living[s, kind])
            return carry

        lax.fori_loop(c * size, c * size + size, each, 0)

    def halo_pair(c):
        solo = c < alone
        down, up = halo(wide1, c * size, z1send, z1recv, c)
        return (down, jnp.logical_or(solo, low)), (up, jnp.logical_or(solo, jnp.logical_not(low)))

    def halo_one(c):
        (down, lower), (up, upper) = halo_pair(c)

        @pl.when(jnp.logical_and(has_next, lower))
        def _():
            down.start()

        @pl.when(jnp.logical_and(has_prev, upper))
        def _():
            up.start()

    def halo_one_wait(c):
        (down, lower), (up, upper) = halo_pair(c)

        @pl.when(jnp.logical_and(has_prev, lower))
        def _():
            down.wait_recv()

        @pl.when(jnp.logical_and(has_next, upper))
        def _():
            up.wait_recv()

    def tally(c, shared, each):
        lo = (c - alone) * size if shared else c * size
        parts = range(group, group + 2) if shared else range(group)

        def step(i, runs):
            new = []
            for part, run in zip(parts, runs):
                new.append(run + each(part, i, starts[part] + i))
                prefix[part, i + 1] = new[-1]
            return tuple(new)

        lax.fori_loop(lo, lo + size, step, tuple(prefix[part, lo] for part in parts))

    def lost_two(part, i, a):
        value = aged2[part, i] if part < group else aged_b[part - group, i]
        return value * (decay[pl.ds(a, 1)] * kinds2[cls[a]]) * dens2[a]

    def keep_one(part, i, a, before):
        value = carried1[part, i] if part < group else carried_b[part - group, i]
        value = value + moved[cls[a]]
        stay = value * (decay[pl.ds(before, 1)] * kinds1[cls[before]])
        out[before] = stay
        return stay * dens1[before]

    def lost_one(part, i, a):
        return keep_one(part, i, a, jnp.maximum(a - 1, 0))

    def finish(month, shift):
        def store(kind, some):
            dead[kind] = some

        ratio = class_sums(store, shift)
        adem = []
        for k in range(forage):
            adem.append(-ratio[k] * feed_sq[month, k])
            sens[month, k] = ratio[k] * feed_sq[2 + month, k] * feed_sq[month, k]
        return adem

    def class_rows(month, adem, short, add):
        def each(kind, carry):
            many, lost = crowd[month, kind], dead[kind]
            for k in range(forage):
                row = jnp.sum(many * adem[k] - lost * short[k], axis=0, keepdims=True)
                if add:
                    row = row + by_class[k, pl.ds(kind, 1)]
                by_class[k, pl.ds(kind, 1)] = row
            return carry

        lax.fori_loop(0, classes, each, 0, unroll=2)

    def live(s, carry):
        shorts = [short_all[s, k] for k in range(forage)]
        fill(living.at[s], shorts, True)
        return carry

    def second(c, carry):
        halo_wait(wide2, c * size, zsend, zrecv, c)

        @pl.when(c >= chunks - halo_ahead)
        def _():
            halo_one(c - chunks + halo_ahead)

        transport(wide2, done2, c)

        @pl.when(c >= out_lag)
        def _():
            aged_start(c - out_lag)

        @pl.when(c == 0)
        def _():
            spread_wait(short_all, 0, ssend, srecv)
            lax.fori_loop(0, group, live, 0)

        middle(c)

        @pl.when(c + 3 < chunks)
        def _():
            lead_wait(c + 3)
            halo_start(wide2, (c + 3) * size, zsend, zrecv, c + 3)

        @pl.when(c + 3 + lead_ahead < chunks)
        def _():
            lead_start(c + 3 + lead_ahead)

        return carry

    spread_pass(short_all, 0, ssend, srecv)
    lead_wait(1)
    halo_start(wide2, size, zsend, zrecv, 1)
    lead_start(5)
    lead_wait(2)
    halo_start(wide2, 2 * size, zsend, zrecv, 2)
    lead_start(6)
    lax.fori_loop(0, chunks, second, 0)
    for c in range(chunks - out_lag, chunks):
        aged_start(c)

    odd = lax.rem(q, 2)
    side = 1 - 2 * odd
    steps = [(jnp.logical_or(low, has_next), half), (jnp.logical_or(~low, has_prev), -half)]
    onward = jnp.where(odd == 0, steps[0][0], steps[1][0])
    inward = jnp.where(odd == 0, steps[1][0], steps[0][0])

    def near_copy(d, i):
        return remote(
            wide_a.at[half], wide_a.at[half - d], asend.at[i], arecv.at[i], me + d
        )

    def near_start():
        for i, (there, d) in enumerate(steps):

            @pl.when(there)
            def _(i=i, d=d):
                near_copy(d, i).start()

        near_copy(side, 2).start()

    def near_from(slot, i):
        spot = wide_a.at[slot]
        remote(spot, spot, asend.at[i], arecv.at[i], twin).wait_recv()

    def near_pass():
        for i, (there, d) in enumerate(steps):

            @pl.when(steps[1 - i][0])
            def _(i=i, d=d):
                near_from(half - d, i)

        @pl.when(onward)
        def _():
            remote(
                wide_a.at[half + half * side], wide_a.at[half + side], asend.at[3], arecv.at[3],
                twin,
            ).start()

    def near_wait():
        near_from(half + side, 2)

        @pl.when(inward)
        def _():
            near_from(half - side, 3)

    def near_sent():
        for i, (there, d) in enumerate(steps):

            @pl.when(there)
            def _(i=i, d=d):
                near_copy(d, i).wait_send()

        near_copy(side, 2).wait_send()

        @pl.when(onward)
        def _():
            near_copy(side, 3).wait_send()

    def gather_two(c, carry):
        out_wait(aged2, c, orecv)
        tally(c, False, lost_two)
        return carry

    def gather_both(c, carry):
        both_wait(aged_b, c, orecv)
        tally(c, True, lost_two)
        return carry

    def leading(c, carry):
        halo_one_wait(c)

        @pl.when(c + halo_ahead < chunks)
        def _():
            halo_one(c + halo_ahead)

        transport(wide1, done1, c)
        out_start(done1, carried1, c, o1send, o1recv)

        @pl.when(c == alone // 2 - 1)
        def _():
            lax.fori_loop(0, alone, gather_two, 0)
            lax.fori_loop(alone, chunks, gather_both, 0)
            adem2 = finish(1, 0)
            for k in range(forage):
                wide_a[half, k] = adem2[k]
            near_start()
            class_rows(1, adem2, [short_all[q, k] for k in range(forage)], False)

        return carry

    lax.fori_loop(0, alone, leading, 0)

    def leading_both(c, carry):
        halo_one_wait(c)

        @pl.when(c + halo_ahead < chunks)
        def _():
            halo_one(c + halo_ahead)

        transport_both(c)
        both_start(done_b, 0, (c - alone) * size, carried_b, c, o1send, o1recv)
        return carry

    lax.fori_loop(alone, chunks, leading_both, 0)
    mine = pl.ds(0, group - 1)
    sent_all(wide2.at[mine], lsend.at[0], lrecv.at[0])
    sent_all(done2.at[mine, pl.ds(0, own)], osend.at[0], orecv.at[0])
    both_sent(done2.at[0, pl.ds(own, both)], osend, orecv)
    spread_sent(short_all, 0, ssend, srecv)
    halo_sent(wide2.at[pl.ds(0, half)], zsend, zrecv)
    for down_count, up_count, here in ((own + both, own, low), (own, own + both, ~low)):

        @pl.when(jnp.logical_and(here, has_next))
        def _(count=down_count):
            sent_all(wide1.at[pl.ds(0, half), pl.ds(0, count)], z1send.at[0], z1recv.at[0, 0])

        @pl.when(jnp.logical_and(here, has_prev))
        def _(count=up_count):
            sent_all(wide1.at[pl.ds(0, half), pl.ds(0, count)], z1send.at[1], z1recv.at[1, 0])

    for f, (src, dst) in enumerate(strips):
        spread_sent(dst, half, fsend.at[f], frecv.at[f])
        halo_sent(dst.at[pl.ds(0, half)], hsend.at[f], hrecv)
    near_pass()
    near_wait()

    reach_rows = rows * (2 * half + 1)
    fields = [
        [wide_a[r // rows, k, row_of(r)] for r in range(reach_rows)] for k in range(forage)
    ]
    for k, field in enumerate(advance(fields, rows * q)):
        for r in range(rows):
            strewn[k, row_of(r)] = field[reach + r]
    fill(moved, [strewn[k] for k in range(forage)])

    def ending(c, carry):
        out_wait(carried1, c, o1recv)
        tally(c, False, lost_one)
        return carry

    def ending_both(c, carry):
        both_wait(carried_b, c, o1recv)
        tally(c, True, lost_one)
        return carry

    lax.fori_loop(0, alone, ending, 0)
    lax.fori_loop(alone, chunks, ending_both, 0)
    gone = keep_one(group + 1, both - 1, cohorts - 1, cohorts - 1)
    prefix[group + 1, both + 1] = prefix[group + 1, both] + gone
    adem1 = finish(0, 1)
    class_rows(0, adem1, [short1[k] for k in range(forage)], True)

    ones = jnp.ones((8, LANES), jnp.float32)
    sums = []
    for k in range(forage):
        lanes_sum = lax.dot_general(
            ones, by_class[k], (((1,), (1,)), ((), ())), precision=lax.Precision.HIGHEST,
            preferred_element_type=jnp.float32,
        )
        sums.append(lanes_sum[0:1])
    totals[me] = jnp.concatenate(sums, axis=0)

    def total_start(t, carry):
        other = lax.rem(me + t, tiles)
        remote(totals.at[me], totals.at[me], nsend.at[0], nrecv.at[0], other).start()
        return carry

    lax.fori_loop(1, tiles, total_start, 0)
    fill(adding, adem1)

    def outgoing(a, carry):
        out[a] = out[a] + adding[cls[a]]
        return carry

    lax.fori_loop(0, cohorts, outgoing, 0, unroll=4)
    sent_all(done1.at[mine], o1send.at[0], o1recv.at[0])
    both_sent(done_b.at[0], o1send, o1recv)
    near_sent()
    others = totals.at[pl.ds(0, tiles - 1)]
    wait_all(others, nrecv.at[0])
    grad_out[...] = lax.fori_loop(
        1, tiles, lambda t, total: total + totals[t], totals[0]
    ) / (tiles * blocks * LANES)
    sent_all(others, nsend.at[0], nrecv.at[0])


def last_kernel(*refs):
    count = len(refs) // 2
    copies = [
        pltpu.make_async_copy(refs[i], refs[count + i], refs[2 * count].at[i])
        for i in range(count)
    ]
    for copy in copies:
        copy.start()
    for copy in copies:
        copy.wait()


def blocked(x):
    rows, columns = x.shape[-2:]
    head = x.shape[:-2]
    n = len(head)
    y = x.reshape(head + (rows, columns // LANES, LANES))
    y = jnp.swapaxes(y, n, n + 1)
    return y.reshape(head + (rows * columns // LANES, LANES))


def unblocked(x, rows):
    head = x.shape[:-2]
    n = len(head)
    y = x.reshape(head + (x.shape[-2] // rows, rows, LANES))
    y = jnp.swapaxes(y, n, n + 1)
    return y.reshape(head + (rows, -1))


def shards(
    final_adjoint,
    first_density,
    second_density,
    forage,
    preference,
    base_mortality,
    age_class,
    land_mask,
    east_velocity,
    north_velocity,
):
    classes, groups = preference.shape
    cohorts, rows, columns = final_adjoint.shape
    tiles = lax.axis_size("tile")
    group = 2 * SUBSTEPS // rows
    size = 5
    chunks = 10
    alone = (cohorts // size - 2 * chunks) // (group - 2)
    own, both = alone * size, (chunks - alone) * size
    blocks = rows * columns // LANES
    f32 = jnp.float32
    dma = pltpu.SemaphoreType.DMA
    vmem = pl.BlockSpec(memory_space=pltpu.VMEM)
    smem = pl.BlockSpec(memory_space=pltpu.SMEM)
    hbm = pl.BlockSpec(memory_space=pl.ANY)
    dims = (tiles, group, rows, cohorts, size, alone, chunks, groups, 4, 4, 3)
    cell = (blocks, LANES)

    def body(*refs):
        kernel(dims, *refs)

    def cells(*lead):
        return pltpu.VMEM(lead + cell, f32)

    results = pl.pallas_call(
        body,
        out_shape=(
            cells(cohorts),
            cells(2, groups),
            pltpu.VMEM((groups, classes), f32),
        ),
        in_specs=[hbm] * 10,
        out_specs=(vmem, vmem, vmem),
        scratch_shapes=[
            cells(2 * group, own + both),
            cells(2 * group, own + both),
            cells(group + 1, groups),
            cells(group, own + both),
            cells(group, own),
            cells(2, both),
            cells(group, own),
            cells(2, both),
            cells(group, own),
            cells(2, both),
            pltpu.VMEM((2 * group,) + cell, jnp.int32),
            cells(2 * group),
            cells(2 * group),
            pltpu.VMEM((2 * group * rows, 5, blocks // rows, LANES), f32),
            cells(group, groups),
            cells(groups),
            cells(groups),
            cells(4, groups),
            cells(cohorts),
            cells(cohorts),
            cells(2, groups),
            pltpu.VMEM((cohorts, LANES), f32),
            cells(classes),
            cells(classes),
            cells(classes),
            cells(classes),
            cells(group, classes),
            cells(2, classes),
            cells(classes),
            cells(group + 2, max(own, both) + 2),
            pltpu.VMEM((groups, classes, LANES), f32),
            pltpu.VMEM((tiles, groups, classes), f32),
            pltpu.SMEM((classes + 1,), jnp.int32),
            pltpu.SMEM((groups, classes), f32),
            pltpu.VMEM((1, cohorts), f32),
            pltpu.SMEM((cohorts,), jnp.int32),
        ]
        + [dma((1,)), dma((chunks,)), dma((2,)), dma((2, chunks)), dma((2,)), dma((chunks,))]
        + [dma((2,)), dma((2, chunks)), dma((2,)), dma((chunks,)), dma((3, 3)), dma((3, 3))]
        + [dma((3, 2)), dma((2, 3)), dma((3,)), dma((3,)), dma((4,)), dma((4,))]
        + [dma((1,)), dma((1,)), dma((9,))],
        compiler_params=pltpu.CompilerParams(
            collective_id=0, has_side_effects=True, vmem_limit_bytes=56 * 1024 * 1024
        ),
        name="adjoint",
    )(
        preference.T,
        base_mortality.reshape(1, -1),
        age_class,
        blocked(final_adjoint),
        blocked(first_density),
        blocked(second_density),
        blocked(forage),
        blocked(land_mask),
        blocked(east_velocity),
        blocked(north_velocity),
    )
    out, sens, grad = pl.pallas_call(
        last_kernel,
        out_shape=tuple(jax.ShapeDtypeStruct(x.shape, x.dtype) for x in results),
        in_specs=[vmem] * len(results),
        out_specs=(hbm,) * len(results),
        scratch_shapes=[dma((len(results),))],
        name="outgoing",
    )(*(pltpu.with_memory_space_constraint(x, pltpu.VMEM) for x in results))
    summed = grad.T
    return (unblocked(out, rows), unblocked(sens, rows), summed)


def solution(mesh):
    in_specs = (
        P("ens", "tile", None),
        P("ens", "tile", None),
        P("ens", "tile", None),
        P("ens", None, "tile", None),
        P("ens", None),
        P(),
        P(),
        P("tile", None),
        P("tile", None),
        P("tile", None),
    )
    out_specs = (P("ens", "tile", None), P("ens", None, "tile", None), P("ens", None))
    return jax.shard_map(shards, mesh=mesh, in_specs=in_specs, out_specs=out_specs, check_vma=False)
```

```python
import jax
import jax.numpy as jnp
from jax import lax
from jax.experimental import pallas as pl
from jax.experimental.pallas import tpu as pltpu
from jax.sharding import PartitionSpec as P

SUBSTEPS = 4
LANES = 128
MESH = pl.DeviceIdType.MESH


def kernel(
    dims,
    table_in,
    base_in,
    cls_in,
    lead,
    dens1_in,
    dens2_in,
    food_in,
    mask_in,
    east_in,
    north_in,
    out,
    sens,
    grad_out,
    wide2,
    wide1,
    wide_a,
    done2,
    done1,
    done_b,
    aged2,
    aged_b,
    carried1,
    carried_b,
    mask_strip,
    east_strip,
    north_strip,
    rates,
    short_all,
    short1,
    strewn,
    feed_sq,
    dens1,
    dens2,
    food,
    decay,
    kinds2,
    kinds1,
    moved,
    adding,
    living,
    crowd,
    dead,
    prefix,
    by_class,
    totals,
    bounds,
    table,
    base_row,
    cls,
    lsend,
    lrecv,
    zsend,
    zrecv,
    osend,
    orecv,
    z1send,
    z1recv,
    o1send,
    o1recv,
    fsend,
    frecv,
    hsend,
    hrecv,
    ssend,
    srecv,
    asend,
    arecv,
    nsend,
    nrecv,
    own_sem,
):
    tiles, group, rows, cohorts, size, alone, chunks, forage, lead_ahead, out_lag, halo_ahead = dims
    half = group // 2
    own = alone * size
    both = (chunks - alone) * size
    pooled = group * own
    blocks = food.shape[2]
    per = blocks // rows
    reach = half * rows
    classes = table.shape[1]
    me = lax.axis_index("tile")
    q = lax.rem(me, group)
    first = me - q
    has_prev = me >= group
    has_next = me < tiles - group

    def peer(o):
        return first + lax.rem(q + o, group)

    def source(o):
        return lax.rem(q + group - o, group)

    barrier = pltpu.get_barrier_semaphore()
    spans = tiles // group
    twin = me + 1 - 2 * lax.rem(q, 2)
    across = peer(half)
    low = q < half
    core = lax.rem(q, 2)
    beyond = [
        (has_next, me + group),
        (has_prev, me - group),
        (jnp.logical_and(jnp.logical_not(low), has_next), me + half),
        (jnp.logical_and(low, has_prev), me - half),
    ]
    if spans > 4:

        def greet(t, carry):
            other = lax.rem(me + t, tiles)
            pl.semaphore_signal(barrier, inc=1, device_id={"tile": other}, device_id_type=MESH)
            return carry

        lax.fori_loop(1, tiles, greet, 0)
    else:
        for o in range(1, group):
            pl.semaphore_signal(barrier, inc=1, device_id={"tile": peer(o)}, device_id_type=MESH)
        for there, other in beyond:

            @pl.when(there)
            def _(other=other):
                pl.semaphore_signal(
                    barrier, inc=1, device_id={"tile": other}, device_id_type=MESH
                )

    smalls = [
        pltpu.make_async_copy(src, dst, own_sem.at[6 + i])
        for i, (src, dst) in enumerate(((base_in, base_row), (cls_in, cls), (table_in, table)))
    ]
    for copy in smalls:
        copy.start()
    loads = [
        pltpu.make_async_copy(src, dst, own_sem.at[3 + i])
        for i, (src, dst) in enumerate(((dens2_in, dens2), (food_in, food), (dens1_in, dens1)))
    ]
    for copy in loads:
        copy.start()
    strips = ((mask_in, mask_strip), (east_in, east_strip), (north_in, north_strip))
    own_fields = [
        pltpu.make_async_copy(src, dst.at[half + q], own_sem.at[f])
        for f, (src, dst) in enumerate(strips)
    ]
    for copy in own_fields:
        copy.start()

    zero = jnp.zeros((blocks, LANES), jnp.float32)

    smalls[0].wait()
    fall = jnp.exp(-base_row[...])
    along = lax.broadcasted_iota(jnp.int32, (cohorts, cohorts), 1)
    down = lax.broadcasted_iota(jnp.int32, (cohorts, cohorts), 0)
    spread = jnp.where(along == down, fall, 0.0)
    decay[...] = jnp.broadcast_to(jnp.sum(spread, axis=1, keepdims=True), (cohorts, LANES))

    def bound(kind):
        spot = jnp.int32(0)
        width = 1
        while 2 * width <= cohorts:
            width = 2 * width
        while width >= 1:
            last = jnp.minimum(spot + width, cohorts) - 1
            ok = jnp.logical_and(spot + width <= cohorts, cls[last] < kind)
            spot = jnp.where(ok, spot + width, spot)
            width = width // 2
        return spot

    smalls[1].wait()
    smalls[2].wait()
    bounds[0] = jnp.int32(0)
    for kind in range(1, classes):
        bounds[kind] = bound(kind)
    bounds[classes] = jnp.int32(cohorts)

    if spans > 4:
        pl.semaphore_wait(barrier, tiles - 1)
    else:
        pl.semaphore_wait(barrier, group - 1 + sum(there.astype(jnp.int32) for there, _ in beyond))

    def remote(src, dst, ssem, rsem, target):
        return pltpu.make_async_remote_copy(
            src_ref=src, dst_ref=dst, send_sem=ssem, recv_sem=rsem,
            device_id={"tile": target}, device_id_type=MESH,
        )

    def spread_copy(buf, slot, ssem, rsem, i, target):
        return remote(buf.at[slot], buf.at[slot], ssem.at[i], rsem.at[i], target)

    def spread_start(buf, lift, ssem, rsem):
        spread_copy(buf, lift + q, ssem, rsem, 1, across).start()
        spread_copy(buf, lift + q, ssem, rsem, 0, twin).start()

    def spread_pass(buf, lift, ssem, rsem):
        slot = lift + across - first
        spread_copy(buf, slot, ssem, rsem, 1, across).wait_recv()
        spread_copy(buf, slot, ssem, rsem, 2, twin).start()

    def spread_wait(buf, lift, ssem, rsem):
        spread_copy(buf, lift + twin - first, ssem, rsem, 0, twin).wait_recv()
        spread_copy(buf, lift + lax.rem(twin - first + half, group), ssem, rsem, 2, twin).wait_recv()

    def spread_sent(buf, lift, ssem, rsem):
        for i in range(3):
            spread_copy(buf, lift + q, ssem, rsem, i, twin).wait_send()

    def halo(buf, lo, ssem, rsem, c):
        def part(begin):
            if lo is None:
                return buf.at[pl.ds(begin, half)]
            return buf.at[pl.ds(begin, half), pl.ds(lo, size)]

        down = remote(part(group), part(0), ssem.at[0], rsem.at[0, c], me + group)
        up = remote(part(half), part(group + half), ssem.at[1], rsem.at[1, c], me - group)
        return down, up

    def halo_start(*args):
        down, up = halo(*args)

        @pl.when(has_next)
        def _():
            down.start()

        @pl.when(has_prev)
        def _():
            up.start()

    def halo_wait(*args):
        down, up = halo(*args)

        @pl.when(has_prev)
        def _():
            down.wait_recv()

        @pl.when(has_next)
        def _():
            up.wait_recv()

    def halo_sent(spot, ssem, rsem):
        @pl.when(has_next)
        def _():
            sent_all(spot, ssem.at[0], rsem.at[0, 0])

        @pl.when(has_prev)
        def _():
            sent_all(spot, ssem.at[1], rsem.at[1, 0])

    for f, (src, dst) in enumerate(strips):
        own_fields[f].wait()
        spread_start(dst, half, fsend.at[f], frecv.at[f])

    def lead_pieces(c):
        return ((c * size, size - 1), (c * size + size - 1, 1))

    def item_shift(c, who):
        shared = pooled + both * lax.rem(who, 2) - own
        return jnp.where(c < alone, own * who, shared)

    def lead_copy(o, c, lo, count):
        begin = jnp.minimum(item_shift(c, lax.rem(q + o, group)) + 1 + lo, cohorts - count)
        return remote(
            lead.at[pl.ds(begin, count)], wide2.at[half + q, pl.ds(lo, count)],
            lsend.at[0], lrecv.at[c], peer(o),
        )

    def lead_own(c, lo, count):
        begin = jnp.minimum(item_shift(c, q) + 1 + lo, cohorts - count)
        return pltpu.make_async_copy(
            lead.at[pl.ds(begin, count)], wide2.at[half + q, pl.ds(lo, count)], lrecv.at[c]
        )

    def lead_start(c):
        for piece in lead_pieces(c):
            for o in range(1, group):
                lead_copy(o, c, *piece).start()
            lead_own(c, *piece).start()

    def wait_all(spot, sem):
        pltpu.make_async_copy(spot, spot, sem).wait()

    def sent_all(spot, ssem, rsem):
        remote(spot, spot, ssem, rsem, peer(1)).wait_send()

    def lead_wait(c):
        wait_all(wide2.at[pl.ds(half, group), pl.ds(c * size, size)], lrecv.at[c])

    lead_start(0)
    lead_start(1)

    strips_all = (mask_strip, east_strip, north_strip)
    wides = (wide2, wide1)

    @pl.when(jnp.logical_not(has_prev))
    def _():
        for strip in strips_all:
            strip[0:half] = jnp.zeros((half,) + strip.shape[1:], strip.dtype)
        for wide in wides:
            wide[0:half] = jnp.zeros((half,) + wide.shape[1:], jnp.float32)

    @pl.when(jnp.logical_not(has_next))
    def _():
        for strip in strips_all:
            strip[group + half :] = jnp.zeros((half,) + strip.shape[1:], strip.dtype)
        for wide in wides:
            wide[group + half :] = jnp.zeros((half,) + wide.shape[1:], jnp.float32)

    for d in (d for d in range(-half, half + 1) if d != 0):

        @pl.when(jnp.logical_not(jnp.logical_and(me + d >= 0, me + d < tiles)))
        def _(d=d):
            wide_a[half + d] = jnp.zeros(wide_a.shape[1:], jnp.float32)

    for part in range(group + 2):
        prefix[part, 0] = zero
    starts = [part * own for part in range(group)] + [pooled, pooled + both]
    lengths = [own] * group + [both] * 2

    def upto(spot):
        total = zero
        for part in range(group + 2):
            top = lengths[part] + (part == group + 1)
            total = total + prefix[part, jnp.clip(spot - starts[part], 0, top)]
        return total

    def weighted(kind, values):
        total = table[0, kind] * values[0]
        for k in range(1, forage):
            total = total + table[k, kind] * values[k]
        return total

    def class_sums(store, shift):
        def step(kind, carry):
            before, sums = carry
            here = upto(bounds[kind + 1] + shift)
            some = here - before
            store(kind, some)
            return here, tuple(sums[k] + table[k, kind] * some for k in range(forage))

        return lax.fori_loop(0, classes, step, (upto(shift), (zero,) * forage), unroll=4)[1]

    def fill(into, values, decaying=False):
        def each(kind, carry):
            total = weighted(kind, values)
            into[kind] = jnp.exp(-total) if decaying else total
            return carry

        lax.fori_loop(0, classes, each, 0, unroll=2)

    def prepare(month, dens, by_kind, short_store):
        def adder(parts):
            def add(i, runs):
                new = []
                for part, run in zip(parts, runs):
                    new.append(run + dens[starts[part] + i])
                    prefix[part, i + 1] = new[-1]
                return tuple(new)

            return add

        for parts in (range(group), range(group, group + 2)):
            lax.fori_loop(
                0, lengths[parts[0]], adder(parts), (zero,) * len(parts), unroll=2
            )

        def store(kind, some):
            crowd[month, kind] = some

        hungry = class_sums(store, 0)
        shorts = []
        for k in range(forage):
            feed = food[month, k]
            total = feed + hungry[k]
            shorts.append(hungry[k] / total)
            short_store(k, shorts[k])
            feed_sq[month, k] = feed / (total * total)
            feed_sq[2 + month, k] = hungry[k]
        return shorts

    def store_two(k, value):
        short_all[q, k] = value

    def store_one(k, value):
        short1[k] = value

    loads[0].wait()
    loads[1].wait()
    shorts2 = prepare(1, dens2, kinds2, store_two)
    spread_start(short_all, 0, ssend, srecv)
    lead_start(2)
    fill(kinds2, shorts2, True)

    for f, (src, dst) in enumerate(strips):
        spread_pass(dst, half, fsend.at[f], frecv.at[f])
    loads[2].wait()
    shorts1 = prepare(0, dens1, kinds1, store_one)
    fill(kinds1, shorts1, True)
    lead_start(3)
    for f, (src, dst) in enumerate(strips):
        spread_wait(dst, half, fsend.at[f], frecv.at[f])
        halo_start(dst, None, hsend.at[f], hrecv, f)

    lane = lax.broadcasted_iota(jnp.int32, (per, LANES), 1)
    last_lane = lane == LANES - 1
    first_lane = lane == 0

    def east_of(x):
        near = pltpu.roll(x, LANES - 1, 1)
        return jnp.where(last_lane, pltpu.roll(near, per - 1, 0), near)

    def west_of(x):
        near = pltpu.roll(x, 1, 1)
        return jnp.where(first_lane, pltpu.roll(near, 1, 0), near)

    def row_of(r):
        return pl.ds(r % rows, per, stride=rows)

    lead_wait(0)
    halo_start(wide2, 0, zsend, zrecv, 0)
    lead_start(4)
    lead_wait(1)
    halo_start(wide2, size, zsend, zrecv, 1)
    lead_start(5)
    for f, (src, dst) in enumerate(strips):
        halo_wait(dst, None, hsend.at[f], hrecv, f)
    span_rows = rows * 2 * group
    masks = [mask_strip[r // rows, row_of(r)].astype(jnp.float32) for r in range(span_rows)]
    for r in range(1, span_rows - 1):
        mask = masks[r]
        east, north = east_strip[r // rows, row_of(r)], north_strip[r // rows, row_of(r)]
        rate_n = mask * masks[r - 1] * (0.1 + jnp.maximum(north, 0.0))
        rate_s = mask * masks[r + 1] * (0.1 + jnp.maximum(-north, 0.0))
        rate_e = mask * east_of(mask) * (0.1 + jnp.maximum(east, 0.0))
        rate_w = mask * west_of(mask) * (0.1 + jnp.maximum(-east, 0.0))
        rates[r, 0] = 1.0 - rate_n - rate_s - rate_e - rate_w
        rates[r, 1] = rate_n
        rates[r, 2] = rate_s
        rates[r, 3] = rate_e
        rates[r, 4] = rate_w

    def advance(fields, shift):
        count = len(fields[0])
        for step in range(SUBSTEPS):
            margin = step + 1
            fresh = [[None] * count for _ in fields]
            for u, old in enumerate(fields):
                for r in range(margin, count - margin):
                    rate = rates.at[r + shift]
                    fresh[u][r] = (
                        rate[0] * old[r]
                        + rate[1] * old[r - 1]
                        + rate[2] * old[r + 1]
                        + rate[3] * east_of(old[r])
                        + rate[4] * west_of(old[r])
                    )
            fields = fresh
        return fields

    def transport(wide, done, c):
        fields = [
            [wide[r // rows, c * size + u, row_of(r)] for r in range(span_rows)]
            for u in range(size)
        ]
        for u, field in enumerate(advance(fields, 0)):
            for r in range(rows * group):
                done[r // rows, c * size + u, row_of(r)] = field[reach + r]

    def transport_both(c):
        base = jnp.where(low, 0, half)
        fields = [
            [wide1[base + r // rows, c * size + u, row_of(r)] for r in range(rows * 3 * half)]
            for u in range(size)
        ]
        for u, field in enumerate(advance(fields, base * rows)):
            for r in range(rows * half):
                done_b[r // rows, (c - alone) * size + u, row_of(r)] = field[reach + r]

    def out_start(done, into, c, ssem, rsem):
        spot = into.at[q, pl.ds(c * size, size)]
        for o in range(1, group):
            part = done.at[lax.rem(q + o, group), pl.ds(c * size, size)]
            remote(part, spot, ssem.at[0], rsem.at[c], peer(o)).start()
        pltpu.make_async_copy(done.at[q, pl.ds(c * size, size)], spot, rsem.at[c]).start()

    def out_wait(into, c, rsem):
        wait_all(into.at[pl.ds(0, group), pl.ds(c * size, size)], rsem.at[c])

    def both_start(done, base, lo, into, c, ssem, rsem):
        spot = into.at[core, pl.ds((c - alone) * size, size)]
        part = done.at[base + 1 - core, pl.ds(lo, size)]
        remote(part, spot, ssem.at[1], rsem.at[c], twin).start()
        pltpu.make_async_copy(done.at[base + core, pl.ds(lo, size)], spot, rsem.at[c]).start()

    def both_wait(into, c, rsem):
        wait_all(into.at[pl.ds(0, 2), pl.ds((c - alone) * size, size)], rsem.at[c])

    def both_sent(spot, ssem, rsem):
        sent_all(spot, ssem.at[1], rsem.at[0])

    def aged_start(c):
        @pl.when(c < alone)
        def _():
            out_start(done2, aged2, c, osend, orecv)

        @pl.when(c >= alone)
        def _():
            both_start(done2, q - core, c * size, aged_b, c, osend, orecv)

    def middle(c):
        def each(i, carry):
            a = item_shift(c, q) + i
            kind = cls[a]
            fading = decay[pl.ds(a, 1)]
            for s in range(group):
                wide1[half + s, i] = done2[s, i] * (fading * living[s, kind])
            return carry

        lax.fori_loop(c * size, c * size + size, each, 0)

    def halo_pair(c):
        solo = c < alone
        down, up = halo(wide1, c * size, z1send, z1recv, c)
        return (down, jnp.logical_or(solo, low)), (up, jnp.logical_or(solo, jnp.logical_not(low)))

    def halo_one(c):
        (down, lower), (up, upper) = halo_pair(c)

        @pl.when(jnp.logical_and(has_next, lower))
        def _():
            down.start()

        @pl.when(jnp.logical_and(has_prev, upper))
        def _():
            up.start()

    def halo_one_wait(c):
        (down, lower), (up, upper) = halo_pair(c)

        @pl.when(jnp.logical_and(has_prev, lower))
        def _():
            down.wait_recv()

        @pl.when(jnp.logical_and(has_next, upper))
        def _():
            up.wait_recv()

    def tally(c, shared, each):
        lo = (c - alone) * size if shared else c * size
        parts = range(group, group + 2) if shared else range(group)

        def step(i, runs):
            new = []
            for part, run in zip(parts, runs):
                new.append(run + each(part, i, starts[part] + i))
                prefix[part, i + 1] = new[-1]
            return tuple(new)

        lax.fori_loop(lo, lo + size, step, tuple(prefix[part, lo] for part in parts))

    def lost_two(part, i, a):
        value = aged2[part, i] if part < group else aged_b[part - group, i]
        return value * (decay[pl.ds(a, 1)] * kinds2[cls[a]]) * dens2[a]

    def keep_one(part, i, a, before):
        value = carried1[part, i] if part < group else carried_b[part - group, i]
        value = value + moved[cls[a]]
        stay = value * (decay[pl.ds(before, 1)] * kinds1[cls[before]])
        out[before] = stay
        return stay * dens1[before]

    def lost_one(part, i, a):
        return keep_one(part, i, a, jnp.maximum(a - 1, 0))

    def finish(month, shift):
        def store(kind, some):
            dead[kind] = some

        ratio = class_sums(store, shift)
        adem = []
        for k in range(forage):
            adem.append(-ratio[k] * feed_sq[month, k])
            sens[month, k] = ratio[k] * feed_sq[2 + month, k] * feed_sq[month, k]
        return adem

    def class_rows(month, adem, short, add):
        def each(kind, carry):
            many, lost = crowd[month, kind], dead[kind]
            for k in range(forage):
                row = jnp.sum(many * adem[k] - lost * short[k], axis=0, keepdims=True)
                if add:
                    row = row + by_class[k, pl.ds(kind, 1)]
                by_class[k, pl.ds(kind, 1)] = row
            return carry

        lax.fori_loop(0, classes, each, 0, unroll=2)

    def live(s, carry):
        shorts = [short_all[s, k] for k in range(forage)]
        fill(living.at[s], shorts, True)
        return carry

    def second(c, carry):
        halo_wait(wide2, c * size, zsend, zrecv, c)

        @pl.when(c >= chunks - halo_ahead)
        def _():
            halo_one(c - chunks + halo_ahead)

        transport(wide2, done2, c)

        @pl.when(c >= out_lag)
        def _():
            aged_start(c - out_lag)

        @pl.when(c == 0)
        def _():
            spread_wait(short_all, 0, ssend, srecv)
            lax.fori_loop(0, group, live, 0)

        middle(c)

        @pl.when(c + 3 < chunks)
        def _():
            lead_wait(c + 3)
            halo_start(wide2, (c + 3) * size, zsend, zrecv, c + 3)

        @pl.when(c + 3 + lead_ahead < chunks)
        def _():
            lead_start(c + 3 + lead_ahead)

        return carry

    spread_pass(short_all, 0, ssend, srecv)
    lead_wait(2)
    halo_start(wide2, 2 * size, zsend, zrecv, 2)
    lead_start(6)
    lax.fori_loop(0, chunks, second, 0)
    for c in range(chunks - out_lag, chunks):
        aged_start(c)

    odd = lax.rem(q, 2)
    side = 1 - 2 * odd
    steps = [(jnp.logical_or(low, has_next), half), (jnp.logical_or(~low, has_prev), -half)]
    onward = jnp.where(odd == 0, steps[0][0], steps[1][0])
    inward = jnp.where(odd == 0, steps[1][0], steps[0][0])

    def near_copy(d, i):
        return remote(
            wide_a.at[half], wide_a.at[half - d], asend.at[i], arecv.at[i], me + d
        )

    def near_start():
        for i, (there, d) in enumerate(steps):

            @pl.when(there)
            def _(i=i, d=d):
                near_copy(d, i).start()

        near_copy(side, 2).start()

    def near_from(slot, i):
        spot = wide_a.at[slot]
        remote(spot, spot, asend.at[i], arecv.at[i], twin).wait_recv()

    def near_pass():
        for i, (there, d) in enumerate(steps):

            @pl.when(steps[1 - i][0])
            def _(i=i, d=d):
                near_from(half - d, i)

        @pl.when(onward)
        def _():
            remote(
                wide_a.at[half + half * side], wide_a.at[half + side], asend.at[3], arecv.at[3],
                twin,
            ).start()

    def near_wait():
        near_from(half + side, 2)

        @pl.when(inward)
        def _():
            near_from(half - side, 3)

    def near_sent():
        for i, (there, d) in enumerate(steps):

            @pl.when(there)
            def _(i=i, d=d):
                near_copy(d, i).wait_send()

        near_copy(side, 2).wait_send()

        @pl.when(onward)
        def _():
            near_copy(side, 3).wait_send()

    def gather_two(c, carry):
        out_wait(aged2, c, orecv)
        tally(c, False, lost_two)
        return carry

    def gather_both(c, carry):
        both_wait(aged_b, c, orecv)
        tally(c, True, lost_two)
        return carry

    def leading(c, carry):
        halo_one_wait(c)

        @pl.when(c + halo_ahead < chunks)
        def _():
            halo_one(c + halo_ahead)

        transport(wide1, done1, c)
        out_start(done1, carried1, c, o1send, o1recv)

        @pl.when(c == alone // 2 - 1)
        def _():
            lax.fori_loop(0, alone, gather_two, 0)
            lax.fori_loop(alone, chunks, gather_both, 0)
            adem2 = finish(1, 0)
            for k in range(forage):
                wide_a[half, k] = adem2[k]
            near_start()
            class_rows(1, adem2, [short_all[q, k] for k in range(forage)], False)

        return carry

    lax.fori_loop(0, alone, leading, 0)

    def ending(c, carry):
        out_wait(carried1, c, o1recv)
        tally(c, False, lost_one)
        return carry

    def leading_both(c, carry):
        @pl.when(c == chunks - 3)
        def _():
            near_pass()

        @pl.when(c == chunks - 1)
        def _():
            lax.fori_loop(0, alone - 2, ending, 0)

        @pl.when(c == chunks - 2)
        def _():
            near_wait()

            reach_rows = rows * (2 * half + 1)
            fields = [
                [wide_a[r // rows, k, row_of(r)] for r in range(reach_rows)] for k in range(forage)
            ]
            for k, field in enumerate(advance(fields, rows * q)):
                for r in range(rows):
                    strewn[k, row_of(r)] = field[reach + r]
            fill(moved, [strewn[k] for k in range(forage)])

        halo_one_wait(c)

        @pl.when(c + halo_ahead < chunks)
        def _():
            halo_one(c + halo_ahead)

        transport_both(c)
        both_start(done_b, 0, (c - alone) * size, carried_b, c, o1send, o1recv)
        return carry

    lax.fori_loop(alone, chunks, leading_both, 0)
    def ending_both(c, carry):
        both_wait(carried_b, c, o1recv)
        tally(c, True, lost_one)
        return carry

    lax.fori_loop(alone - 2, alone, ending, 0)
    lax.fori_loop(alone, chunks, ending_both, 0)
    gone = keep_one(group + 1, both - 1, cohorts - 1, cohorts - 1)
    prefix[group + 1, both + 1] = prefix[group + 1, both] + gone
    adem1 = finish(0, 1)
    class_rows(0, adem1, [short1[k] for k in range(forage)], True)

    ones = jnp.ones((8, LANES), jnp.float32)
    sums = []
    for k in range(forage):
        lanes_sum = lax.dot_general(
            ones, by_class[k], (((1,), (1,)), ((), ())), precision=lax.Precision.HIGHEST,
            preferred_element_type=jnp.float32,
        )
        sums.append(lanes_sum[0:1])
    totals[me] = jnp.concatenate(sums, axis=0)

    def total_start(t, carry):
        other = lax.rem(me + t, tiles)
        remote(totals.at[me], totals.at[me], nsend.at[0], nrecv.at[0], other).start()
        return carry

    lax.fori_loop(1, tiles, total_start, 0)
    fill(adding, adem1)

    def outgoing(a, carry):
        out[a] = out[a] + adding[cls[a]]
        return carry

    lax.fori_loop(0, cohorts, outgoing, 0, unroll=4)
    mine = pl.ds(0, group - 1)
    sent_all(wide2.at[mine], lsend.at[0], lrecv.at[0])
    sent_all(done2.at[mine, pl.ds(0, own)], osend.at[0], orecv.at[0])
    both_sent(done2.at[0, pl.ds(own, both)], osend, orecv)
    spread_sent(short_all, 0, ssend, srecv)
    halo_sent(wide2.at[pl.ds(0, half)], zsend, zrecv)
    for down_count, up_count, here in ((own + both, own, low), (own, own + both, ~low)):

        @pl.when(jnp.logical_and(here, has_next))
        def _(count=down_count):
            sent_all(wide1.at[pl.ds(0, half), pl.ds(0, count)], z1send.at[0], z1recv.at[0, 0])

        @pl.when(jnp.logical_and(here, has_prev))
        def _(count=up_count):
            sent_all(wide1.at[pl.ds(0, half), pl.ds(0, count)], z1send.at[1], z1recv.at[1, 0])

    for f, (src, dst) in enumerate(strips):
        spread_sent(dst, half, fsend.at[f], frecv.at[f])
        halo_sent(dst.at[pl.ds(0, half)], hsend.at[f], hrecv)
    sent_all(done1.at[mine], o1send.at[0], o1recv.at[0])
    both_sent(done_b.at[0], o1send, o1recv)
    near_sent()
    others = totals.at[pl.ds(0, tiles - 1)]
    wait_all(others, nrecv.at[0])
    grad_out[...] = lax.fori_loop(
        1, tiles, lambda t, total: total + totals[t], totals[0]
    ) / (tiles * blocks * LANES)
    sent_all(others, nsend.at[0], nrecv.at[0])


def last_kernel(*refs):
    count = len(refs) // 2
    copies = [
        pltpu.make_async_copy(refs[i], refs[count + i], refs[2 * count].at[i])
        for i in range(count)
    ]
    for copy in copies:
        copy.start()
    for copy in copies:
        copy.wait()


def blocked(x):
    rows, columns = x.shape[-2:]
    head = x.shape[:-2]
    n = len(head)
    y = x.reshape(head + (rows, columns // LANES, LANES))
    y = jnp.swapaxes(y, n, n + 1)
    return y.reshape(head + (rows * columns // LANES, LANES))


def unblocked(x, rows):
    head = x.shape[:-2]
    n = len(head)
    y = x.reshape(head + (x.shape[-2] // rows, rows, LANES))
    y = jnp.swapaxes(y, n, n + 1)
    return y.reshape(head + (rows, -1))


def shards(
    final_adjoint,
    first_density,
    second_density,
    forage,
    preference,
    base_mortality,
    age_class,
    land_mask,
    east_velocity,
    north_velocity,
):
    classes, groups = preference.shape
    cohorts, rows, columns = final_adjoint.shape
    tiles = lax.axis_size("tile")
    group = 2 * SUBSTEPS // rows
    size = 5
    chunks = 10
    alone = (cohorts // size - 2 * chunks) // (group - 2)
    own, both = alone * size, (chunks - alone) * size
    blocks = rows * columns // LANES
    f32 = jnp.float32
    dma = pltpu.SemaphoreType.DMA
    vmem = pl.BlockSpec(memory_space=pltpu.VMEM)
    smem = pl.BlockSpec(memory_space=pltpu.SMEM)
    hbm = pl.BlockSpec(memory_space=pl.ANY)
    dims = (tiles, group, rows, cohorts, size, alone, chunks, groups, 4, 4, 3)
    cell = (blocks, LANES)

    def body(*refs):
        kernel(dims, *refs)

    def cells(*lead):
        return pltpu.VMEM(lead + cell, f32)

    results = pl.pallas_call(
        body,
        out_shape=(
            cells(cohorts),
            cells(2, groups),
            pltpu.VMEM((groups, classes), f32),
        ),
        in_specs=[hbm] * 10,
        out_specs=(vmem, vmem, vmem),
        scratch_shapes=[
            cells(2 * group, own + both),
            cells(2 * group, own + both),
            cells(group + 1, groups),
            cells(group, own + both),
            cells(group, own),
            cells(2, both),
            cells(group, own),
            cells(2, both),
            cells(group, own),
            cells(2, both),
            pltpu.VMEM((2 * group,) + cell, jnp.int32),
            cells(2 * group),
            cells(2 * group),
            pltpu.VMEM((2 * group * rows, 5, blocks // rows, LANES), f32),
            cells(group, groups),
            cells(groups),
            cells(groups),
            cells(4, groups),
            cells(cohorts),
            cells(cohorts),
            cells(2, groups),
            pltpu.VMEM((cohorts, LANES), f32),
            cells(classes),
            cells(classes),
            cells(classes),
            cells(classes),
            cells(group, classes),
            cells(2, classes),
            cells(classes),
            cells(group + 2, max(own, both) + 2),
            pltpu.VMEM((groups, classes, LANES), f32),
            pltpu.VMEM((tiles, groups, classes), f32),
            pltpu.SMEM((classes + 1,), jnp.int32),
            pltpu.SMEM((groups, classes), f32),
            pltpu.VMEM((1, cohorts), f32),
            pltpu.SMEM((cohorts,), jnp.int32),
        ]
        + [dma((1,)), dma((chunks,)), dma((2,)), dma((2, chunks)), dma((2,)), dma((chunks,))]
        + [dma((2,)), dma((2, chunks)), dma((2,)), dma((chunks,)), dma((3, 3)), dma((3, 3))]
        + [dma((3, 2)), dma((2, 3)), dma((3,)), dma((3,)), dma((4,)), dma((4,))]
        + [dma((1,)), dma((1,)), dma((9,))],
        compiler_params=pltpu.CompilerParams(
            collective_id=0, has_side_effects=True, vmem_limit_bytes=56 * 1024 * 1024
        ),
        name="adjoint",
    )(
        preference.T,
        base_mortality.reshape(1, -1),
        age_class,
        blocked(final_adjoint),
        blocked(first_density),
        blocked(second_density),
        blocked(forage),
        blocked(land_mask),
        blocked(east_velocity),
        blocked(north_velocity),
    )
    out, sens, grad = pl.pallas_call(
        last_kernel,
        out_shape=tuple(jax.ShapeDtypeStruct(x.shape, x.dtype) for x in results),
        in_specs=[vmem] * len(results),
        out_specs=(hbm,) * len(results),
        scratch_shapes=[dma((len(results),))],
        name="outgoing",
    )(*(pltpu.with_memory_space_constraint(x, pltpu.VMEM) for x in results))
    summed = grad.T
    return (unblocked(out, rows), unblocked(sens, rows), summed)


def solution(mesh):
    in_specs = (
        P("ens", "tile", None),
        P("ens", "tile", None),
        P("ens", "tile", None),
        P("ens", None, "tile", None),
        P("ens", None),
        P(),
        P(),
        P("tile", None),
        P("tile", None),
        P("tile", None),
    )
    out_specs = (P("ens", "tile", None), P("ens", None, "tile", None), P("ens", None))
    return jax.shard_map(shards, mesh=mesh, in_specs=in_specs, out_specs=out_specs, check_vma=False)
```

```python
import jax
import jax.numpy as jnp
from jax import lax
from jax.experimental import pallas as pl
from jax.experimental.pallas import tpu as pltpu
from jax.sharding import PartitionSpec as P

SUBSTEPS = 4
LANES = 128
MESH = pl.DeviceIdType.MESH


def kernel(
    dims,
    table_in,
    base_in,
    cls_in,
    lead,
    dens1_in,
    dens2_in,
    food_in,
    mask_in,
    east_in,
    north_in,
    out,
    sens,
    grad_out,
    wide2,
    wide1,
    wide_a,
    done2,
    done1,
    done_b,
    aged2,
    aged_b,
    carried1,
    carried_b,
    mask_strip,
    east_strip,
    north_strip,
    rates,
    short_all,
    short1,
    strewn,
    feed_sq,
    dens1,
    dens2,
    food,
    decay,
    kinds2,
    kinds1,
    moved,
    adding,
    living,
    crowd,
    dead,
    prefix,
    by_class,
    totals,
    bounds,
    table,
    base_row,
    cls,
    lsend,
    lrecv,
    zsend,
    zrecv,
    osend,
    orecv,
    z1send,
    z1recv,
    o1send,
    o1recv,
    fsend,
    frecv,
    hsend,
    hrecv,
    ssend,
    srecv,
    asend,
    arecv,
    nsend,
    nrecv,
    own_sem,
):
    tiles, group, rows, cohorts, size, alone, chunks, forage, lead_ahead, out_lag, halo_ahead = dims
    half = group // 2
    own = alone * size
    both = (chunks - alone) * size
    pooled = group * own
    blocks = food.shape[2]
    per = blocks // rows
    reach = half * rows
    classes = table.shape[1]
    me = lax.axis_index("tile")
    q = lax.rem(me, group)
    first = me - q
    has_prev = me >= group
    has_next = me < tiles - group

    def peer(o):
        return first + lax.rem(q + o, group)

    def source(o):
        return lax.rem(q + group - o, group)

    barrier = pltpu.get_barrier_semaphore()
    spans = tiles // group
    twin = me + 1 - 2 * lax.rem(q, 2)
    across = peer(half)
    low = q < half
    core = lax.rem(q, 2)
    beyond = [
        (has_next, me + group),
        (has_prev, me - group),
        (jnp.logical_and(jnp.logical_not(low), has_next), me + half),
        (jnp.logical_and(low, has_prev), me - half),
    ]
    if spans > 4:

        def greet(t, carry):
            other = lax.rem(me + t, tiles)
            pl.semaphore_signal(barrier, inc=1, device_id={"tile": other}, device_id_type=MESH)
            return carry

        lax.fori_loop(1, tiles, greet, 0)
    else:
        for o in range(1, group):
            pl.semaphore_signal(barrier, inc=1, device_id={"tile": peer(o)}, device_id_type=MESH)
        for there, other in beyond:

            @pl.when(there)
            def _(other=other):
                pl.semaphore_signal(
                    barrier, inc=1, device_id={"tile": other}, device_id_type=MESH
                )

    smalls = [
        pltpu.make_async_copy(src, dst, own_sem.at[6 + i])
        for i, (src, dst) in enumerate(((base_in, base_row), (cls_in, cls), (table_in, table)))
    ]
    for copy in smalls:
        copy.start()
    loads = [
        pltpu.make_async_copy(src, dst, own_sem.at[3 + i])
        for i, (src, dst) in enumerate(((dens2_in, dens2), (food_in, food), (dens1_in, dens1)))
    ]
    for copy in loads:
        copy.start()
    strips = ((mask_in, mask_strip), (east_in, east_strip), (north_in, north_strip))
    own_fields = [
        pltpu.make_async_copy(src, dst.at[half + q], own_sem.at[f])
        for f, (src, dst) in enumerate(strips)
    ]
    for copy in own_fields:
        copy.start()

    zero = jnp.zeros((blocks, LANES), jnp.float32)

    smalls[0].wait()
    fall = jnp.exp(-base_row[...])
    along = lax.broadcasted_iota(jnp.int32, (cohorts, cohorts), 1)
    down = lax.broadcasted_iota(jnp.int32, (cohorts, cohorts), 0)
    spread = jnp.where(along == down, fall, 0.0)
    decay[...] = jnp.broadcast_to(jnp.sum(spread, axis=1, keepdims=True), (cohorts, LANES))

    def bound(kind):
        spot = jnp.int32(0)
        width = 1
        while 2 * width <= cohorts:
            width = 2 * width
        while width >= 1:
            last = jnp.minimum(spot + width, cohorts) - 1
            ok = jnp.logical_and(spot + width <= cohorts, cls[last] < kind)
            spot = jnp.where(ok, spot + width, spot)
            width = width // 2
        return spot

    smalls[1].wait()
    smalls[2].wait()
    bounds[0] = jnp.int32(0)
    for kind in range(1, classes):
        bounds[kind] = bound(kind)
    bounds[classes] = jnp.int32(cohorts)

    if spans > 4:
        pl.semaphore_wait(barrier, tiles - 1)
    else:
        pl.semaphore_wait(barrier, group - 1 + sum(there.astype(jnp.int32) for there, _ in beyond))

    def remote(src, dst, ssem, rsem, target):
        return pltpu.make_async_remote_copy(
            src_ref=src, dst_ref=dst, send_sem=ssem, recv_sem=rsem,
            device_id={"tile": target}, device_id_type=MESH,
        )

    def spread_copy(buf, slot, ssem, rsem, i, target):
        return remote(buf.at[slot], buf.at[slot], ssem.at[i], rsem.at[i], target)

    def spread_start(buf, lift, ssem, rsem):
        spread_copy(buf, lift + q, ssem, rsem, 1, across).start()
        spread_copy(buf, lift + q, ssem, rsem, 0, twin).start()

    def spread_onward(buf, lift, ssem, rsem):
        spread_copy(buf, lift + across - first, ssem, rsem, 2, twin).start()

    def spread_pass(buf, lift, ssem, rsem):
        spread_copy(buf, lift + across - first, ssem, rsem, 1, across).wait_recv()
        spread_onward(buf, lift, ssem, rsem)

    def spread_wait(buf, lift, ssem, rsem):
        spread_copy(buf, lift + twin - first, ssem, rsem, 0, twin).wait_recv()
        spread_copy(buf, lift + lax.rem(twin - first + half, group), ssem, rsem, 2, twin).wait_recv()

    def spread_sent(buf, lift, ssem, rsem):
        for i in range(3):
            spread_copy(buf, lift + q, ssem, rsem, i, twin).wait_send()

    def halo(buf, lo, ssem, rsem, c):
        def part(begin):
            if lo is None:
                return buf.at[pl.ds(begin, half)]
            return buf.at[pl.ds(begin, half), pl.ds(lo, size)]

        down = remote(part(group), part(0), ssem.at[0], rsem.at[c], me + group)
        up = remote(part(half), part(group + half), ssem.at[1], rsem.at[c], me - group)
        return down, up

    def halo_start(*args):
        down, up = halo(*args)

        @pl.when(has_next)
        def _():
            down.start()

        @pl.when(has_prev)
        def _():
            up.start()

    def halo_arrive(buf, lo, sem, above, below):
        def part(count):
            if lo is None:
                return buf.at[pl.ds(0, count)]
            return buf.at[pl.ds(0, count), pl.ds(lo, size)]

        @pl.when(jnp.logical_and(above, below))
        def _():
            wait_all(part(2 * half), sem)

        @pl.when(jnp.logical_xor(above, below))
        def _():
            wait_all(part(half), sem)

    def halo_wait(buf, lo, ssem, rsem, c):
        halo_arrive(buf, lo, rsem.at[c], has_prev, has_next)

    def halo_sent(spot, ssem, rsem):
        @pl.when(has_next)
        def _():
            sent_all(spot, ssem.at[0], rsem.at[0])

        @pl.when(has_prev)
        def _():
            sent_all(spot, ssem.at[1], rsem.at[0])

    for f, (src, dst) in enumerate(strips):
        own_fields[f].wait()
        spread_start(dst, half, fsend, frecv)

    def lead_pieces(c):
        return ((c * size, size - 1), (c * size + size - 1, 1))

    def item_shift(c, who):
        shared = pooled + both * lax.rem(who, 2) - own
        return jnp.where(c < alone, own * who, shared)

    def lead_copy(o, c, lo, count):
        begin = jnp.minimum(item_shift(c, lax.rem(q + o, group)) + 1 + lo, cohorts - count)
        return remote(
            lead.at[pl.ds(begin, count)], wide2.at[half + q, pl.ds(lo, count)],
            lsend.at[0], lrecv.at[c], peer(o),
        )

    def lead_own(c, lo, count):
        begin = jnp.minimum(item_shift(c, q) + 1 + lo, cohorts - count)
        return pltpu.make_async_copy(
            lead.at[pl.ds(begin, count)], wide2.at[half + q, pl.ds(lo, count)], lrecv.at[c]
        )

    def lead_start(c):
        for piece in lead_pieces(c):
            for o in range(1, group):
                lead_copy(o, c, *piece).start()
            lead_own(c, *piece).start()

    def wait_all(spot, sem):
        pltpu.make_async_copy(spot, spot, sem).wait()

    def sent_all(spot, ssem, rsem):
        remote(spot, spot, ssem, rsem, peer(1)).wait_send()

    def lead_wait(c):
        wait_all(wide2.at[pl.ds(half, group), pl.ds(c * size, size)], lrecv.at[c])

    lead_start(0)
    lead_start(1)

    strips_all = (mask_strip, east_strip, north_strip)
    wides = (wide2, wide1)

    @pl.when(jnp.logical_not(has_prev))
    def _():
        for strip in strips_all:
            strip[0:half] = jnp.zeros((half,) + strip.shape[1:], strip.dtype)
        for wide in wides:
            wide[0:half] = jnp.zeros((half,) + wide.shape[1:], jnp.float32)

    @pl.when(jnp.logical_not(has_next))
    def _():
        for strip in strips_all:
            strip[group + half :] = jnp.zeros((half,) + strip.shape[1:], strip.dtype)
        for wide in wides:
            wide[group + half :] = jnp.zeros((half,) + wide.shape[1:], jnp.float32)

    for d in (d for d in range(-half, half + 1) if d != 0):

        @pl.when(jnp.logical_not(jnp.logical_and(me + d >= 0, me + d < tiles)))
        def _(d=d):
            wide_a[half + d] = jnp.zeros(wide_a.shape[1:], jnp.float32)

    for part in range(group + 2):
        prefix[part, 0] = zero
    starts = [part * own for part in range(group)] + [pooled, pooled + both]
    lengths = [own] * group + [both] * 2

    def upto(spot):
        total = zero
        for part in range(group + 2):
            top = lengths[part] + (part == group + 1)
            total = total + prefix[part, jnp.clip(spot - starts[part], 0, top)]
        return total

    def weighted(kind, values):
        total = table[0, kind] * values[0]
        for k in range(1, forage):
            total = total + table[k, kind] * values[k]
        return total

    def class_sums(store, shift):
        def step(kind, carry):
            before, sums = carry
            here = upto(bounds[kind + 1] + shift)
            some = here - before
            store(kind, some)
            return here, tuple(sums[k] + table[k, kind] * some for k in range(forage))

        return lax.fori_loop(0, classes, step, (upto(shift), (zero,) * forage), unroll=4)[1]

    def fill(into, values, decaying=False):
        def each(kind, carry):
            total = weighted(kind, values)
            into[kind] = jnp.exp(-total) if decaying else total
            return carry

        lax.fori_loop(0, classes, each, 0, unroll=2)

    def prepare(month, dens, by_kind, short_store):
        def adder(parts):
            def add(i, runs):
                new = []
                for part, run in zip(parts, runs):
                    new.append(run + dens[starts[part] + i])
                    prefix[part, i + 1] = new[-1]
                return tuple(new)

            return add

        for parts in (range(group), range(group, group + 2)):
            lax.fori_loop(
                0, lengths[parts[0]], adder(parts), (zero,) * len(parts), unroll=2
            )

        def store(kind, some):
            crowd[month, kind] = some

        hungry = class_sums(store, 0)
        shorts = []
        for k in range(forage):
            feed = food[month, k]
            total = feed + hungry[k]
            shorts.append(hungry[k] / total)
            short_store(k, shorts[k])
            feed_sq[month, k] = feed / (total * total)
            feed_sq[2 + month, k] = hungry[k]
        return shorts

    def store_two(k, value):
        short_all[q, k] = value

    def store_one(k, value):
        short1[k] = value

    loads[0].wait()
    loads[1].wait()
    shorts2 = prepare(1, dens2, kinds2, store_two)
    spread_start(short_all, 0, ssend, srecv)
    lead_start(2)
    fill(kinds2, shorts2, True)

    three = east_strip.at[pl.ds(0, 3)]
    wait_all(three, frecv.at[1])
    for src, dst in strips:
        spread_onward(dst, half, fsend, frecv)
    loads[2].wait()
    shorts1 = prepare(0, dens1, kinds1, store_one)
    fill(kinds1, shorts1, True)
    lead_start(3)
    wait_all(three, frecv.at[0])
    wait_all(three, frecv.at[2])
    for f, (src, dst) in enumerate(strips):
        halo_start(dst, None, hsend.at[f], hrecv, f)

    lane = lax.broadcasted_iota(jnp.int32, (per, LANES), 1)
    last_lane = lane == LANES - 1
    first_lane = lane == 0

    def east_of(x):
        near = pltpu.roll(x, LANES - 1, 1)
        return jnp.where(last_lane, pltpu.roll(near, per - 1, 0), near)

    def west_of(x):
        near = pltpu.roll(x, 1, 1)
        return jnp.where(first_lane, pltpu.roll(near, 1, 0), near)

    def row_of(r):
        return pl.ds(r % rows, per, stride=rows)

    lead_wait(0)
    halo_start(wide2, 0, zsend, zrecv, 0)
    lead_start(4)
    lead_wait(1)
    halo_start(wide2, size, zsend, zrecv, 1)
    lead_start(5)
    for f, (src, dst) in enumerate(strips):
        halo_wait(dst, None, hsend.at[f], hrecv, f)
    span_rows = rows * 2 * group
    masks = [mask_strip[r // rows, row_of(r)].astype(jnp.float32) for r in range(span_rows)]
    for r in range(1, span_rows - 1):
        mask = masks[r]
        east, north = east_strip[r // rows, row_of(r)], north_strip[r // rows, row_of(r)]
        rate_n = mask * masks[r - 1] * (0.1 + jnp.maximum(north, 0.0))
        rate_s = mask * masks[r + 1] * (0.1 + jnp.maximum(-north, 0.0))
        rate_e = mask * east_of(mask) * (0.1 + jnp.maximum(east, 0.0))
        rate_w = mask * west_of(mask) * (0.1 + jnp.maximum(-east, 0.0))
        rates[r, 0] = 1.0 - rate_n - rate_s - rate_e - rate_w
        rates[r, 1] = rate_n
        rates[r, 2] = rate_s
        rates[r, 3] = rate_e
        rates[r, 4] = rate_w

    def advance(fields, shift):
        count = len(fields[0])
        for step in range(SUBSTEPS):
            margin = step + 1
            fresh = [[None] * count for _ in fields]
            for u, old in enumerate(fields):
                for r in range(margin, count - margin):
                    rate = rates.at[r + shift]
                    fresh[u][r] = (
                        rate[0] * old[r]
                        + rate[1] * old[r - 1]
                        + rate[2] * old[r + 1]
                        + rate[3] * east_of(old[r])
                        + rate[4] * west_of(old[r])
                    )
            fields = fresh
        return fields

    def transport(wide, done, c):
        fields = [
            [wide[r // rows, c * size + u, row_of(r)] for r in range(span_rows)]
            for u in range(size)
        ]
        for u, field in enumerate(advance(fields, 0)):
            for r in range(rows * group):
                done[r // rows, c * size + u, row_of(r)] = field[reach + r]

    def transport_both(c):
        base = jnp.where(low, 0, half)
        fields = [
            [wide1[base + r // rows, c * size + u, row_of(r)] for r in range(rows * 3 * half)]
            for u in range(size)
        ]
        for u, field in enumerate(advance(fields, base * rows)):
            for r in range(rows * half):
                done_b[r // rows, (c - alone) * size + u, row_of(r)] = field[reach + r]

    def out_start(done, into, c, ssem, rsem):
        spot = into.at[q, pl.ds(c * size, size)]
        for o in range(1, group):
            part = done.at[lax.rem(q + o, group), pl.ds(c * size, size)]
            remote(part, spot, ssem.at[0], rsem, peer(o)).start()
        pltpu.make_async_copy(done.at[q, pl.ds(c * size, size)], spot, rsem).start()

    def out_wait(into, c, rsem):
        wait_all(into.at[pl.ds(0, group), pl.ds(c * size, size)], rsem.at[c])

    def both_start(done, base, lo, into, c, ssem, rsem):
        spot = into.at[core, pl.ds((c - alone) * size, size)]
        part = done.at[base + 1 - core, pl.ds(lo, size)]
        remote(part, spot, ssem.at[1], rsem, twin).start()
        pltpu.make_async_copy(done.at[base + core, pl.ds(lo, size)], spot, rsem).start()

    def both_wait(into, c, rsem):
        wait_all(into.at[pl.ds(0, 2), pl.ds((c - alone) * size, size)], rsem.at[c])

    def both_sent(spot, ssem, rsem):
        sent_all(spot, ssem.at[1], rsem.at[0])

    def aged_start(c):
        @pl.when(c < alone)
        def _():
            out_start(done2, aged2, c, osend, orecv.at[0])

        @pl.when(c >= alone)
        def _():
            both_start(done2, q - core, c * size, aged_b, c, osend, orecv.at[1])

    def middle(c):
        def each(i, carry):
            a = item_shift(c, q) + i
            kind = cls[a]
            fading = decay[pl.ds(a, 1)]
            for s in range(group):
                wide1[half + s, i] = done2[s, i] * (fading * living[s, kind])
            return carry

        lax.fori_loop(c * size, c * size + size, each, 0)

    def halo_sides(c):
        solo = c < alone
        return jnp.logical_or(solo, low), jnp.logical_or(solo, jnp.logical_not(low))

    def halo_one(c):
        down, up = halo(wide1, c * size, z1send, z1recv, c)
        lower, upper = halo_sides(c)

        @pl.when(jnp.logical_and(has_next, lower))
        def _():
            down.start()

        @pl.when(jnp.logical_and(has_prev, upper))
        def _():
            up.start()

    def halo_one_wait(c):
        lower, upper = halo_sides(c)
        above, below = jnp.logical_and(has_prev, lower), jnp.logical_and(has_next, upper)
        halo_arrive(wide1, c * size, z1recv.at[c], above, below)

    def tally(c, shared, each):
        lo = (c - alone) * size if shared else c * size
        parts = range(group, group + 2) if shared else range(group)

        def step(i, runs):
            new = []
            for part, run in zip(parts, runs):
                new.append(run + each(part, i, starts[part] + i))
                prefix[part, i + 1] = new[-1]
            return tuple(new)

        lax.fori_loop(lo, lo + size, step, tuple(prefix[part, lo] for part in parts))

    def lost_two(part, i, a):
        value = aged2[part, i] if part < group else aged_b[part - group, i]
        return value * (decay[pl.ds(a, 1)] * kinds2[cls[a]]) * dens2[a]

    def keep_one(part, i, a, before):
        value = carried1[part, i] if part < group else carried_b[part - group, i]
        value = value + moved[cls[a]]
        stay = value * (decay[pl.ds(before, 1)] * kinds1[cls[before]])
        out[before] = stay
        return stay * dens1[before]

    def lost_one(part, i, a):
        return keep_one(part, i, a, jnp.maximum(a - 1, 0))

    def finish(month, shift):
        def store(kind, some):
            dead[kind] = some

        ratio = class_sums(store, shift)
        adem = []
        for k in range(forage):
            adem.append(-ratio[k] * feed_sq[month, k])
            sens[month, k] = ratio[k] * feed_sq[2 + month, k] * feed_sq[month, k]
        return adem

    def class_rows(month, adem, short, add):
        def each(kind, carry):
            many, lost = crowd[month, kind], dead[kind]
            for k in range(forage):
                row = jnp.sum(many * adem[k] - lost * short[k], axis=0, keepdims=True)
                if add:
                    row = row + by_class[k, pl.ds(kind, 1)]
                by_class[k, pl.ds(kind, 1)] = row
            return carry

        lax.fori_loop(0, classes, each, 0, unroll=2)

    def live(s, carry):
        shorts = [short_all[s, k] for k in range(forage)]
        fill(living.at[s], shorts, True)
        return carry

    def second(c, carry):
        halo_wait(wide2, c * size, zsend, zrecv, c)

        @pl.when(c >= chunks - halo_ahead)
        def _():
            halo_one(c - chunks + halo_ahead)

        transport(wide2, done2, c)

        @pl.when(c >= out_lag)
        def _():
            aged_start(c - out_lag)

        @pl.when(c == 0)
        def _():
            spread_wait(short_all, 0, ssend, srecv)
            lax.fori_loop(0, group, live, 0)

        middle(c)

        @pl.when(c + 3 < chunks)
        def _():
            lead_wait(c + 3)
            halo_start(wide2, (c + 3) * size, zsend, zrecv, c + 3)

        @pl.when(c + 3 + lead_ahead < chunks)
        def _():
            lead_start(c + 3 + lead_ahead)

        return carry

    spread_pass(short_all, 0, ssend, srecv)
    lead_wait(2)
    halo_start(wide2, 2 * size, zsend, zrecv, 2)
    lead_start(6)
    lax.fori_loop(0, chunks, second, 0)
    for c in range(chunks - out_lag, chunks):
        aged_start(c)

    odd = lax.rem(q, 2)
    side = 1 - 2 * odd
    steps = [(jnp.logical_or(low, has_next), half), (jnp.logical_or(~low, has_prev), -half)]
    onward = jnp.where(odd == 0, steps[0][0], steps[1][0])
    inward = jnp.where(odd == 0, steps[1][0], steps[0][0])

    def near_copy(d, i):
        return remote(
            wide_a.at[half], wide_a.at[half - d], asend.at[i], arecv.at[i], me + d
        )

    def near_start():
        for i, (there, d) in enumerate(steps):

            @pl.when(there)
            def _(i=i, d=d):
                near_copy(d, i).start()

        near_copy(side, 2).start()

    def near_from(slot, i):
        spot = wide_a.at[slot]
        remote(spot, spot, asend.at[i], arecv.at[i], twin).wait_recv()

    def near_pass():
        for i, (there, d) in enumerate(steps):

            @pl.when(steps[1 - i][0])
            def _(i=i, d=d):
                near_from(half - d, i)

        @pl.when(onward)
        def _():
            remote(
                wide_a.at[half + half * side], wide_a.at[half + side], asend.at[3], arecv.at[3],
                twin,
            ).start()

    def near_wait():
        near_from(half + side, 2)

        @pl.when(inward)
        def _():
            near_from(half - side, 3)

    def near_sent():
        for i, (there, d) in enumerate(steps):

            @pl.when(there)
            def _(i=i, d=d):
                near_copy(d, i).wait_send()

        near_copy(side, 2).wait_send()

        @pl.when(onward)
        def _():
            near_copy(side, 3).wait_send()

    def gather_two(c, carry):
        tally(c, False, lost_two)
        return carry

    def gather_both(c, carry):
        tally(c, True, lost_two)
        return carry

    def leading(c, carry):
        halo_one_wait(c)

        @pl.when(c + halo_ahead < chunks)
        def _():
            halo_one(c + halo_ahead)

        transport(wide1, done1, c)
        out_start(done1, carried1, c, o1send, o1recv.at[c])

        @pl.when(c == alone // 2 - 1)
        def _():
            wait_all(aged2, orecv.at[0])
            lax.fori_loop(0, alone, gather_two, 0)
            wait_all(aged_b, orecv.at[1])
            lax.fori_loop(alone, chunks, gather_both, 0)
            adem2 = finish(1, 0)
            for k in range(forage):
                wide_a[half, k] = adem2[k]
            near_start()
            class_rows(1, adem2, [short_all[q, k] for k in range(forage)], False)

        return carry

    lax.fori_loop(0, alone, leading, 0)

    def ending(c, carry):
        out_wait(carried1, c, o1recv)
        tally(c, False, lost_one)
        return carry

    def leading_both(c, carry):
        @pl.when(c == chunks - 3)
        def _():
            near_pass()

        @pl.when(c == chunks - 1)
        def _():
            lax.fori_loop(0, alone - 2, ending, 0)

        @pl.when(c == chunks - 2)
        def _():
            near_wait()

            reach_rows = rows * (2 * half + 1)
            fields = [
                [wide_a[r // rows, k, row_of(r)] for r in range(reach_rows)] for k in range(forage)
            ]
            for k, field in enumerate(advance(fields, rows * q)):
                for r in range(rows):
                    strewn[k, row_of(r)] = field[reach + r]
            fill(moved, [strewn[k] for k in range(forage)])

        halo_one_wait(c)

        @pl.when(c + halo_ahead < chunks)
        def _():
            halo_one(c + halo_ahead)

        transport_both(c)
        both_start(done_b, 0, (c - alone) * size, carried_b, c, o1send, o1recv.at[c])
        return carry

    lax.fori_loop(alone, chunks, leading_both, 0)
    def ending_both(c, carry):
        both_wait(carried_b, c, o1recv)
        tally(c, True, lost_one)
        return carry

    lax.fori_loop(alone - 2, alone, ending, 0)
    lax.fori_loop(alone, chunks, ending_both, 0)
    gone = keep_one(group + 1, both - 1, cohorts - 1, cohorts - 1)
    prefix[group + 1, both + 1] = prefix[group + 1, both] + gone
    adem1 = finish(0, 1)
    class_rows(0, adem1, [short1[k] for k in range(forage)], True)

    ones = jnp.ones((8, LANES), jnp.float32)
    sums = []
    for k in range(forage):
        lanes_sum = lax.dot_general(
            ones, by_class[k], (((1,), (1,)), ((), ())), precision=lax.Precision.HIGHEST,
            preferred_element_type=jnp.float32,
        )
        sums.append(lanes_sum[0:1])
    totals[me] = jnp.concatenate(sums, axis=0)

    def total_start(t, carry):
        other = lax.rem(me + t, tiles)
        remote(totals.at[me], totals.at[me], nsend.at[0], nrecv.at[0], other).start()
        return carry

    lax.fori_loop(1, tiles, total_start, 0)
    fill(adding, adem1)

    def outgoing(a, carry):
        out[a] = out[a] + adding[cls[a]]
        return carry

    lax.fori_loop(0, cohorts, outgoing, 0, unroll=4)
    mine = pl.ds(0, group - 1)
    sent_all(wide2.at[mine], lsend.at[0], lrecv.at[0])
    sent_all(done2.at[mine, pl.ds(0, own)], osend.at[0], orecv.at[0])
    both_sent(done2.at[0, pl.ds(own, both)], osend, orecv)
    spread_sent(short_all, 0, ssend, srecv)
    halo_sent(wide2.at[pl.ds(0, half)], zsend, zrecv)
    for down_count, up_count, here in ((own + both, own, low), (own, own + both, ~low)):

        @pl.when(jnp.logical_and(here, has_next))
        def _(count=down_count):
            sent_all(wide1.at[pl.ds(0, half), pl.ds(0, count)], z1send.at[0], z1recv.at[0])

        @pl.when(jnp.logical_and(here, has_prev))
        def _(count=up_count):
            sent_all(wide1.at[pl.ds(0, half), pl.ds(0, count)], z1send.at[1], z1recv.at[0])

    for f, (src, dst) in enumerate(strips):
        sent_all(three, fsend.at[f], frecv.at[f])
        halo_sent(dst.at[pl.ds(0, half)], hsend.at[f], hrecv)
    sent_all(done1.at[mine], o1send.at[0], o1recv.at[0])
    both_sent(done_b.at[0], o1send, o1recv)
    near_sent()
    others = totals.at[pl.ds(0, tiles - 1)]
    wait_all(others, nrecv.at[0])
    grad_out[...] = lax.fori_loop(
        1, tiles, lambda t, total: total + totals[t], totals[0]
    ) / (tiles * blocks * LANES)
    sent_all(others, nsend.at[0], nrecv.at[0])


def last_kernel(*refs):
    count = len(refs) // 2
    copies = [
        pltpu.make_async_copy(refs[i], refs[count + i], refs[2 * count].at[i])
        for i in range(count)
    ]
    for copy in copies:
        copy.start()
    for copy in copies:
        copy.wait()


def blocked(x):
    rows, columns = x.shape[-2:]
    head = x.shape[:-2]
    n = len(head)
    y = x.reshape(head + (rows, columns // LANES, LANES))
    y = jnp.swapaxes(y, n, n + 1)
    return y.reshape(head + (rows * columns // LANES, LANES))


def unblocked(x, rows):
    head = x.shape[:-2]
    n = len(head)
    y = x.reshape(head + (x.shape[-2] // rows, rows, LANES))
    y = jnp.swapaxes(y, n, n + 1)
    return y.reshape(head + (rows, -1))


def shards(
    final_adjoint,
    first_density,
    second_density,
    forage,
    preference,
    base_mortality,
    age_class,
    land_mask,
    east_velocity,
    north_velocity,
):
    classes, groups = preference.shape
    cohorts, rows, columns = final_adjoint.shape
    tiles = lax.axis_size("tile")
    group = 2 * SUBSTEPS // rows
    size = 5
    chunks = 10
    alone = (cohorts // size - 2 * chunks) // (group - 2)
    own, both = alone * size, (chunks - alone) * size
    blocks = rows * columns // LANES
    f32 = jnp.float32
    dma = pltpu.SemaphoreType.DMA
    vmem = pl.BlockSpec(memory_space=pltpu.VMEM)
    smem = pl.BlockSpec(memory_space=pltpu.SMEM)
    hbm = pl.BlockSpec(memory_space=pl.ANY)
    dims = (tiles, group, rows, cohorts, size, alone, chunks, groups, 4, 4, 3)
    cell = (blocks, LANES)

    def body(*refs):
        kernel(dims, *refs)

    def cells(*lead):
        return pltpu.VMEM(lead + cell, f32)

    results = pl.pallas_call(
        body,
        out_shape=(
            cells(cohorts),
            cells(2, groups),
            pltpu.VMEM((groups, classes), f32),
        ),
        in_specs=[hbm] * 10,
        out_specs=(vmem, vmem, vmem),
        scratch_shapes=[
            cells(2 * group, own + both),
            cells(2 * group, own + both),
            cells(group + 1, groups),
            cells(group, own + both),
            cells(group, own),
            cells(2, both),
            cells(group, own),
            cells(2, both),
            cells(group, own),
            cells(2, both),
            pltpu.VMEM((2 * group,) + cell, jnp.int32),
            cells(2 * group),
            cells(2 * group),
            pltpu.VMEM((2 * group * rows, 5, blocks // rows, LANES), f32),
            cells(group, groups),
            cells(groups),
            cells(groups),
            cells(4, groups),
            cells(cohorts),
            cells(cohorts),
            cells(2, groups),
            pltpu.VMEM((cohorts, LANES), f32),
            cells(classes),
            cells(classes),
            cells(classes),
            cells(classes),
            cells(group, classes),
            cells(2, classes),
            cells(classes),
            cells(group + 2, max(own, both) + 2),
            pltpu.VMEM((groups, classes, LANES), f32),
            pltpu.VMEM((tiles, groups, classes), f32),
            pltpu.SMEM((classes + 1,), jnp.int32),
            pltpu.SMEM((groups, classes), f32),
            pltpu.VMEM((1, cohorts), f32),
            pltpu.SMEM((cohorts,), jnp.int32),
        ]
        + [dma((1,)), dma((chunks,)), dma((2,)), dma((chunks,)), dma((2,)), dma((2,))]
        + [dma((2,)), dma((chunks,)), dma((2,)), dma((chunks,)), dma((3,)), dma((3,))]
        + [dma((3, 2)), dma((3,)), dma((3,)), dma((3,)), dma((4,)), dma((4,))]
        + [dma((1,)), dma((1,)), dma((9,))],
        compiler_params=pltpu.CompilerParams(
            collective_id=0, has_side_effects=True, vmem_limit_bytes=56 * 1024 * 1024
        ),
        name="adjoint",
    )(
        preference.T,
        base_mortality.reshape(1, -1),
        age_class,
        blocked(final_adjoint),
        blocked(first_density),
        blocked(second_density),
        blocked(forage),
        blocked(land_mask),
        blocked(east_velocity),
        blocked(north_velocity),
    )
    out, sens, grad = pl.pallas_call(
        last_kernel,
        out_shape=tuple(jax.ShapeDtypeStruct(x.shape, x.dtype) for x in results),
        in_specs=[vmem] * len(results),
        out_specs=(hbm,) * len(results),
        scratch_shapes=[dma((len(results),))],
        name="outgoing",
    )(*(pltpu.with_memory_space_constraint(x, pltpu.VMEM) for x in results))
    summed = grad.T
    return (unblocked(out, rows), unblocked(sens, rows), summed)


def solution(mesh):
    in_specs = (
        P("ens", "tile", None),
        P("ens", "tile", None),
        P("ens", "tile", None),
        P("ens", None, "tile", None),
        P("ens", None),
        P(),
        P(),
        P("tile", None),
        P("tile", None),
        P("tile", None),
    )
    out_specs = (P("ens", "tile", None), P("ens", None, "tile", None), P("ens", None))
    return jax.shard_map(shards, mesh=mesh, in_specs=in_specs, out_specs=out_specs, check_vma=False)
```

```python
import jax
import jax.numpy as jnp
from jax import lax
from jax.experimental import pallas as pl
from jax.experimental.pallas import tpu as pltpu
from jax.sharding import PartitionSpec as P

SUBSTEPS = 4
LANES = 128
MESH = pl.DeviceIdType.MESH


def kernel(
    dims,
    table_in,
    base_in,
    cls_in,
    lead,
    dens1_in,
    dens2_in,
    food_in,
    mask_in,
    east_in,
    north_in,
    out,
    sens,
    grad_out,
    wide2,
    wide1,
    wide_a,
    done2,
    done1,
    done_b,
    aged2,
    aged_b,
    carried1,
    carried_b,
    mask_strip,
    east_strip,
    north_strip,
    rates,
    short_all,
    short1,
    strewn,
    feed_sq,
    dens1,
    dens2,
    food,
    decay,
    kinds2,
    kinds1,
    moved,
    adding,
    living,
    crowd,
    dead,
    prefix,
    by_class,
    totals,
    bounds,
    table,
    base_row,
    cls,
    lsend,
    lrecv,
    zsend,
    zrecv,
    osend,
    orecv,
    z1send,
    z1recv,
    o1send,
    o1recv,
    fsend,
    frecv,
    hsend,
    hrecv,
    ssend,
    srecv,
    asend,
    arecv,
    nsend,
    nrecv,
    own_sem,
):
    tiles, group, rows, cohorts, size, alone, chunks, forage, lead_ahead, out_lag, halo_ahead = dims
    half = group // 2
    own = alone * size
    both = (chunks - alone) * size
    pooled = group * own
    blocks = food.shape[2]
    per = blocks // rows
    reach = half * rows
    classes = table.shape[1]
    me = lax.axis_index("tile")
    q = lax.rem(me, group)
    first = me - q
    has_prev = me >= group
    has_next = me < tiles - group

    def peer(o):
        return first + lax.rem(q + o, group)

    def source(o):
        return lax.rem(q + group - o, group)

    barrier = pltpu.get_barrier_semaphore()
    spans = tiles // group
    twin = me + 1 - 2 * lax.rem(q, 2)
    across = peer(half)
    low = q < half
    core = lax.rem(q, 2)
    beyond = [
        (has_next, me + group),
        (has_prev, me - group),
        (jnp.logical_and(jnp.logical_not(low), has_next), me + half),
        (jnp.logical_and(low, has_prev), me - half),
    ]
    if spans > 4:

        def greet(t, carry):
            other = lax.rem(me + t, tiles)
            pl.semaphore_signal(barrier, inc=1, device_id={"tile": other}, device_id_type=MESH)
            return carry

        lax.fori_loop(1, tiles, greet, 0)
    else:
        for o in range(1, group):
            pl.semaphore_signal(barrier, inc=1, device_id={"tile": peer(o)}, device_id_type=MESH)
        for there, other in beyond:

            @pl.when(there)
            def _(other=other):
                pl.semaphore_signal(
                    barrier, inc=1, device_id={"tile": other}, device_id_type=MESH
                )

    smalls = [
        pltpu.make_async_copy(src, dst, own_sem.at[6 + i])
        for i, (src, dst) in enumerate(((base_in, base_row), (cls_in, cls), (table_in, table)))
    ]
    for copy in smalls:
        copy.start()
    loads = [
        pltpu.make_async_copy(src, dst, own_sem.at[3 + i])
        for i, (src, dst) in enumerate(((dens2_in, dens2), (food_in, food), (dens1_in, dens1)))
    ]
    for copy in loads:
        copy.start()
    strips = ((mask_in, mask_strip), (east_in, east_strip), (north_in, north_strip))
    own_fields = [
        pltpu.make_async_copy(src, dst.at[half + q], own_sem.at[f])
        for f, (src, dst) in enumerate(strips)
    ]
    for copy in own_fields:
        copy.start()

    zero = jnp.zeros((blocks, LANES), jnp.float32)

    smalls[0].wait()
    fall = jnp.exp(-base_row[...])
    along = lax.broadcasted_iota(jnp.int32, (cohorts, cohorts), 1)
    down = lax.broadcasted_iota(jnp.int32, (cohorts, cohorts), 0)
    spread = jnp.where(along == down, fall, 0.0)
    decay[...] = jnp.broadcast_to(jnp.sum(spread, axis=1, keepdims=True), (cohorts, LANES))

    def bound(kind):
        spot = jnp.int32(0)
        width = 1
        while 2 * width <= cohorts:
            width = 2 * width
        while width >= 1:
            last = jnp.minimum(spot + width, cohorts) - 1
            ok = jnp.logical_and(spot + width <= cohorts, cls[last] < kind)
            spot = jnp.where(ok, spot + width, spot)
            width = width // 2
        return spot

    smalls[1].wait()
    smalls[2].wait()
    bounds[0] = jnp.int32(0)
    for kind in range(1, classes):
        bounds[kind] = bound(kind)
    bounds[classes] = jnp.int32(cohorts)

    if spans > 4:
        pl.semaphore_wait(barrier, tiles - 1)
    else:
        pl.semaphore_wait(barrier, group - 1 + sum(there.astype(jnp.int32) for there, _ in beyond))

    def remote(src, dst, ssem, rsem, target):
        return pltpu.make_async_remote_copy(
            src_ref=src, dst_ref=dst, send_sem=ssem, recv_sem=rsem,
            device_id={"tile": target}, device_id_type=MESH,
        )

    def spread_copy(buf, slot, ssem, rsem, i, target):
        return remote(buf.at[slot], buf.at[slot], ssem.at[i], rsem.at[i], target)

    def spread_start(buf, lift, ssem, rsem):
        spread_copy(buf, lift + q, ssem, rsem, 1, across).start()
        spread_copy(buf, lift + q, ssem, rsem, 0, twin).start()

    def spread_onward(buf, lift, ssem, rsem):
        spread_copy(buf, lift + across - first, ssem, rsem, 2, twin).start()

    def spread_pass(buf, lift, ssem, rsem):
        spread_copy(buf, lift + across - first, ssem, rsem, 1, across).wait_recv()
        spread_onward(buf, lift, ssem, rsem)

    def spread_wait(buf, lift, ssem, rsem):
        spread_copy(buf, lift + twin - first, ssem, rsem, 0, twin).wait_recv()
        spread_copy(buf, lift + lax.rem(twin - first + half, group), ssem, rsem, 2, twin).wait_recv()

    def spread_sent(buf, lift, ssem, rsem):
        for i in range(3):
            spread_copy(buf, lift + q, ssem, rsem, i, twin).wait_send()

    def halo(buf, lo, ssem, rsem, c):
        def part(begin):
            if lo is None:
                return buf.at[pl.ds(begin, half)]
            return buf.at[pl.ds(begin, half), pl.ds(lo, size)]

        down = remote(part(group), part(0), ssem.at[0], rsem.at[c], me + group)
        up = remote(part(half), part(group + half), ssem.at[1], rsem.at[c], me - group)
        return down, up

    def halo_start(*args):
        down, up = halo(*args)

        @pl.when(has_next)
        def _():
            down.start()

        @pl.when(has_prev)
        def _():
            up.start()

    def halo_arrive(buf, lo, sem, above, below):
        def part(count):
            if lo is None:
                return buf.at[pl.ds(0, count)]
            return buf.at[pl.ds(0, count), pl.ds(lo, size)]

        @pl.when(jnp.logical_and(above, below))
        def _():
            wait_all(part(2 * half), sem)

        @pl.when(jnp.logical_xor(above, below))
        def _():
            wait_all(part(half), sem)

    def halo_wait(buf, lo, ssem, rsem, c):
        halo_arrive(buf, lo, rsem.at[c], has_prev, has_next)

    def halo_sent(spot, ssem, rsem):
        @pl.when(has_next)
        def _():
            sent_all(spot, ssem.at[0], rsem.at[0])

        @pl.when(has_prev)
        def _():
            sent_all(spot, ssem.at[1], rsem.at[0])

    for f, (src, dst) in enumerate(strips):
        own_fields[f].wait()
        spread_start(dst, half, fsend, frecv)

    def lead_pieces(c):
        if isinstance(c, int) and c < alone:
            return ((c * size, size),)
        return ((c * size, size - 1), (c * size + size - 1, 1))

    def item_shift(c, who):
        shared = pooled + both * lax.rem(who, 2) - own
        return jnp.where(c < alone, own * who, shared)

    def lead_copy(o, c, lo, count):
        begin = jnp.minimum(item_shift(c, lax.rem(q + o, group)) + 1 + lo, cohorts - count)
        return remote(
            lead.at[pl.ds(begin, count)], wide2.at[half + q, pl.ds(lo, count)],
            lsend.at[0], lrecv.at[c], peer(o),
        )

    def lead_own(c, lo, count):
        begin = jnp.minimum(item_shift(c, q) + 1 + lo, cohorts - count)
        return pltpu.make_async_copy(
            lead.at[pl.ds(begin, count)], wide2.at[half + q, pl.ds(lo, count)], lrecv.at[c]
        )

    def lead_start(c):
        for piece in lead_pieces(c):
            for o in range(1, group):
                lead_copy(o, c, *piece).start()
            lead_own(c, *piece).start()

    def wait_all(spot, sem):
        pltpu.make_async_copy(spot, spot, sem).wait()

    def sent_all(spot, ssem, rsem):
        remote(spot, spot, ssem, rsem, peer(1)).wait_send()

    def lead_wait(c):
        wait_all(wide2.at[pl.ds(half, group), pl.ds(c * size, size)], lrecv.at[c])

    lead_start(0)
    lead_start(1)

    strips_all = (mask_strip, east_strip, north_strip)
    wides = (wide2, wide1)

    @pl.when(jnp.logical_not(has_prev))
    def _():
        for strip in strips_all:
            strip[0:half] = jnp.zeros((half,) + strip.shape[1:], strip.dtype)
        for wide in wides:
            wide[0:half] = jnp.zeros((half,) + wide.shape[1:], jnp.float32)

    @pl.when(jnp.logical_not(has_next))
    def _():
        for strip in strips_all:
            strip[group + half :] = jnp.zeros((half,) + strip.shape[1:], strip.dtype)
        for wide in wides:
            wide[group + half :] = jnp.zeros((half,) + wide.shape[1:], jnp.float32)

    for d in (d for d in range(-half, half + 1) if d != 0):

        @pl.when(jnp.logical_not(jnp.logical_and(me + d >= 0, me + d < tiles)))
        def _(d=d):
            wide_a[half + d] = jnp.zeros(wide_a.shape[1:], jnp.float32)

    for part in range(group + 2):
        prefix[part, 0] = zero
    starts = [part * own for part in range(group)] + [pooled, pooled + both]
    lengths = [own] * group + [both] * 2

    def upto(spot):
        total = zero
        for part in range(group + 2):
            top = lengths[part] + (part == group + 1)
            total = total + prefix[part, jnp.clip(spot - starts[part], 0, top)]
        return total

    def weighted(kind, values):
        total = table[0, kind] * values[0]
        for k in range(1, forage):
            total = total + table[k, kind] * values[k]
        return total

    def class_sums(store, shift):
        def step(kind, carry):
            before, sums = carry
            here = upto(bounds[kind + 1] + shift)
            some = here - before
            store(kind, some)
            return here, tuple(sums[k] + table[k, kind] * some for k in range(forage))

        return lax.fori_loop(0, classes, step, (upto(shift), (zero,) * forage), unroll=4)[1]

    def fill(into, values, decaying=False):
        def each(kind, carry):
            total = weighted(kind, values)
            into[kind] = jnp.exp(-total) if decaying else total
            return carry

        lax.fori_loop(0, classes, each, 0, unroll=2)

    def prepare(month, dens, by_kind, short_store):
        def adder(parts):
            def add(i, runs):
                new = []
                for part, run in zip(parts, runs):
                    new.append(run + dens[starts[part] + i])
                    prefix[part, i + 1] = new[-1]
                return tuple(new)

            return add

        for parts in (range(group), range(group, group + 2)):
            lax.fori_loop(
                0, lengths[parts[0]], adder(parts), (zero,) * len(parts), unroll=2
            )

        def store(kind, some):
            crowd[month, kind] = some

        hungry = class_sums(store, 0)
        shorts = []
        for k in range(forage):
            feed = food[month, k]
            total = feed + hungry[k]
            shorts.append(hungry[k] / total)
            short_store(k, shorts[k])
            feed_sq[month, k] = feed / (total * total)
            feed_sq[2 + month, k] = hungry[k]
        return shorts

    def store_two(k, value):
        short_all[q, k] = value

    def store_one(k, value):
        short1[k] = value

    loads[0].wait()
    loads[1].wait()
    shorts2 = prepare(1, dens2, kinds2, store_two)
    spread_start(short_all, 0, ssend, srecv)
    lead_start(2)
    fill(kinds2, shorts2, True)

    three = east_strip.at[pl.ds(0, 3)]
    wait_all(three, frecv.at[1])
    for src, dst in strips:
        spread_onward(dst, half, fsend, frecv)
    loads[2].wait()
    shorts1 = prepare(0, dens1, kinds1, store_one)
    fill(kinds1, shorts1, True)
    lead_start(3)
    wait_all(three, frecv.at[0])
    wait_all(three, frecv.at[2])
    for f, (src, dst) in enumerate(strips):
        halo_start(dst, None, hsend.at[f], hrecv, f)

    lane = lax.broadcasted_iota(jnp.int32, (per, LANES), 1)
    last_lane = lane == LANES - 1
    first_lane = lane == 0

    def east_of(x):
        near = pltpu.roll(x, LANES - 1, 1)
        return jnp.where(last_lane, pltpu.roll(near, per - 1, 0), near)

    def west_of(x):
        near = pltpu.roll(x, 1, 1)
        return jnp.where(first_lane, pltpu.roll(near, 1, 0), near)

    def row_of(r):
        return pl.ds(r % rows, per, stride=rows)

    lead_wait(0)
    halo_start(wide2, 0, zsend, zrecv, 0)
    lead_start(4)
    lead_wait(1)
    halo_start(wide2, size, zsend, zrecv, 1)
    lead_start(5)
    for f, (src, dst) in enumerate(strips):
        halo_wait(dst, None, hsend.at[f], hrecv, f)
    span_rows = rows * 2 * group
    masks = [mask_strip[r // rows, row_of(r)].astype(jnp.float32) for r in range(span_rows)]
    for r in range(1, span_rows - 1):
        mask = masks[r]
        east, north = east_strip[r // rows, row_of(r)], north_strip[r // rows, row_of(r)]
        rate_n = mask * masks[r - 1] * (0.1 + jnp.maximum(north, 0.0))
        rate_s = mask * masks[r + 1] * (0.1 + jnp.maximum(-north, 0.0))
        rate_e = mask * east_of(mask) * (0.1 + jnp.maximum(east, 0.0))
        rate_w = mask * west_of(mask) * (0.1 + jnp.maximum(-east, 0.0))
        rates[r, 0] = 1.0 - rate_n - rate_s - rate_e - rate_w
        rates[r, 1] = rate_n
        rates[r, 2] = rate_s
        rates[r, 3] = rate_e
        rates[r, 4] = rate_w

    def advance(fields, shift):
        count = len(fields[0])
        for step in range(SUBSTEPS):
            margin = step + 1
            fresh = [[None] * count for _ in fields]
            for u, old in enumerate(fields):
                for r in range(margin, count - margin):
                    rate = rates.at[r + shift]
                    fresh[u][r] = (
                        rate[0] * old[r]
                        + rate[1] * old[r - 1]
                        + rate[2] * old[r + 1]
                        + rate[3] * east_of(old[r])
                        + rate[4] * west_of(old[r])
                    )
            fields = fresh
        return fields

    def transport(wide, done, c):
        fields = [
            [wide[r // rows, c * size + u, row_of(r)] for r in range(span_rows)]
            for u in range(size)
        ]
        for u, field in enumerate(advance(fields, 0)):
            for r in range(rows * group):
                done[r // rows, c * size + u, row_of(r)] = field[reach + r]

    def transport_both(c):
        base = jnp.where(low, 0, half)
        fields = [
            [wide1[base + r // rows, c * size + u, row_of(r)] for r in range(rows * 3 * half)]
            for u in range(size)
        ]
        for u, field in enumerate(advance(fields, base * rows)):
            for r in range(rows * half):
                done_b[r // rows, (c - alone) * size + u, row_of(r)] = field[reach + r]

    def out_start(done, into, c, ssem, rsem):
        spot = into.at[q, pl.ds(c * size, size)]
        for o in range(1, group):
            part = done.at[lax.rem(q + o, group), pl.ds(c * size, size)]
            remote(part, spot, ssem.at[0], rsem, peer(o)).start()
        pltpu.make_async_copy(done.at[q, pl.ds(c * size, size)], spot, rsem).start()

    def out_wait(into, c, rsem):
        wait_all(into.at[pl.ds(0, group), pl.ds(c * size, size)], rsem.at[c])

    def both_start(done, base, lo, into, c, ssem, rsem):
        spot = into.at[core, pl.ds((c - alone) * size, size)]
        part = done.at[base + 1 - core, pl.ds(lo, size)]
        remote(part, spot, ssem.at[1], rsem, twin).start()
        pltpu.make_async_copy(done.at[base + core, pl.ds(lo, size)], spot, rsem).start()

    def both_wait(into, c, rsem):
        wait_all(into.at[pl.ds(0, 2), pl.ds((c - alone) * size, size)], rsem.at[c])

    def both_sent(spot, ssem, rsem):
        sent_all(spot, ssem.at[1], rsem.at[0])

    def aged_start(c):
        @pl.when(c < alone)
        def _():
            out_start(done2, aged2, c, osend, orecv.at[0])

        @pl.when(c >= alone)
        def _():
            both_start(done2, q - core, c * size, aged_b, c, osend, orecv.at[1])

    def middle(c):
        def each(i, carry):
            a = item_shift(c, q) + i
            kind = cls[a]
            fading = decay[pl.ds(a, 1)]
            for s in range(group):
                wide1[half + s, i] = done2[s, i] * (fading * living[s, kind])
            return carry

        lax.fori_loop(c * size, c * size + size, each, 0)

    def halo_sides(c):
        solo = c < alone
        return jnp.logical_or(solo, low), jnp.logical_or(solo, jnp.logical_not(low))

    def halo_one(c):
        down, up = halo(wide1, c * size, z1send, z1recv, c)
        lower, upper = halo_sides(c)

        @pl.when(jnp.logical_and(has_next, lower))
        def _():
            down.start()

        @pl.when(jnp.logical_and(has_prev, upper))
        def _():
            up.start()

    def halo_one_wait(c):
        lower, upper = halo_sides(c)
        above, below = jnp.logical_and(has_prev, lower), jnp.logical_and(has_next, upper)
        halo_arrive(wide1, c * size, z1recv.at[c], above, below)

    def tally(c, shared, each):
        lo = (c - alone) * size if shared else c * size
        parts = range(group, group + 2) if shared else range(group)

        def step(i, runs):
            new = []
            for part, run in zip(parts, runs):
                new.append(run + each(part, i, starts[part] + i))
                prefix[part, i + 1] = new[-1]
            return tuple(new)

        lax.fori_loop(lo, lo + size, step, tuple(prefix[part, lo] for part in parts))

    def lost_two(part, i, a):
        value = aged2[part, i] if part < group else aged_b[part - group, i]
        return value * (decay[pl.ds(a, 1)] * kinds2[cls[a]]) * dens2[a]

    def keep_one(part, i, a, before):
        value = carried1[part, i] if part < group else carried_b[part - group, i]
        value = value + moved[cls[a]]
        stay = value * (decay[pl.ds(before, 1)] * kinds1[cls[before]])
        out[before] = stay
        return stay * dens1[before]

    def lost_one(part, i, a):
        return keep_one(part, i, a, jnp.maximum(a - 1, 0))

    def finish(month, shift):
        def store(kind, some):
            dead[kind] = some

        ratio = class_sums(store, shift)
        adem = []
        for k in range(forage):
            adem.append(-ratio[k] * feed_sq[month, k])
            sens[month, k] = ratio[k] * feed_sq[2 + month, k] * feed_sq[month, k]
        return adem

    def class_rows(month, adem, short, add):
        def each(kind, carry):
            many, lost = crowd[month, kind], dead[kind]
            for k in range(forage):
                row = jnp.sum(many * adem[k] - lost * short[k], axis=0, keepdims=True)
                if add:
                    row = row + by_class[k, pl.ds(kind, 1)]
                by_class[k, pl.ds(kind, 1)] = row
            return carry

        lax.fori_loop(0, classes, each, 0, unroll=2)

    def live(s, carry):
        shorts = [short_all[s, k] for k in range(forage)]
        fill(living.at[s], shorts, True)
        return carry

    def second(c, carry):
        halo_wait(wide2, c * size, zsend, zrecv, c)

        @pl.when(c >= chunks - halo_ahead)
        def _():
            halo_one(c - chunks + halo_ahead)

        transport(wide2, done2, c)

        @pl.when(c >= out_lag)
        def _():
            aged_start(c - out_lag)

        @pl.when(c == 0)
        def _():
            spread_wait(short_all, 0, ssend, srecv)
            lax.fori_loop(0, group, live, 0)

        middle(c)

        @pl.when(c + 3 < chunks)
        def _():
            lead_wait(c + 3)
            halo_start(wide2, (c + 3) * size, zsend, zrecv, c + 3)

        @pl.when(c + 3 + lead_ahead < chunks)
        def _():
            lead_start(c + 3 + lead_ahead)

        return carry

    spread_pass(short_all, 0, ssend, srecv)
    lead_wait(2)
    halo_start(wide2, 2 * size, zsend, zrecv, 2)
    lead_start(6)
    lax.fori_loop(0, chunks, second, 0)
    for c in range(chunks - out_lag, chunks):
        aged_start(c)

    odd = lax.rem(q, 2)
    side = 1 - 2 * odd
    steps = [(jnp.logical_or(low, has_next), half), (jnp.logical_or(~low, has_prev), -half)]
    onward = jnp.where(odd == 0, steps[0][0], steps[1][0])
    inward = jnp.where(odd == 0, steps[1][0], steps[0][0])

    def near_copy(d, i):
        return remote(
            wide_a.at[half], wide_a.at[half - d], asend.at[i], arecv.at[i], me + d
        )

    def near_start():
        for i, (there, d) in enumerate(steps):

            @pl.when(there)
            def _(i=i, d=d):
                near_copy(d, i).start()

        near_copy(side, 2).start()

    def near_from(slot, i):
        spot = wide_a.at[slot]
        remote(spot, spot, asend.at[i], arecv.at[i], twin).wait_recv()

    def near_pass():
        for i, (there, d) in enumerate(steps):

            @pl.when(steps[1 - i][0])
            def _(i=i, d=d):
                near_from(half - d, i)

        @pl.when(onward)
        def _():
            remote(
                wide_a.at[half + half * side], wide_a.at[half + side], asend.at[3], arecv.at[3],
                twin,
            ).start()

    def near_wait():
        near_from(half + side, 2)

        @pl.when(inward)
        def _():
            near_from(half - side, 3)

    def near_sent():
        for i, (there, d) in enumerate(steps):

            @pl.when(there)
            def _(i=i, d=d):
                near_copy(d, i).wait_send()

        near_copy(side, 2).wait_send()

        @pl.when(onward)
        def _():
            near_copy(side, 3).wait_send()

    def gather_two(c, carry):
        tally(c, False, lost_two)
        return carry

    def gather_both(c, carry):
        tally(c, True, lost_two)
        return carry

    def leading(c, carry):
        halo_one_wait(c)

        @pl.when(c + halo_ahead < chunks)
        def _():
            halo_one(c + halo_ahead)

        transport(wide1, done1, c)
        out_start(done1, carried1, c, o1send, o1recv.at[c])

        @pl.when(c == alone // 2 - 1)
        def _():
            wait_all(aged2, orecv.at[0])
            lax.fori_loop(0, alone, gather_two, 0)
            wait_all(aged_b, orecv.at[1])
            lax.fori_loop(alone, chunks, gather_both, 0)
            adem2 = finish(1, 0)
            for k in range(forage):
                wide_a[half, k] = adem2[k]
            near_start()
            class_rows(1, adem2, [short_all[q, k] for k in range(forage)], False)

        return carry

    lax.fori_loop(0, alone, leading, 0)

    def ending(c, carry):
        out_wait(carried1, c, o1recv)
        tally(c, False, lost_one)
        return carry

    def leading_both(c, carry):
        @pl.when(c == chunks - 3)
        def _():
            near_pass()

        @pl.when(c == chunks - 1)
        def _():
            lax.fori_loop(0, alone - 2, ending, 0)

        @pl.when(c == chunks - 2)
        def _():
            near_wait()

            reach_rows = rows * (2 * half + 1)
            fields = [
                [wide_a[r // rows, k, row_of(r)] for r in range(reach_rows)] for k in range(forage)
            ]
            for k, field in enumerate(advance(fields, rows * q)):
                for r in range(rows):
                    strewn[k, row_of(r)] = field[reach + r]
            fill(moved, [strewn[k] for k in range(forage)])

        halo_one_wait(c)

        @pl.when(c + halo_ahead < chunks)
        def _():
            halo_one(c + halo_ahead)

        transport_both(c)
        both_start(done_b, 0, (c - alone) * size, carried_b, c, o1send, o1recv.at[c])
        return carry

    lax.fori_loop(alone, chunks, leading_both, 0)
    def ending_both(c, carry):
        both_wait(carried_b, c, o1recv)
        tally(c, True, lost_one)
        return carry

    lax.fori_loop(alone - 2, alone, ending, 0)
    lax.fori_loop(alone, chunks, ending_both, 0)
    gone = keep_one(group + 1, both - 1, cohorts - 1, cohorts - 1)
    prefix[group + 1, both + 1] = prefix[group + 1, both] + gone
    adem1 = finish(0, 1)
    class_rows(0, adem1, [short1[k] for k in range(forage)], True)

    ones = jnp.ones((8, LANES), jnp.float32)
    sums = []
    for k in range(forage):
        lanes_sum = lax.dot_general(
            ones, by_class[k], (((1,), (1,)), ((), ())), precision=lax.Precision.HIGHEST,
            preferred_element_type=jnp.float32,
        )
        sums.append(lanes_sum[0:1])
    totals[me] = jnp.concatenate(sums, axis=0)

    def total_start(t, carry):
        other = lax.rem(me + t, tiles)
        remote(totals.at[me], totals.at[me], nsend.at[0], nrecv.at[0], other).start()
        return carry

    lax.fori_loop(1, tiles, total_start, 0)
    fill(adding, adem1)

    def outgoing(a, carry):
        out[a] = out[a] + adding[cls[a]]
        return carry

    lax.fori_loop(0, cohorts, outgoing, 0, unroll=4)
    mine = pl.ds(0, group - 1)
    sent_all(wide2.at[mine], lsend.at[0], lrecv.at[0])
    sent_all(done2.at[mine, pl.ds(0, own)], osend.at[0], orecv.at[0])
    both_sent(done2.at[0, pl.ds(own, both)], osend, orecv)
    spread_sent(short_all, 0, ssend, srecv)
    halo_sent(wide2.at[pl.ds(0, half)], zsend, zrecv)
    for down_count, up_count, here in ((own + both, own, low), (own, own + both, ~low)):

        @pl.when(jnp.logical_and(here, has_next))
        def _(count=down_count):
            sent_all(wide1.at[pl.ds(0, half), pl.ds(0, count)], z1send.at[0], z1recv.at[0])

        @pl.when(jnp.logical_and(here, has_prev))
        def _(count=up_count):
            sent_all(wide1.at[pl.ds(0, half), pl.ds(0, count)], z1send.at[1], z1recv.at[0])

    for f, (src, dst) in enumerate(strips):
        sent_all(three, fsend.at[f], frecv.at[f])
        halo_sent(dst.at[pl.ds(0, half)], hsend.at[f], hrecv)
    sent_all(done1.at[mine], o1send.at[0], o1recv.at[0])
    both_sent(done_b.at[0], o1send, o1recv)
    near_sent()
    others = totals.at[pl.ds(0, tiles - 1)]
    wait_all(others, nrecv.at[0])
    grad_out[...] = lax.fori_loop(
        1, tiles, lambda t, total: total + totals[t], totals[0]
    ) / (tiles * blocks * LANES)
    sent_all(others, nsend.at[0], nrecv.at[0])


def last_kernel(*refs):
    count = len(refs) // 2
    copies = [
        pltpu.make_async_copy(refs[i], refs[count + i], refs[2 * count].at[i])
        for i in range(count)
    ]
    for copy in copies:
        copy.start()
    for copy in copies:
        copy.wait()


def blocked(x):
    rows, columns = x.shape[-2:]
    head = x.shape[:-2]
    n = len(head)
    y = x.reshape(head + (rows, columns // LANES, LANES))
    y = jnp.swapaxes(y, n, n + 1)
    return y.reshape(head + (rows * columns // LANES, LANES))


def unblocked(x, rows):
    head = x.shape[:-2]
    n = len(head)
    y = x.reshape(head + (x.shape[-2] // rows, rows, LANES))
    y = jnp.swapaxes(y, n, n + 1)
    return y.reshape(head + (rows, -1))


def shards(
    final_adjoint,
    first_density,
    second_density,
    forage,
    preference,
    base_mortality,
    age_class,
    land_mask,
    east_velocity,
    north_velocity,
):
    classes, groups = preference.shape
    cohorts, rows, columns = final_adjoint.shape
    tiles = lax.axis_size("tile")
    group = 2 * SUBSTEPS // rows
    size = 5
    chunks = 10
    alone = (cohorts // size - 2 * chunks) // (group - 2)
    own, both = alone * size, (chunks - alone) * size
    blocks = rows * columns // LANES
    f32 = jnp.float32
    dma = pltpu.SemaphoreType.DMA
    vmem = pl.BlockSpec(memory_space=pltpu.VMEM)
    smem = pl.BlockSpec(memory_space=pltpu.SMEM)
    hbm = pl.BlockSpec(memory_space=pl.ANY)
    dims = (tiles, group, rows, cohorts, size, alone, chunks, groups, 4, 4, 3)
    cell = (blocks, LANES)

    def body(*refs):
        kernel(dims, *refs)

    def cells(*lead):
        return pltpu.VMEM(lead + cell, f32)

    results = pl.pallas_call(
        body,
        out_shape=(
            cells(cohorts),
            cells(2, groups),
            pltpu.VMEM((groups, classes), f32),
        ),
        in_specs=[hbm] * 10,
        out_specs=(vmem, vmem, vmem),
        scratch_shapes=[
            cells(2 * group, own + both),
            cells(2 * group, own + both),
            cells(group + 1, groups),
            cells(group, own + both),
            cells(group, own),
            cells(2, both),
            cells(group, own),
            cells(2, both),
            cells(group, own),
            cells(2, both),
            pltpu.VMEM((2 * group,) + cell, jnp.int32),
            cells(2 * group),
            cells(2 * group),
            pltpu.VMEM((2 * group * rows, 5, blocks // rows, LANES), f32),
            cells(group, groups),
            cells(groups),
            cells(groups),
            cells(4, groups),
            cells(cohorts),
            cells(cohorts),
            cells(2, groups),
            pltpu.VMEM((cohorts, LANES), f32),
            cells(classes),
            cells(classes),
            cells(classes),
            cells(classes),
            cells(group, classes),
            cells(2, classes),
            cells(classes),
            cells(group + 2, max(own, both) + 2),
            pltpu.VMEM((groups, classes, LANES), f32),
            pltpu.VMEM((tiles, groups, classes), f32),
            pltpu.SMEM((classes + 1,), jnp.int32),
            pltpu.SMEM((groups, classes), f32),
            pltpu.VMEM((1, cohorts), f32),
            pltpu.SMEM((cohorts,), jnp.int32),
        ]
        + [dma((1,)), dma((chunks,)), dma((2,)), dma((chunks,)), dma((2,)), dma((2,))]
        + [dma((2,)), dma((chunks,)), dma((2,)), dma((chunks,)), dma((3,)), dma((3,))]
        + [dma((3, 2)), dma((3,)), dma((3,)), dma((3,)), dma((4,)), dma((4,))]
        + [dma((1,)), dma((1,)), dma((9,))],
        compiler_params=pltpu.CompilerParams(
            collective_id=0, has_side_effects=True, vmem_limit_bytes=56 * 1024 * 1024
        ),
        name="adjoint",
    )(
        preference.T,
        base_mortality.reshape(1, -1),
        age_class,
        blocked(final_adjoint),
        blocked(first_density),
        blocked(second_density),
        blocked(forage),
        blocked(land_mask),
        blocked(east_velocity),
        blocked(north_velocity),
    )
    out, sens, grad = pl.pallas_call(
        last_kernel,
        out_shape=tuple(jax.ShapeDtypeStruct(x.shape, x.dtype) for x in results),
        in_specs=[vmem] * len(results),
        out_specs=(hbm,) * len(results),
        scratch_shapes=[dma((len(results),))],
        name="outgoing",
    )(*(pltpu.with_memory_space_constraint(x, pltpu.VMEM) for x in results))
    summed = grad.T
    return (unblocked(out, rows), unblocked(sens, rows), summed)


def solution(mesh):
    in_specs = (
        P("ens", "tile", None),
        P("ens", "tile", None),
        P("ens", "tile", None),
        P("ens", None, "tile", None),
        P("ens", None),
        P(),
        P(),
        P("tile", None),
        P("tile", None),
        P("tile", None),
    )
    out_specs = (P("ens", "tile", None), P("ens", None, "tile", None), P("ens", None))
    return jax.shard_map(shards, mesh=mesh, in_specs=in_specs, out_specs=out_specs, check_vma=False)
```
